32 devices in a mesh: energy: 8 (over z, y), mom: 4 (over x, core).
Axes of the slice: x: 2, y: 2, z: 4, core: 2. Of those that a mesh axis runs over, the one named last changes fastest.
Arguments:
- green_ret: bfloat16 [16, 16, 2, 512, 512], P('mom', 'energy'), may hold values from -0.25 to 0.25
- broadening: float32 [16, 16, 512], P('mom', 'energy'), may hold values from 0.2 to 2
- coupling: bfloat16 [16, 512, 512], P(None, 'mom'), may hold values from -1.5 to 1.5
- shift_steps: int32 [4], replicated, may hold values from 1 to 2, as said below
- mode_weight: float32 [4], replicated, may hold values from 0.05 to 0.25
- occupation: float32 [4], replicated, may hold values from 0.1 to 2
- momentum_map: int32 [16, 16], replicated, may hold values from 0 to 15, as said below
Outputs:
- self_energy: bfloat16 [16, 16, 2, 512, 512], P(None, 'energy', None, 'mom')
- density: float32 [512, 16, 2, 512], P('energy', 'mom')
The draws below stay inside these ranges and needn't reach their ends.
Inputs may be any that keep to these rules, and one draw needn't show every extreme that they name: `shift_steps`: some entry equals 2. `momentum_map`: every row and every column holds each of the 16 momentum indices once.
All inputs are finite; a program needn't handle non-finite values.
Results may differ from the reference program's by a relative error of at most 0.02.
Values may be sent and summed in bfloat16 or wider, within the bound.
No kernel may reach another device: no remote copies, remote signals or barrier semaphores. Data moves between devices by JAX's collectives and lax.ppermute only.
A program may use at most 192 MiB of HBM per device.

```python
import math
import jax
import jax.numpy as jnp
from jax import lax

NORB = 512
NK = 16
NMODE = 4
SHIFT_MAX = 2
NE = 16


def draw_shift_steps(key, part):
    first_key, second_key = jax.random.split(jax.random.fold_in(key, 11))
    values = jax.random.randint(first_key, (NMODE,), 1, SHIFT_MAX + 1)
    chosen = jax.random.randint(second_key, (), 0, NMODE)
    return jnp.where(jnp.arange(NMODE) == chosen, SHIFT_MAX, values).astype(jnp.int32)


def draw_momentum_map(key, part):
    first_key, second_key = jax.random.split(jax.random.fold_in(key, 23))
    row_perm = jax.random.permutation(first_key, NK)
    column_perm = jax.random.permutation(second_key, NK)
    return ((row_perm[:, None] + column_perm[None, :]) % NK).astype(jnp.int32)


def block_levels(own_key, shape, cuts, least, high):
    factor_of, own = 1.0, jax.random.fold_in(own_key, 6)
    for position, blocks in cuts:
        heights = jnp.exp(jax.random.uniform(jax.random.fold_in(own, position), (blocks,), jnp.float32, least / len(cuts), high / len(cuts)))
        factor_of = factor_of * jnp.repeat(heights, shape[position] // blocks).reshape([-1 if axis == position else 1 for axis in range(len(shape))])
    return factor_of


def scatter_about(own_key, dims, width, reach, shards=(), held_as=jnp.bfloat16):
    drawn = jax.random.normal(own_key, dims, jnp.float32) * width
    if len(shards) > 0:
        drawn = block_levels(own_key, dims, shards, -0.22, 0.18) * drawn
    return jnp.clip(drawn, min=-reach, max=reach).astype(held_as)


def setup_inputs(seed: int = 0) -> dict:
    keys = jax.random.split(jax.random.key(seed), 8)
    green_ret = scatter_about(keys[0], (NK, NE, 2, NORB, NORB), NORB ** -0.5, 0.25, ((0, 4), (1, 8)))
    broadening = jnp.clip(jnp.exp(math.log(2.0) - 2.3025851 * jax.random.uniform(keys[1], (NK, NE, NORB), jnp.float32) ** block_levels(keys[1], (NK, NE, NORB), ((0, 4), (1, 8)), -0.2, 0.2)), 0.2, 2.0)
    coupling = scatter_about(keys[2], (NK, NORB, NORB), 0.25, 1.5, ((1, 4),))
    shift_steps = draw_shift_steps(jax.random.fold_in(keys[7], 71), 0)
    mode_weight = jnp.clip(jnp.exp(jax.random.uniform(keys[4], (NMODE,), jnp.float32, math.log(0.05), math.log(0.25))), 0.05, 0.25)
    occupation = jnp.clip(jnp.exp(jax.random.uniform(keys[5], (NMODE,), jnp.float32, math.log(0.1), math.log(2.0))), 0.1, 2.0)
    momentum_map = draw_momentum_map(jax.random.fold_in(keys[7], 71), 0)
    return dict(green_ret=green_ret, broadening=broadening, coupling=coupling, shift_steps=shift_steps, mode_weight=mode_weight, occupation=occupation, momentum_map=momentum_map)


def sandwich(left, right):
    left_full = left.astype(jnp.float32)
    right_full = right.astype(jnp.float32)
    real_part = jnp.einsum('ecij,ecmj->eim', left_full, right_full)
    imag_part = jnp.einsum('eij,emj->eim', left_full[:, 1], right_full[:, 0]) - jnp.einsum('eij,emj->eim', left_full[:, 0], right_full[:, 1])
    return jnp.stack([real_part, imag_part], axis=1)


def complex_product(left, right):
    left_full = left.astype(jnp.float32)
    right_full = right.astype(jnp.float32)
    real_part = jnp.einsum('eij,ejm->eim', left_full[:, 0], right_full[:, 0]) - jnp.einsum('eij,ejm->eim', left_full[:, 1], right_full[:, 1])
    imag_part = jnp.einsum('eij,ejm->eim', left_full[:, 0], right_full[:, 1]) + jnp.einsum('eij,ejm->eim', left_full[:, 1], right_full[:, 0])
    return jnp.stack([real_part, imag_part], axis=1)


def scale_columns(green, gamma):
    return (green.astype(jnp.float32) * gamma[:, None, None, :]).astype(jnp.bfloat16)


def reference(green_ret, broadening, coupling, shift_steps, mode_weight, occupation, momentum_map):
    def first_pass(inputs):
        green, gamma = inputs
        return sandwich(scale_columns(green, gamma), green).astype(jnp.bfloat16)

    lesser = lax.map(first_pass, (green_ret, broadening))
    padded = jnp.pad(lesser, ((0, 0), (SHIFT_MAX, SHIFT_MAX), (0, 0), (0, 0), (0, 0)))

    def shifted(padded_one):
        total = jnp.zeros((NE,) + padded_one.shape[1:], jnp.float32)
        for branch in range(NMODE):
            offset = shift_steps[branch].astype(jnp.int32)
            above = lax.dynamic_slice_in_dim(padded_one, (SHIFT_MAX + offset).astype(jnp.int32), NE, 0).astype(jnp.float32)
            below = lax.dynamic_slice_in_dim(padded_one, (SHIFT_MAX - offset).astype(jnp.int32), NE, 0).astype(jnp.float32)
            total = total + mode_weight[branch] * ((occupation[branch] + 1.0) * above + occupation[branch] * below)
        return total.astype(jnp.bfloat16)

    source = lax.map(shifted, padded)

    def convolve(target):
        def add_term(qpoint, total):
            donor_index = momentum_map[target, qpoint].astype(jnp.int32)
            donor = lax.dynamic_index_in_dim(source, donor_index, 0, keepdims=False).astype(jnp.float32)
            weight = lax.dynamic_index_in_dim(coupling, qpoint, 0, keepdims=False).astype(jnp.float32)
            return total + weight[None, None] * donor

        total = lax.fori_loop(0, NK, add_term, jnp.zeros(source.shape[1:], jnp.float32))
        return total.astype(jnp.bfloat16)

    self_energy = lax.map(convolve, jnp.arange(NK, dtype=jnp.int32))

    def second_pass(inputs):
        green, gamma, sigma = inputs
        scaled = scale_columns(green, gamma)
        mixed = (complex_product(green, sigma) + scaled.astype(jnp.float32)).astype(jnp.bfloat16)
        return jnp.sum(sandwich(mixed, green), axis=0) / NE

    density_blocks = lax.map(second_pass, (green_ret, broadening, self_energy))
    density = jnp.transpose(density_blocks, (2, 0, 1, 3))
    return self_energy, density
```

```python
import functools

import jax
import jax.numpy as jnp
from jax import lax
from jax.experimental import pallas as pl
from jax.experimental.pallas import tpu as pltpu
from jax.sharding import PartitionSpec as P

SHIFT_MAX = 2
F32 = jnp.float32
BF16 = jnp.bfloat16


def params(**kw):
    return pltpu.CompilerParams(vmem_limit_bytes=56 * 1024 * 1024, **kw)


def cost(flops, nbytes):
    return pl.CostEstimate(flops=int(flops), bytes_accessed=int(nbytes), transcendentals=0)


def dot_nt(a, b):
    return lax.dot_general(a, b, (((1,), (1,)), ((), ())), preferred_element_type=F32)


def dot_nn(a, b):
    return lax.dot_general(a, b, (((1,), (0,)), ((), ())), preferred_element_type=F32)


def row_col(rows, cols):
    return lax.broadcasted_iota(jnp.int32, (rows, cols), 0), lax.broadcasted_iota(jnp.int32, (rows, cols), 1)


def lesser_kernel(sel, g_ref, gamma_ref, out_ref):
    n = g_ref.shape[-1]
    half = n // 2
    e = pl.program_id(1)
    gamma = gamma_ref[0, pl.ds(e, 1), :]
    g_re, g_im = g_ref[0, 0, 0], g_ref[0, 0, 1]
    s_re = (g_re.astype(F32) * gamma).astype(BF16)
    s_im = (g_im.astype(F32) * gamma).astype(BF16)
    row, col = row_col(half, half)

    def real(i, j):
        i, j = slice(i * half, (i + 1) * half), slice(j * half, (j + 1) * half)
        return dot_nt(s_re[i], g_re[j]) + dot_nt(s_im[i], g_im[j])

    def imag(i, j):
        i, j = slice(i * half, (i + 1) * half), slice(j * half, (j + 1) * half)
        return dot_nt(s_im[i], g_re[j]) - dot_nt(s_re[i], g_im[j])

    for d in range(2):
        out_ref[0, 0, d * half:(d + 1) * half, d * half:(d + 1) * half] = jnp.where(
            col >= row, real(d, d), imag(d, d)).astype(BF16)
    out_ref[0, 0, :half, half:] = real(0, 1).astype(BF16)
    out_ref[0, 0, half:, :half] = imag(1, 0).astype(BF16)


def lesser_packed(block, green, broadening, count):
    _, le, _, n, _ = green.shape
    return pl.pallas_call(
        lesser_kernel,
        out_shape=jax.ShapeDtypeStruct((count, le, n, n), BF16),
        grid_spec=pltpu.PrefetchScalarGridSpec(
            num_scalar_prefetch=1,
            grid=(count, le),
            in_specs=[
                pl.BlockSpec((1, 1, 2, n, n), lambda k, e, sel: (sel[0] * count + k, e, 0, 0, 0)),
                pl.BlockSpec((1, le, n), lambda k, e, sel: (sel[0] * count + k, 0, 0)),
            ],
            out_specs=pl.BlockSpec((1, 1, n, n), lambda k, e, sel: (k, e, 0, 0)),
        ),
        compiler_params=params(),
        cost_estimate=cost(count * le * 6 * n**3, count * le * n * n * 6),
        name="lesser",
    )(block, green, broadening)


def source_kernel(odd, w_ref, keep, recv, kz, rz, *outs):
    le = keep.shape[1]

    def emit(order):
        line = [(ref, e) for ref in order for e in range(le)]
        for e in range(le):
            for ref, target in ((keep, outs[e]), (recv, outs[le + e])):
                at = [i for i, held in enumerate(order) if held is ref][0] * le + e
                total = None
                for s in range(1, SHIFT_MAX + 1):
                    for j, sign in ((0, s), (1, -s)):
                        source, index = line[at + sign]
                        term = w_ref[2 * (s - 1) + j] * source[0, index].astype(F32)
                        total = term if total is None else total + term
                target[0] = total.astype(BF16)

    @pl.when(odd[0] == 0)
    def _():
        emit((rz, keep, recv, kz))

    @pl.when(odd[0] == 1)
    def _():
        emit((kz, recv, keep, rz))


def sources(odd, weights, keep, recv, kz, rz):
    count, le, n, _ = keep.shape
    rows = n // 4
    big = pl.BlockSpec((1, le, rows, n), lambda k, r, *_: (k, 0, r, 0))
    one = pl.BlockSpec((1, rows, n), lambda k, r, *_: (k, r, 0))
    return pl.pallas_call(
        source_kernel,
        out_shape=[jax.ShapeDtypeStruct((count, n, n), BF16)] * (2 * le),
        grid_spec=pltpu.PrefetchScalarGridSpec(
            num_scalar_prefetch=2,
            grid=(count, n // rows),
            in_specs=[big] * 4,
            out_specs=[one] * (2 * le),
        ),
        compiler_params=params(),
        cost_estimate=cost(count * le * n * n * 16, count * le * n * n * 12),
        name="source",
    )(odd, weights, keep, recv, kz, rz)


def home_kernel(lk, pieces, slots, *refs):
    ins, (c_ref, ct_ref, x_ref, y_ref, q_ref) = refs[:pieces], refs[pieces:]
    each, rows, n = ins[0].shape
    for s in range(pieces):
        for j in range(each):
            q_ref[s * each + j] = ins[s][j].astype(F32)
    count = pieces * each
    tr, tc = 16, 256

    def tile(index, _):
        r = pl.ds(pl.multiple_of((index // (n // tc)) * tr, tr), tr)
        m = pl.ds(pl.multiple_of((index % (n // tc)) * tc, tc), tc)
        xs, ys = [None] * lk, [None] * lk
        for q in range(count):
            c, ct = c_ref[0, q, r, m].astype(F32), ct_ref[q, r, m].astype(F32)
            for k in range(lk):
                v = q_ref[slots[k * count + q], r, m]
                xs[k] = c * v if q == 0 else xs[k] + c * v
                ys[k] = ct * v if q == 0 else ys[k] + ct * v
        for k in range(lk):
            x_ref[k, r, m] = xs[k].astype(BF16)
            y_ref[k, r, m] = ys[k].astype(BF16)
        return 0

    lax.fori_loop(0, (rows // tr) * (n // tc), tile, 0)


def home_blocks(slots, pieces, c4, ct, lk):
    each, n, _ = pieces[0].shape
    count = each * len(pieces)
    rows = 64
    per = c4.shape[2] // rows
    return pl.pallas_call(
        functools.partial(home_kernel, lk, len(pieces)),
        out_shape=[jax.ShapeDtypeStruct((lk, n, n), BF16)] * 2,
        grid_spec=pltpu.PrefetchScalarGridSpec(
            num_scalar_prefetch=1,
            grid=(n // rows,),
            in_specs=[pl.BlockSpec((each, rows, n), lambda g, s: (0, g, 0))] * len(pieces) + [
                pl.BlockSpec((1, count, rows, n), lambda g, s: (g // per, 0, g % per, 0)),
                pl.BlockSpec((count, rows, n), lambda g, s: (0, g, 0)),
            ],
            out_specs=[pl.BlockSpec((lk, rows, n), lambda g, s: (0, g, 0))] * 2,
            scratch_shapes=[pltpu.VMEM((count, rows, n), F32)],
        ),
        compiler_params=params(),
        cost_estimate=cost(4 * lk * count * n * n, n * n * (6 * count + 4 * lk)),
        name="home",
    )(slots, *pieces, c4, ct)


def rows_kernel(pieces, aliased, mine, slots, *refs):
    a_refs, b_refs, refs = refs[:pieces], refs[pieces:2 * pieces], refs[2 * pieces:]
    c_ref, out_ref, re_ref, im_ref = (refs[0],) + refs[-3:]
    each, rows, cols = a_refs[0].shape
    count = pieces * each
    row, col = row_col(rows, cols)
    above = (col - row) + (pl.program_id(0) * cols - mine[0] * rows)
    for s in range(pieces):
        for j in range(each):
            a, b = a_refs[s][j].astype(F32), b_refs[s][j].astype(F32).T
            re_ref[s * each + j] = jnp.where(above >= 0, a, b)
            im_ref[s * each + j] = jnp.where(above < 0, a, jnp.where(above > 0, -b, 0.0))
    tr, kg = 16, 8

    def tile(index, _):
        r = pl.ds(pl.multiple_of((index % (rows // tr)) * tr, tr), tr)
        k0 = (index // (rows // tr)) * kg
        res, ims = [None] * kg, [None] * kg
        for q in range(count):
            c = c_ref[q, r, :].astype(F32)
            for k in range(kg):
                slot = slots[(k0 + k) * count + q]
                u, v = c * re_ref[slot, r, :], c * im_ref[slot, r, :]
                res[k] = u if q == 0 else res[k] + u
                ims[k] = v if q == 0 else ims[k] + v
        for k in range(kg):
            out_ref[k0 + k, 0, 0, r, :] = res[k].astype(BF16)
            out_ref[k0 + k, 0, 1, r, :] = ims[k].astype(BF16)
        return 0

    lax.fori_loop(0, (rows // tr) * (count // kg), tile, 0)


def own_rows(mine, slots, pieces, coupling, energy, le, held):
    each, n, _ = pieces[0].shape
    count, rows, _ = coupling.shape
    cols = rows
    alias = held is not None
    out_map = lambda t, mine, slots: (0, energy, 0, 0, t)
    in_specs = (
        [pl.BlockSpec((each, rows, cols), lambda t, mine, slots: (0, mine[0], t))] * len(pieces)
        + [pl.BlockSpec((each, cols, rows), lambda t, mine, slots: (0, t, mine[0]))] * len(pieces)
        + [pl.BlockSpec((count, rows, cols), lambda t, mine, slots: (0, 0, t))]
        + ([pl.BlockSpec(memory_space=pl.ANY)] if alias else [])
    )
    return pl.pallas_call(
        functools.partial(rows_kernel, len(pieces), alias),
        out_shape=jax.ShapeDtypeStruct((count, le, 2, rows, n), BF16),
        grid_spec=pltpu.PrefetchScalarGridSpec(
            num_scalar_prefetch=2,
            grid=(n // cols,),
            in_specs=in_specs,
            out_specs=pl.BlockSpec((count, 1, 2, rows, cols), out_map),
            scratch_shapes=[pltpu.VMEM((count, rows, cols), F32)] * 2,
        ),
        input_output_aliases={2 + len(in_specs) - 1: 0} if alias else {},
        compiler_params=params(),
        cost_estimate=cost(4 * count * count * rows * n, rows * n * count * 10),
        name="rows",
    )(mine, slots, *pieces, *pieces, coupling, *([held] if alias else []))


def density_kernel(scale, energy, first, last, g_ref, gamma_ref, x_ref, y_ref, *refs):
    out_ref = refs[-1]
    n = g_ref.shape[-1]
    gamma = gamma_ref[0, energy:energy + 1, :]
    g_re, g_im = g_ref[0, 0, 0], g_ref[0, 0, 1]
    row, col = row_col(n, n)
    x, yt = x_ref[0].astype(F32), y_ref[0].astype(F32).T
    s_re = jnp.where(col >= row, x, yt).astype(BF16)
    s_im = jnp.where(col < row, x, jnp.where(col > row, -yt, 0.0)).astype(BF16)
    scaled_re = (g_re.astype(F32) * gamma).astype(BF16).astype(F32)
    scaled_im = (g_im.astype(F32) * gamma).astype(BF16).astype(F32)
    m_re = (dot_nn(g_re, s_re) - dot_nn(g_im, s_im) + scaled_re).astype(BF16)
    m_im = (dot_nn(g_re, s_im) + dot_nn(g_im, s_re) + scaled_im).astype(BF16)
    d_re = dot_nt(m_re, g_re) + dot_nt(m_im, g_im)
    d_im = dot_nt(m_im, g_re) - dot_nt(m_re, g_im)
    if not first:
        d_re, d_im = d_re + refs[0][0, 0], d_im + refs[0][0, 1]
    if last:
        d_re, d_im = d_re * scale, d_im * scale
    out_ref[0, 0] = d_re.astype(out_ref.dtype)
    out_ref[0, 1] = d_im.astype(out_ref.dtype)


def density_term(scale, energy, le, green, broadening, x, y, held):
    lk, _, _, n, _ = green.shape
    last = energy == le - 1
    pair = pl.BlockSpec((1, 2, n, n), lambda k: (k, 0, 0, 0))
    one = pl.BlockSpec((1, n, n), lambda k: (k, 0, 0))
    return pl.pallas_call(
        functools.partial(density_kernel, scale, energy, held is None, last),
        out_shape=jax.ShapeDtypeStruct((lk, 2, n, n), BF16 if last else F32),
        grid=(lk,),
        in_specs=[
            pl.BlockSpec((1, 1, 2, n, n), lambda k: (k, energy, 0, 0, 0)),
            pl.BlockSpec((1, le, n), lambda k: (k, 0, 0)),
            one,
            one,
        ] + ([] if held is None else [pair]),
        out_specs=pair,
        compiler_params=params(),
        cost_estimate=cost(16 * lk * n**3, lk * n * n * 20),
        name="density",
    )(green, broadening, x, y, *([] if held is None else [held]))


def on_device(green_ret, broadening, coupling, shift_steps, mode_weight, occupation, momentum_map):
    lk, le, _, n, _ = green_ret.shape
    ne, nm = lax.axis_size("energy"), lax.axis_size("mom")
    if le != SHIFT_MAX or lk % 2 or ne % 2 or nm & (nm - 1):
        raise ValueError("unsupported sizes")
    hk, nk = lk // 2, lk * nm
    me, mine = lax.axis_index("energy"), lax.axis_index("mom")
    odd = (me % 2).astype(jnp.int32)
    pairs = [(i, i ^ 1) for i in range(ne)]
    away = [(i, i + (2 if i % 2 else -2)) for i in range(ne) if 0 <= i + (2 if i % 2 else -2) < ne]
    across = [(i, i + (-2 if i % 2 else 2)) for i in range(ne) if 0 <= i + (-2 if i % 2 else 2) < ne]

    def swap(x, stride):
        return lax.ppermute(x, "mom", [(i, i ^ stride) for i in range(nm)])

    c4 = lax.all_gather(coupling, "mom", axis=0)
    ct = jnp.transpose(c4, (1, 3, 0, 2)).reshape(nk, n, n)

    weights = []
    for s in range(1, SHIFT_MAX + 1):
        held = shift_steps == s
        weights.append(jnp.sum(jnp.where(held, mode_weight * (occupation + 1.0), 0.0)))
        weights.append(jnp.sum(jnp.where(held, mode_weight * occupation, 0.0)))
    weights = jnp.stack(weights)

    send = lesser_packed((1 - odd)[None], green_ret, broadening, hk)
    recv = lax.ppermute(send, "energy", pairs)
    keep = lesser_packed(odd[None], green_ret, broadening, hk)
    kz = lax.ppermute(keep, "energy", away)
    rz = lax.ppermute(recv, "energy", across)
    got = sources(odd[None], weights, keep, recv, kz, rz)

    owner, inner = momentum_map // lk, momentum_map % lk
    relative = owner ^ mine
    strides = []
    stride = nm // 2
    while stride:
        strides.append(stride)
        stride //= 2
    place = jnp.zeros_like(relative)
    for bit, s in enumerate(strides):
        place = place + jnp.where((relative & s) != 0, 1 << bit, 0)
    slots = (place * lk + ((inner // hk) ^ odd) * hk + inner % hk).astype(jnp.int32)
    own_slots = lax.dynamic_slice_in_dim(slots, mine * lk, lk, 0).reshape(-1)
    all_slots = slots.reshape(-1)
    mine_ref = mine.astype(jnp.int32)[None]

    held_rows, held_density = None, None
    scale = 1.0 / (le * ne)
    for e in range(le):
        back = lax.ppermute(got[le + e], "energy", pairs)
        pieces = [got[e], back]
        for s in strides:
            pieces = pieces + [swap(piece, s) for piece in pieces]
        x, y = home_blocks(own_slots, pieces, c4, ct, lk)
        held_density = density_term(scale, e, le, green_ret, broadening, x, y, held_density)
        held_rows = own_rows(mine_ref, all_slots, pieces, coupling, e, le, held_rows)
    density = lax.psum_scatter(held_density, "energy", scatter_dimension=2, tiled=True)
    return held_rows, jnp.transpose(density, (2, 0, 1, 3)).astype(F32)


def solution(mesh):
    return jax.shard_map(
        on_device,
        mesh=mesh,
        in_specs=(
            P("mom", "energy", None, None, None),
            P("mom", "energy", None),
            P(None, "mom", None),
            P(),
            P(),
            P(),
            P(),
        ),
        out_specs=(P(None, "energy", None, "mom", None), P("energy", "mom", None, None)),
        check_vma=False,
    )
```

```python
import functools

import jax
import jax.numpy as jnp
from jax import lax
from jax.experimental import pallas as pl
from jax.experimental.pallas import tpu as pltpu
from jax.sharding import PartitionSpec as P

SHIFT_MAX = 2
F32 = jnp.float32
BF16 = jnp.bfloat16


def params(**kw):
    return pltpu.CompilerParams(vmem_limit_bytes=56 * 1024 * 1024, **kw)


def cost(flops, nbytes):
    return pl.CostEstimate(flops=int(flops), bytes_accessed=int(nbytes), transcendentals=0)


def dot_nt(a, b):
    return lax.dot_general(a, b, (((1,), (1,)), ((), ())), preferred_element_type=F32)


def dot_nn(a, b):
    return lax.dot_general(a, b, (((1,), (0,)), ((), ())), preferred_element_type=F32)


def row_col(rows, cols):
    return lax.broadcasted_iota(jnp.int32, (rows, cols), 0), lax.broadcasted_iota(jnp.int32, (rows, cols), 1)


def lesser_kernel(sel, g_ref, gamma_ref, *outs):
    n = g_ref.shape[-1]
    half, hr = n // 2, outs[0].shape[2]
    e = pl.program_id(0)
    gamma = gamma_ref[0, pl.ds(e, 1), :]
    g_re, g_im = g_ref[0, 0, 0], g_ref[0, 0, 1]
    s_re = (g_re.astype(F32) * gamma).astype(BF16)
    s_im = (g_im.astype(F32) * gamma).astype(BF16)
    row, col = row_col(half, half)

    def real(i, j):
        i, j = slice(i * half, (i + 1) * half), slice(j * half, (j + 1) * half)
        return dot_nt(s_re[i], g_re[j]) + dot_nt(s_im[i], g_im[j])

    def imag(i, j):
        i, j = slice(i * half, (i + 1) * half), slice(j * half, (j + 1) * half)
        return dot_nt(s_im[i], g_re[j]) - dot_nt(s_re[i], g_im[j])

    def put(i, j, value):
        value = value.astype(BF16)
        for t in range(half // hr):
            at = i * (half // hr) + t
            outs[at % 2][0, at // 2, :, j * half:(j + 1) * half] = value[t * hr:(t + 1) * hr]

    for d in range(2):
        put(d, d, jnp.where(col >= row, real(d, d), imag(d, d)))
    put(0, 1, real(0, 1))
    put(1, 0, imag(1, 0))


def lesser_packed(which, green, broadening, nm):
    _, le, _, n, _ = green.shape
    hr = n // (2 * nm)
    return pl.pallas_call(
        lesser_kernel,
        out_shape=[jax.ShapeDtypeStruct((le, nm, hr, n), BF16)] * 2,
        grid_spec=pltpu.PrefetchScalarGridSpec(
            num_scalar_prefetch=1,
            grid=(le,),
            in_specs=[
                pl.BlockSpec((1, 1, 2, n, n), lambda e, sel: (sel[0], e, 0, 0, 0)),
                pl.BlockSpec((1, le, n), lambda e, sel: (sel[0], 0, 0)),
            ],
            out_specs=[pl.BlockSpec((1, nm, hr, n), lambda e, sel: (e, 0, 0, 0))] * 2,
        ),
        compiler_params=params(),
        cost_estimate=cost(le * 6 * n**3, le * n * n * 6),
        name="lesser",
    )(which[None], green, broadening)


def place_kernel(where, c_ref, *refs):
    full_ref, turned_ref = refs[-2:]
    full_ref[...] = c_ref[...]
    for q in range(c_ref.shape[0]):
        turned_ref[q] = c_ref[q].T


def place_coupling(where, piece, held):
    nk, rows, n = piece.shape
    each = 4
    alias = [] if held is None else list(held)
    return pl.pallas_call(
        place_kernel,
        out_shape=[jax.ShapeDtypeStruct((nk, n, n), BF16)] * 2,
        grid_spec=pltpu.PrefetchScalarGridSpec(
            num_scalar_prefetch=1,
            grid=(nk // each,),
            in_specs=[pl.BlockSpec((each, rows, n), lambda q, w: (q, 0, 0))]
            + [pl.BlockSpec(memory_space=pl.ANY)] * len(alias),
            out_specs=[
                pl.BlockSpec((each, rows, n), lambda q, w: (q, w[0], 0)),
                pl.BlockSpec((each, n, rows), lambda q, w: (q, 0, w[0])),
            ],
        ),
        input_output_aliases={2: 0, 3: 1} if alias else {},
        compiler_params=params(),
        cost_estimate=cost(nk * rows * n * 4, nk * rows * n * 6),
        name="place",
    )(where[None], piece, *alias)


def source_kernel(odd, w_ref, keep, recv, kz, rz, *outs):
    le = keep.shape[0]

    def emit(order):
        line = [(ref, e) for ref in order for e in range(le)]
        for e in range(le):
            for ref, target in ((keep, outs[e]), (recv, outs[le + e])):
                at = [i for i, held in enumerate(order) if held is ref][0] * le + e
                total = None
                for s in range(1, SHIFT_MAX + 1):
                    for j, sign in ((0, s), (1, -s)):
                        source, index = line[at + sign]
                        term = w_ref[2 * (s - 1) + j] * source[index, 0].astype(F32)
                        total = term if total is None else total + term
                target[0] = total.astype(BF16)

    @pl.when(odd[0] == 0)
    def _():
        emit((rz, keep, recv, kz))

    @pl.when(odd[0] == 1)
    def _():
        emit((kz, recv, keep, rz))


def sources(odd, weights, keep, recv, kz, rz):
    le, nm, hr, n = keep.shape
    big = pl.BlockSpec((le, 1, hr, n), lambda r, *_: (0, r, 0, 0))
    one = pl.BlockSpec((1, hr, n), lambda r, *_: (r, 0, 0))
    return pl.pallas_call(
        source_kernel,
        out_shape=[jax.ShapeDtypeStruct((nm, hr, n), BF16)] * (2 * le),
        grid_spec=pltpu.PrefetchScalarGridSpec(
            num_scalar_prefetch=2,
            grid=(nm,),
            in_specs=[big] * 4,
            out_specs=[one] * (2 * le),
        ),
        compiler_params=params(),
        cost_estimate=cost(le * nm * hr * n * 16, le * nm * hr * n * 12),
        name="source",
    )(odd[None], weights, keep, recv, kz, rz)


def home_kernel(lk, count, slots, *refs):
    ins = refs[:count]
    c_ref, ct_ref = refs[count:count + 2]
    x_ref, y_ref, q_ref = refs[-3:]
    _, rows, n = ins[0].shape
    for s in range(count):
        q_ref[s] = ins[s][0].astype(F32)
    tr, tc = 16, 256

    def tile(index, _):
        r = pl.ds(pl.multiple_of((index // (n // tc)) * tr, tr), tr)
        m = pl.ds(pl.multiple_of((index % (n // tc)) * tc, tc), tc)
        xs, ys = [None] * lk, [None] * lk
        for q in range(count):
            c, ct = c_ref[q, r, m].astype(F32), ct_ref[q, r, m].astype(F32)
            for k in range(lk):
                v = q_ref[slots[k * count + q], r, m]
                xs[k] = c * v if q == 0 else xs[k] + c * v
                ys[k] = ct * v if q == 0 else ys[k] + ct * v
        for k in range(lk):
            x_ref[k, r, m] = xs[k].astype(BF16)
            y_ref[k, r, m] = ys[k].astype(BF16)
        return 0

    lax.fori_loop(0, (rows // tr) * (n // tc), tile, 0)


def home_blocks(slots, h, pieces, full, turned, lk, held):
    count = len(pieces)
    nm, hr, n = pieces[0].shape
    alias = [] if held is None else list(held)
    block = lambda lead: pl.BlockSpec((lead, hr, n), lambda g, s: (0, 2 * g + h, 0))
    return pl.pallas_call(
        functools.partial(home_kernel, lk, count),
        out_shape=[jax.ShapeDtypeStruct((lk, n, n), BF16)] * 2,
        grid_spec=pltpu.PrefetchScalarGridSpec(
            num_scalar_prefetch=1,
            grid=(nm,),
            in_specs=[pl.BlockSpec((1, hr, n), lambda g, s: (g, 0, 0))] * count
            + [block(count), block(count)]
            + [pl.BlockSpec(memory_space=pl.ANY)] * len(alias),
            out_specs=[block(lk), block(lk)],
            scratch_shapes=[pltpu.VMEM((count, hr, n), F32)],
        ),
        input_output_aliases={count + 3: 0, count + 4: 1} if alias else {},
        compiler_params=params(),
        cost_estimate=cost(2 * lk * count * n * n, n * n * (3 * count + 2 * lk)),
        name="home",
    )(slots, *pieces, full, turned, *alias)


def rows_kernel(count, mine, slots, *refs):
    a_refs, b_refs, refs = refs[:2 * count], refs[2 * count:4 * count], refs[4 * count:]
    c_ref, out_ref, re_ref, im_ref = (refs[0],) + refs[-3:]
    _, hr, cols = a_refs[0].shape
    rows = 2 * hr
    row, col = row_col(rows, cols)
    above = (col - row) + (pl.program_id(0) * cols - mine[0] * rows)
    for s in range(count):
        a = jnp.concatenate([a_refs[s][0], a_refs[count + s][0]], axis=0).astype(F32)
        b = jnp.concatenate([b_refs[s][0], b_refs[count + s][0]], axis=0).astype(F32).T
        re_ref[s] = jnp.where(above >= 0, a, b)
        im_ref[s] = jnp.where(above < 0, a, jnp.where(above > 0, -b, 0.0))
    tr, kg = 16, 8

    def tile(index, _):
        r = pl.ds(pl.multiple_of((index % (rows // tr)) * tr, tr), tr)
        k0 = (index // (rows // tr)) * kg
        res, ims = [None] * kg, [None] * kg
        for q in range(count):
            c = c_ref[q, r, :].astype(F32)
            for k in range(kg):
                slot = slots[(k0 + k) * count + q]
                u, v = c * re_ref[slot, r, :], c * im_ref[slot, r, :]
                res[k] = u if q == 0 else res[k] + u
                ims[k] = v if q == 0 else ims[k] + v
        for k in range(kg):
            out_ref[k0 + k, 0, 0, r, :] = res[k].astype(BF16)
            out_ref[k0 + k, 0, 1, r, :] = ims[k].astype(BF16)
        return 0

    lax.fori_loop(0, (rows // tr) * (count // kg), tile, 0)


def own_rows(mine, slots, pieces, coupling, energy, le, held):
    count, rows, n = coupling.shape
    nm, hr, _ = pieces[0].shape
    cols = n // nm
    alias = [] if held is None else [held]
    in_specs = (
        [pl.BlockSpec((1, hr, cols), lambda t, mine, slots: (mine[0], 0, t))] * (2 * count)
        + [pl.BlockSpec((1, hr, rows), lambda t, mine, slots: (t, 0, mine[0]))] * (2 * count)
        + [pl.BlockSpec((count, rows, cols), lambda t, mine, slots: (0, 0, t))]
        + [pl.BlockSpec(memory_space=pl.ANY)] * len(alias)
    )
    return pl.pallas_call(
        functools.partial(rows_kernel, count),
        out_shape=jax.ShapeDtypeStruct((count, le, 2, rows, n), BF16),
        grid_spec=pltpu.PrefetchScalarGridSpec(
            num_scalar_prefetch=2,
            grid=(nm,),
            in_specs=in_specs,
            out_specs=pl.BlockSpec((count, 1, 2, rows, cols), lambda t, mine, slots: (0, energy, 0, 0, t)),
            scratch_shapes=[pltpu.VMEM((count, rows, cols), F32)] * 2,
        ),
        input_output_aliases={2 + len(in_specs) - 1: 0} if alias else {},
        compiler_params=params(),
        cost_estimate=cost(4 * count * count * rows * n, rows * n * count * 10),
        name="rows",
    )(mine[None], slots, *pieces, *pieces, coupling, *alias)


def density_terms(energy, g_ref, gamma_ref, x_ref, y_ref):
    n = g_ref.shape[-1]
    gamma = gamma_ref[0, energy:energy + 1, :]
    g_re, g_im = g_ref[0, 0, 0], g_ref[0, 0, 1]
    row, col = row_col(n, n)
    x, yt = x_ref[0].astype(F32), y_ref[0].astype(F32).T
    s_re = jnp.where(col >= row, x, yt).astype(BF16)
    s_im = jnp.where(col < row, x, jnp.where(col > row, -yt, 0.0)).astype(BF16)
    scaled_re = (g_re.astype(F32) * gamma).astype(BF16).astype(F32)
    scaled_im = (g_im.astype(F32) * gamma).astype(BF16).astype(F32)
    m_re = (dot_nn(g_re, s_re) - dot_nn(g_im, s_im) + scaled_re).astype(BF16)
    m_im = (dot_nn(g_re, s_im) + dot_nn(g_im, s_re) + scaled_im).astype(BF16)
    return dot_nt(m_re, g_re) + dot_nt(m_im, g_im), dot_nt(m_im, g_re) - dot_nt(m_re, g_im)


def first_density_kernel(energy, first, g_ref, gamma_ref, x_ref, y_ref, *refs):
    for c, d in enumerate(density_terms(energy, g_ref, gamma_ref, x_ref, y_ref)):
        refs[-1][0, c] = d if first else d + refs[0][0, c]


def first_density(energy, green, broadening, x, y, held):
    lk, le, _, n, _ = green.shape
    alias = [] if held is None else [held]
    pair = pl.BlockSpec((1, 2, n, n), lambda k: (k, 0, 0, 0))
    one = pl.BlockSpec((1, n, n), lambda k: (k, 0, 0))
    return pl.pallas_call(
        functools.partial(first_density_kernel, energy, held is None),
        out_shape=jax.ShapeDtypeStruct((lk, 2, n, n), F32),
        grid=(lk,),
        in_specs=[
            pl.BlockSpec((1, 1, 2, n, n), lambda k: (k, energy, 0, 0, 0)),
            pl.BlockSpec((1, le, n), lambda k: (k, 0, 0)),
            one,
            one,
        ] + [pair] * len(alias),
        out_specs=pair,
        compiler_params=params(),
        cost_estimate=cost(16 * lk * n**3, lk * n * n * 20),
        name="density",
    )(green, broadening, x, y, *alias)


def last_density_kernel(scale, energy, odd, g_ref, gamma_ref, x_ref, y_ref, held_ref, keep_ref, send_ref, d_ref):
    groups, _, rows, _ = keep_ref.shape
    for c, d in enumerate(density_terms(energy, g_ref, gamma_ref, x_ref, y_ref)):
        d_ref[c] = (d + held_ref[0, c]) * scale
        for g in range(groups):
            mine = pl.multiple_of((2 * g + odd[0]) * rows, rows)
            other = pl.multiple_of((2 * g + 1 - odd[0]) * rows, rows)
            keep_ref[g, c] = d_ref[c, pl.ds(mine, rows), :].astype(BF16)
            send_ref[g, c] = d_ref[c, pl.ds(other, rows), :].astype(BF16)


def last_density(scale, energy, k, groups, odd, green, broadening, x, y, held):
    _, le, _, n, _ = green.shape
    rows = n // (2 * groups)
    one = pl.BlockSpec((1, n, n), lambda i, odd: (k, 0, 0))
    out = pl.BlockSpec((groups, 2, rows, n), lambda i, odd: (0, 0, 0, 0))
    return pl.pallas_call(
        functools.partial(last_density_kernel, scale, energy),
        out_shape=[jax.ShapeDtypeStruct((groups, 2, rows, n), BF16)] * 2,
        grid_spec=pltpu.PrefetchScalarGridSpec(
            num_scalar_prefetch=1,
            grid=(1,),
            in_specs=[
                pl.BlockSpec((1, 1, 2, n, n), lambda i, odd: (k, energy, 0, 0, 0)),
                pl.BlockSpec((1, le, n), lambda i, odd: (k, 0, 0)),
                one,
                one,
                pl.BlockSpec((1, 2, n, n), lambda i, odd: (k, 0, 0, 0)),
            ],
            out_specs=[out, out],
            scratch_shapes=[pltpu.VMEM((2, n, n), F32)],
        ),
        compiler_params=params(),
        cost_estimate=cost(16 * n**3, n * n * 20),
        name="density",
    )(odd[None], green, broadening, x, y, held)


def pair_sum_kernel(group, keep_ref, recv_ref, *outs):
    groups = len(outs)
    for d in range(groups):
        at = lax.rem(group[0] + d, groups)
        outs[d][...] = (keep_ref[at].astype(F32) + recv_ref[at].astype(F32)).astype(BF16)


def pair_sum(group, keep, recv):
    groups = keep.shape[0]
    vmem = pl.BlockSpec(memory_space=pltpu.VMEM)
    return pl.pallas_call(
        pair_sum_kernel,
        out_shape=[jax.ShapeDtypeStruct(keep.shape[1:], BF16)] * groups,
        in_specs=[pl.BlockSpec(memory_space=pltpu.SMEM), vmem, vmem],
        out_specs=[vmem] * groups,
        compiler_params=params(),
        cost_estimate=cost(keep.size, keep.size * 6),
        name="pairsum",
    )(group[None], keep, recv)


def on_device(green_ret, broadening, coupling, shift_steps, mode_weight, occupation, momentum_map):
    lk, le, _, n, _ = green_ret.shape
    ne, nm = lax.axis_size("energy"), lax.axis_size("mom")
    if le != SHIFT_MAX or lk % 2 or ne % 2 or nm & (nm - 1):
        raise ValueError("unsupported sizes")
    hk, groups = lk // 2, ne // 2
    me, mine = lax.axis_index("energy").astype(jnp.int32), lax.axis_index("mom").astype(jnp.int32)
    odd, group = me & 1, me >> 1
    pairs = [(i, i ^ 1) for i in range(ne)]
    away = [(i, i + (2 if i % 2 else -2)) for i in range(ne) if 0 <= i + (2 if i % 2 else -2) < ne]
    across = [(i, i + (-2 if i % 2 else 2)) for i in range(ne) if 0 <= i + (-2 if i % 2 else 2) < ne]
    strides = []
    while (nm >> (len(strides) + 1)) > 0:
        strides.append(nm >> (len(strides) + 1))

    def over_energy(x, perm):
        return lax.ppermute(x, "energy", perm)

    def swap(x, stride):
        return lax.ppermute(x, "mom", [(i, i ^ stride) for i in range(nm)])

    def spread(x):
        held = [x]
        for s in strides:
            held = held + [swap(piece, s) for piece in held]
        return held

    order = [0]
    for s in strides:
        order = order + [o ^ s for o in order]

    weights = []
    for s in range(1, SHIFT_MAX + 1):
        held = shift_steps == s
        weights.append(jnp.sum(jnp.where(held, mode_weight * (occupation + 1.0), 0.0)))
        weights.append(jnp.sum(jnp.where(held, mode_weight * occupation, 0.0)))
    weights = jnp.stack(weights)

    owner, inner = momentum_map // lk, momentum_map % lk
    place = jnp.zeros_like(owner)
    for at, o in enumerate(order):
        place = jnp.where((owner ^ mine) == o, at, place)
    slots = (place * lk + ((inner // hk) ^ odd) * hk + inner % hk).astype(jnp.int32)
    own_slots = lax.dynamic_slice_in_dim(slots, mine * lk, lk, 0).reshape(-1)
    all_slots = slots.reshape(-1)

    coupling_pieces = spread(coupling)

    send = [lesser_packed((1 - odd) * hk + j, green_ret, broadening, nm) for j in range(hk)]
    recv = [[over_energy(send[j][h], pairs) for h in range(2)] for j in range(hk)]
    keep = [lesser_packed(odd * hk + j, green_ret, broadening, nm) for j in range(hk)]
    kz = [[over_energy(keep[j][h], away) for h in range(2)] for j in range(hk)]
    rz = [[over_energy(recv[j][h], across) for h in range(2)] for j in range(hk)]
    got = [[sources(odd, weights, keep[j][h], recv[j][h], kz[j][h], rz[j][h]) for h in range(2)] for j in range(hk)]

    placed = None
    for at, o in enumerate(order):
        placed = place_coupling(mine ^ o, coupling_pieces[at], placed)
    full, turned = placed

    held_rows, held_density = None, None
    scale = 1.0 / (le * ne)
    late = []
    for e in range(le):
        pieces = []
        for h in range(2):
            fresh = [spread(got[j][h][e]) for j in range(hk)]
            back = [spread(over_energy(got[j][h][le + e], pairs)) for j in range(hk)]
            pieces.append([part[at] for at in range(nm) for part in fresh + back])
        xy = None
        for h in range(2):
            xy = home_blocks(own_slots, h, pieces[h], full, turned, lk, xy)
        x, y = xy
        if e < le - 1:
            held_density = first_density(e, green_ret, broadening, x, y, held_density)
        else:
            for k in range(lk):
                kept, sent = last_density(scale, e, k, groups, odd, green_ret, broadening, x, y, held_density)
                parts = pair_sum(group, kept, over_energy(sent, pairs))
                total = parts[0].astype(F32)
                for d in range(1, groups):
                    perm = [(i, (i + 2 * d) % ne) for i in range(ne)]
                    total = total + over_energy(parts[d], perm).astype(F32)
                late.append(total)
        held_rows = own_rows(mine, all_slots, pieces[0] + pieces[1], coupling, e, le, held_rows)
    density = jnp.transpose(jnp.stack(late), (2, 0, 1, 3))
    return held_rows, density


def solution(mesh):
    return jax.shard_map(
        on_device,
        mesh=mesh,
        in_specs=(
            P("mom", "energy", None, None, None),
            P("mom", "energy", None),
            P(None, "mom", None),
            P(),
            P(),
            P(),
            P(),
        ),
        out_specs=(P(None, "energy", None, "mom", None), P("energy", "mom", None, None)),
        check_vma=False,
    )
```

```python
import functools

import jax
import jax.numpy as jnp
from jax import lax
from jax.experimental import pallas as pl
from jax.experimental.pallas import tpu as pltpu
from jax.sharding import PartitionSpec as P

SHIFT_MAX = 2
F32 = jnp.float32
BF16 = jnp.bfloat16


def params(**kw):
    return pltpu.CompilerParams(vmem_limit_bytes=56 * 1024 * 1024, **kw)


def cost(flops, nbytes):
    return pl.CostEstimate(flops=int(flops), bytes_accessed=int(nbytes), transcendentals=0)


def dot_nt(a, b):
    return lax.dot_general(a, b, (((1,), (1,)), ((), ())), preferred_element_type=F32)


def dot_nn(a, b):
    return lax.dot_general(a, b, (((1,), (0,)), ((), ())), preferred_element_type=F32)


def row_col(rows, cols):
    return lax.broadcasted_iota(jnp.int32, (rows, cols), 0), lax.broadcasted_iota(jnp.int32, (rows, cols), 1)


def lesser_kernel(sel, g_ref, gamma_ref, out_ref):
    n = g_ref.shape[-1]
    half = n // 2
    e = pl.program_id(0)
    gamma = gamma_ref[0, pl.ds(e, 1), :]
    g_re, g_im = g_ref[0, 0, 0], g_ref[0, 0, 1]
    s_re = (g_re.astype(F32) * gamma).astype(BF16)
    s_im = (g_im.astype(F32) * gamma).astype(BF16)
    row, col = row_col(half, half)

    def real(i, j):
        i, j = slice(i * half, (i + 1) * half), slice(j * half, (j + 1) * half)
        return dot_nt(s_re[i], g_re[j]) + dot_nt(s_im[i], g_im[j])

    def imag(i, j):
        i, j = slice(i * half, (i + 1) * half), slice(j * half, (j + 1) * half)
        return dot_nt(s_im[i], g_re[j]) - dot_nt(s_re[i], g_im[j])

    for d in range(2):
        out_ref[0, d * half:(d + 1) * half, d * half:(d + 1) * half] = jnp.where(
            col >= row, real(d, d), imag(d, d)).astype(BF16)
    out_ref[0, :half, half:] = real(0, 1).astype(BF16)
    out_ref[0, half:, :half] = imag(1, 0).astype(BF16)


def lesser_packed(which, green, broadening):
    _, le, _, n, _ = green.shape
    return pl.pallas_call(
        lesser_kernel,
        out_shape=jax.ShapeDtypeStruct((le, n, n), BF16),
        grid_spec=pltpu.PrefetchScalarGridSpec(
            num_scalar_prefetch=1,
            grid=(le,),
            in_specs=[
                pl.BlockSpec((1, 1, 2, n, n), lambda e, sel: (sel[0], e, 0, 0, 0)),
                pl.BlockSpec((1, le, n), lambda e, sel: (sel[0], 0, 0)),
            ],
            out_specs=pl.BlockSpec((1, n, n), lambda e, sel: (e, 0, 0)),
        ),
        compiler_params=params(),
        cost_estimate=cost(le * 6 * n**3, le * n * n * 6),
        name="lesser",
    )(which[None], green, broadening)


def place_kernel(where, c_ref, *refs):
    full_ref, turned_ref = refs[-2:]
    full_ref[...] = c_ref[...]
    for q in range(c_ref.shape[0]):
        turned_ref[q] = c_ref[q].T


def place_coupling(where, piece, held):
    nk, rows, n = piece.shape
    each = 4
    alias = [] if held is None else list(held)
    return pl.pallas_call(
        place_kernel,
        out_shape=[jax.ShapeDtypeStruct((nk, n, n), BF16)] * 2,
        grid_spec=pltpu.PrefetchScalarGridSpec(
            num_scalar_prefetch=1,
            grid=(nk // each,),
            in_specs=[pl.BlockSpec((each, rows, n), lambda q, w: (q, 0, 0))]
            + [pl.BlockSpec(memory_space=pl.ANY)] * len(alias),
            out_specs=[
                pl.BlockSpec((each, rows, n), lambda q, w: (q, w[0], 0)),
                pl.BlockSpec((each, n, rows), lambda q, w: (q, 0, w[0])),
            ],
        ),
        input_output_aliases={2: 0, 3: 1} if alias else {},
        compiler_params=params(),
        cost_estimate=cost(nk * rows * n * 4, nk * rows * n * 6),
        name="place",
    )(where[None], piece, *alias)


def source_kernel(odd, w_ref, keep, recv, kz, rz, *refs):
    le = keep.shape[0]
    outs = refs[-2 * le:]

    def emit(order):
        line = [(ref, e) for ref in order for e in range(le)]
        for e in range(le):
            for ref, target in ((keep, outs[e]), (recv, outs[le + e])):
                at = [i for i, held in enumerate(order) if held is ref][0] * le + e
                total = None
                for s in range(1, SHIFT_MAX + 1):
                    for j, sign in ((0, s), (1, -s)):
                        source, index = line[at + sign]
                        term = w_ref[2 * (s - 1) + j] * source[index].astype(F32)
                        total = term if total is None else total + term
                target[0] = total.astype(BF16)

    @pl.when(odd[0] == 0)
    def _():
        emit((rz, keep, recv, kz))

    @pl.when(odd[0] == 1)
    def _():
        emit((kz, recv, keep, rz))


def sources(odd, weights, j, hk, keep, recv, kz, rz, held):
    le, n, _ = keep.shape
    rows = n // 4
    big = pl.BlockSpec((le, rows, n), lambda r, *_: (0, r, 0))
    first = pl.BlockSpec((1, rows, n), lambda r, *_: (0, r, 0))
    later = pl.BlockSpec((1, rows, n), lambda r, *_: (j, r, 0))
    shapes = [(1 if e == 0 else hk, n, n) for e in range(le)] * 2
    specs = [first if e == 0 else later for e in range(le)] * 2
    alias = {}
    extra = []
    if held is not None:
        for at, value in enumerate(held):
            if at % le:
                alias[6 + len(extra)] = at
                extra.append(value)
    return pl.pallas_call(
        source_kernel,
        out_shape=[jax.ShapeDtypeStruct(shape, BF16) for shape in shapes],
        grid_spec=pltpu.PrefetchScalarGridSpec(
            num_scalar_prefetch=2,
            grid=(n // rows,),
            in_specs=[big] * 4 + [pl.BlockSpec(memory_space=pl.ANY)] * len(extra),
            out_specs=specs,
        ),
        input_output_aliases=alias,
        compiler_params=params(),
        cost_estimate=cost(le * n * n * 16, le * n * n * 12),
        name="source",
    )(odd[None], weights, keep, recv, kz, rz, *extra)


def home_kernel(lk, pieces, slots, *refs):
    ins, (c_ref, ct_ref, x_ref, y_ref, q_ref) = refs[:pieces], refs[pieces:]
    each, rows, n = ins[0].shape
    count = pieces * each
    for s in range(pieces):
        for j in range(each):
            q_ref[s * each + j] = ins[s][j]
    tr, tc = 16, 256

    def tile(index, _):
        r = pl.ds(pl.multiple_of((index // (n // tc)) * tr, tr), tr)
        m = pl.ds(pl.multiple_of((index % (n // tc)) * tc, tc), tc)
        xs, ys = [None] * lk, [None] * lk
        for q in range(0, count, 4):
            px, py = [None] * lk, [None] * lk
            for p in (q, q + 2):
                c, ct = [c_ref[p + i, r, m] for i in range(2)], [ct_ref[p + i, r, m] for i in range(2)]
                for k in range(lk):
                    v = [q_ref[slots[k * count + p + i], r, m] for i in range(2)]
                    x, y = c[0] * v[0] + c[1] * v[1], ct[0] * v[0] + ct[1] * v[1]
                    px[k] = x if p == q else px[k] + x
                    py[k] = y if p == q else py[k] + y
            for k in range(lk):
                xs[k] = px[k] if q == 0 else xs[k] + px[k]
                ys[k] = py[k] if q == 0 else ys[k] + py[k]
        for k in range(lk):
            x_ref[k, r, m] = xs[k]
            y_ref[k, r, m] = ys[k]
        return 0

    lax.fori_loop(0, (rows // tr) * (n // tc), tile, 0)


def home_blocks(slots, pieces, full, turned, lk):
    each, n, _ = pieces[0].shape
    count = each * len(pieces)
    rows = n // 8
    block = lambda lead: pl.BlockSpec((lead, rows, n), lambda g, s: (0, g, 0))
    return pl.pallas_call(
        functools.partial(home_kernel, lk, len(pieces)),
        out_shape=[jax.ShapeDtypeStruct((lk, n, n), BF16)] * 2,
        grid_spec=pltpu.PrefetchScalarGridSpec(
            num_scalar_prefetch=1,
            grid=(n // rows,),
            in_specs=[block(each)] * len(pieces) + [block(count), block(count)],
            out_specs=[block(lk), block(lk)],
            scratch_shapes=[pltpu.VMEM((count, rows, n), BF16)],
        ),
        compiler_params=params(),
        cost_estimate=cost(4 * lk * count * n * n, n * n * (6 * count + 4 * lk)),
        name="home",
    )(slots, *pieces, full, turned)


def rows_kernel(pieces, mine, slots, *refs):
    a_refs, b_refs, refs = refs[:pieces], refs[pieces:2 * pieces], refs[2 * pieces:]
    c_ref, out_ref, re_ref, im_ref = (refs[0],) + refs[-3:]
    each, rows, cols = a_refs[0].shape
    count = pieces * each
    row, col = row_col(rows, cols)
    above = (col - row) + (pl.program_id(0) * cols - mine[0] * rows)
    for s in range(pieces):
        for j in range(each):
            a, b = a_refs[s][j].astype(F32), b_refs[s][j].astype(F32).T
            re_ref[s * each + j] = jnp.where(above >= 0, a, b).astype(BF16)
            im_ref[s * each + j] = jnp.where(above < 0, a, jnp.where(above > 0, -b, 0.0)).astype(BF16)
    tr, kg = 16, 8

    def tile(index, _):
        r = pl.ds(pl.multiple_of((index % (rows // tr)) * tr, tr), tr)
        k0 = (index // (rows // tr)) * kg
        us, vs = [None] * kg, [None] * kg
        for q in range(0, count, 4):
            pu, pv = [None] * kg, [None] * kg
            for p in (q, q + 2):
                c = [c_ref[p + i, r, :] for i in range(2)]
                for k in range(kg):
                    slot = [slots[(k0 + k) * count + p + i] for i in range(2)]
                    u = c[0] * re_ref[slot[0], r, :] + c[1] * re_ref[slot[1], r, :]
                    v = c[0] * im_ref[slot[0], r, :] + c[1] * im_ref[slot[1], r, :]
                    pu[k] = u if p == q else pu[k] + u
                    pv[k] = v if p == q else pv[k] + v
            for k in range(kg):
                us[k] = pu[k] if q == 0 else us[k] + pu[k]
                vs[k] = pv[k] if q == 0 else vs[k] + pv[k]
        for k in range(kg):
            out_ref[k0 + k, 0, 0, r, :] = us[k]
            out_ref[k0 + k, 0, 1, r, :] = vs[k]
        return 0

    lax.fori_loop(0, (rows // tr) * (count // kg), tile, 0)


def own_rows(mine, slots, pieces, coupling, energy, le, held):
    each, n, _ = pieces[0].shape
    count, rows, _ = coupling.shape
    cols = rows
    alias = [] if held is None else [held]
    in_specs = (
        [pl.BlockSpec((each, rows, cols), lambda t, mine, slots: (0, mine[0], t))] * len(pieces)
        + [pl.BlockSpec((each, cols, rows), lambda t, mine, slots: (0, t, mine[0]))] * len(pieces)
        + [pl.BlockSpec((count, rows, cols), lambda t, mine, slots: (0, 0, t))]
        + [pl.BlockSpec(memory_space=pl.ANY)] * len(alias)
    )
    return pl.pallas_call(
        functools.partial(rows_kernel, len(pieces)),
        out_shape=jax.ShapeDtypeStruct((count, le, 2, rows, n), BF16),
        grid_spec=pltpu.PrefetchScalarGridSpec(
            num_scalar_prefetch=2,
            grid=(n // cols,),
            in_specs=in_specs,
            out_specs=pl.BlockSpec((count, 1, 2, rows, cols), lambda t, mine, slots: (0, energy, 0, 0, t)),
            scratch_shapes=[pltpu.VMEM((count, rows, cols), BF16)] * 2,
        ),
        input_output_aliases={2 + len(in_specs) - 1: 0} if alias else {},
        compiler_params=params(),
        cost_estimate=cost(4 * count * count * rows * n, rows * n * count * 10),
        name="rows",
    )(mine[None], slots, *pieces, *pieces, coupling, *alias)


def density_terms(energy, g_ref, gamma_ref, x_ref, y_ref):
    n = g_ref.shape[-1]
    gamma = gamma_ref[0, energy:energy + 1, :]
    g_re, g_im = g_ref[0, 0, 0], g_ref[0, 0, 1]
    row, col = row_col(n, n)
    x, yt = x_ref[0].astype(F32), y_ref[0].astype(F32).T
    s_re = jnp.where(col >= row, x, yt).astype(BF16)
    s_im = jnp.where(col < row, x, jnp.where(col > row, -yt, 0.0)).astype(BF16)
    scaled_re = (g_re.astype(F32) * gamma).astype(BF16).astype(F32)
    scaled_im = (g_im.astype(F32) * gamma).astype(BF16).astype(F32)
    m_re = (dot_nn(g_re, s_re) - dot_nn(g_im, s_im) + scaled_re).astype(BF16)
    m_im = (dot_nn(g_re, s_im) + dot_nn(g_im, s_re) + scaled_im).astype(BF16)
    return dot_nt(m_re, g_re) + dot_nt(m_im, g_im), dot_nt(m_im, g_re) - dot_nt(m_re, g_im)


def first_density_kernel(energy, first, g_ref, gamma_ref, x_ref, y_ref, *refs):
    for c, d in enumerate(density_terms(energy, g_ref, gamma_ref, x_ref, y_ref)):
        refs[-1][0, c] = d if first else d + refs[0][0, c]


def first_density(energy, green, broadening, x, y, held):
    lk, le, _, n, _ = green.shape
    alias = [] if held is None else [held]
    pair = pl.BlockSpec((1, 2, n, n), lambda k: (k, 0, 0, 0))
    one = pl.BlockSpec((1, n, n), lambda k: (k, 0, 0))
    return pl.pallas_call(
        functools.partial(first_density_kernel, energy, held is None),
        out_shape=jax.ShapeDtypeStruct((lk, 2, n, n), F32),
        grid=(lk,),
        in_specs=[
            pl.BlockSpec((1, 1, 2, n, n), lambda k: (k, energy, 0, 0, 0)),
            pl.BlockSpec((1, le, n), lambda k: (k, 0, 0)),
            one,
            one,
        ] + [pair] * len(alias),
        out_specs=pair,
        compiler_params=params(),
        cost_estimate=cost(16 * lk * n**3, lk * n * n * 20),
        name="density",
    )(green, broadening, x, y, *alias)


def last_density_kernel(scale, energy, odd, g_ref, gamma_ref, x_ref, y_ref, held_ref, keep_ref, send_ref, d_ref):
    groups, _, rows, _ = keep_ref.shape
    for c, d in enumerate(density_terms(energy, g_ref, gamma_ref, x_ref, y_ref)):
        d_ref[c] = (d + held_ref[0, c]) * scale
        for g in range(groups):
            mine = pl.multiple_of((2 * g + odd[0]) * rows, rows)
            other = pl.multiple_of((2 * g + 1 - odd[0]) * rows, rows)
            keep_ref[g, c] = d_ref[c, pl.ds(mine, rows), :].astype(BF16)
            send_ref[g, c] = d_ref[c, pl.ds(other, rows), :].astype(BF16)


def last_density(scale, energy, k, groups, odd, green, broadening, x, y, held):
    _, le, _, n, _ = green.shape
    rows = n // (2 * groups)
    one = pl.BlockSpec((1, n, n), lambda i, odd: (k, 0, 0))
    out = pl.BlockSpec((groups, 2, rows, n), lambda i, odd: (0, 0, 0, 0))
    return pl.pallas_call(
        functools.partial(last_density_kernel, scale, energy),
        out_shape=[jax.ShapeDtypeStruct((groups, 2, rows, n), BF16)] * 2,
        grid_spec=pltpu.PrefetchScalarGridSpec(
            num_scalar_prefetch=1,
            grid=(1,),
            in_specs=[
                pl.BlockSpec((1, 1, 2, n, n), lambda i, odd: (k, energy, 0, 0, 0)),
                pl.BlockSpec((1, le, n), lambda i, odd: (k, 0, 0)),
                one,
                one,
                pl.BlockSpec((1, 2, n, n), lambda i, odd: (k, 0, 0, 0)),
            ],
            out_specs=[out, out],
            scratch_shapes=[pltpu.VMEM((2, n, n), F32)],
        ),
        compiler_params=params(),
        cost_estimate=cost(16 * n**3, n * n * 20),
        name="density",
    )(odd[None], green, broadening, x, y, held)


def pair_sum_kernel(group, keep_ref, recv_ref, *outs):
    groups = len(outs)
    for d in range(groups):
        at = lax.rem(group[0] + d, groups)
        outs[d][...] = (keep_ref[at].astype(F32) + recv_ref[at].astype(F32)).astype(BF16)


def pair_sum(group, keep, recv):
    groups = keep.shape[0]
    vmem = pl.BlockSpec(memory_space=pltpu.VMEM)
    return pl.pallas_call(
        pair_sum_kernel,
        out_shape=[jax.ShapeDtypeStruct(keep.shape[1:], BF16)] * groups,
        in_specs=[pl.BlockSpec(memory_space=pltpu.SMEM), vmem, vmem],
        out_specs=[vmem] * groups,
        compiler_params=params(),
        cost_estimate=cost(keep.size, keep.size * 6),
        name="pairsum",
    )(group[None], keep, recv)


def on_device(green_ret, broadening, coupling, shift_steps, mode_weight, occupation, momentum_map):
    lk, le, _, n, _ = green_ret.shape
    ne, nm = lax.axis_size("energy"), lax.axis_size("mom")
    if le != SHIFT_MAX or lk % 2 or ne % 2 or nm & (nm - 1):
        raise ValueError("unsupported sizes")
    hk, groups = lk // 2, ne // 2
    me, mine = lax.axis_index("energy").astype(jnp.int32), lax.axis_index("mom").astype(jnp.int32)
    odd, group = me & 1, me >> 1
    pairs = [(i, i ^ 1) for i in range(ne)]
    away = [(i, i + (2 if i % 2 else -2)) for i in range(ne) if 0 <= i + (2 if i % 2 else -2) < ne]
    across = [(i, i + (-2 if i % 2 else 2)) for i in range(ne) if 0 <= i + (-2 if i % 2 else 2) < ne]
    strides = []
    while (nm >> (len(strides) + 1)) > 0:
        strides.append(nm >> (len(strides) + 1))

    def over_energy(name, x, perm):
        with jax.named_scope(name):
            return lax.ppermute(x, "energy", perm)

    def swap(name, x, stride):
        with jax.named_scope(name):
            return lax.ppermute(x, "mom", [(i, i ^ stride) for i in range(nm)])

    def spread(name, x):
        held = [x]
        for at, s in enumerate(strides):
            held = held + [swap(f"{name}_{at}_{i}", piece, s) for i, piece in enumerate(held)]
        return held

    def scoped(name, f, *args):
        with jax.named_scope(name):
            return f(*args)

    order = [0]
    for s in strides:
        order = order + [o ^ s for o in order]

    weights = []
    for s in range(1, SHIFT_MAX + 1):
        held = shift_steps == s
        weights.append(jnp.sum(jnp.where(held, mode_weight * (occupation + 1.0), 0.0)))
        weights.append(jnp.sum(jnp.where(held, mode_weight * occupation, 0.0)))
    weights = jnp.stack(weights)

    owner, inner = momentum_map // lk, momentum_map % lk
    place = jnp.zeros_like(owner)
    for at, o in enumerate(order):
        place = jnp.where((owner ^ mine) == o, at, place)
    slots = (place * lk + ((inner // hk) ^ odd) * hk + inner % hk).astype(jnp.int32)
    own_slots = lax.dynamic_slice_in_dim(slots, mine * lk, lk, 0).reshape(-1)
    all_slots = slots.reshape(-1)

    coupling_pieces = spread("cpl", coupling)

    send = [scoped(f"lesser_s{j}", lesser_packed, (1 - odd) * hk + j, green_ret, broadening) for j in range(hk)]
    recv = [over_energy(f"pair_{j}", send[j], pairs) for j in range(hk)]
    keep = [scoped(f"lesser_k{j}", lesser_packed, odd * hk + j, green_ret, broadening) for j in range(hk)]
    kz = [over_energy(f"kz_{j}", keep[j], away) for j in range(hk)]
    rz = [over_energy(f"rz_{j}", recv[j], across) for j in range(hk)]
    got, last = [], None
    for j in range(hk):
        last = scoped(f"source_{j}", sources, odd, weights, j, hk, keep[j], recv[j], kz[j], rz[j], last)
        got.append(last)

    placed = None
    for at, o in enumerate(order):
        placed = scoped(f"place_{at}", place_coupling, mine ^ o, coupling_pieces[at], placed)
    full, turned = placed

    held_rows, held_density = None, None
    scale = 1.0 / (le * ne)
    late = []
    for e in range(le):
        use = [got[j] for j in range(hk)] if e == 0 else [last]
        fresh = [spread(f"fresh{e}{j}", part[e]) for j, part in enumerate(use)]
        back = [
            spread(f"back{e}{j}", over_energy(f"ret{e}{j}", part[le + e], pairs)) for j, part in enumerate(use)
        ]
        pieces = [part[at] for at in range(nm) for part in fresh + back]
        x, y = scoped(f"home_{e}", home_blocks, own_slots, pieces, full, turned, lk)
        if e < le - 1:
            held_density = scoped(f"density_{e}", first_density, e, green_ret, broadening, x, y, held_density)
        else:
            for k in range(lk):
                kept, sent = scoped(
                    f"density_{e}{k}", last_density, scale, e, k, groups, odd, green_ret, broadening, x, y, held_density)
                other = over_energy(f"sum_{k}", sent, pairs)
                parts = scoped(f"pairsum_{k}", pair_sum, group, kept, other)
                total = parts[0].astype(F32)
                for d in range(1, groups):
                    perm = [(i, (i + 2 * d) % ne) for i in range(ne)]
                    total = total + over_energy(f"line_{k}{d}", parts[d], perm).astype(F32)
                late.append(total)
        held_rows = scoped(f"rows_{e}", own_rows, mine, all_slots, pieces, coupling, e, le, held_rows)
    density = jnp.transpose(jnp.stack(late), (2, 0, 1, 3))
    return held_rows, density


def solution(mesh):
    return jax.shard_map(
        on_device,
        mesh=mesh,
        in_specs=(
            P("mom", "energy", None, None, None),
            P("mom", "energy", None),
            P(None, "mom", None),
            P(),
            P(),
            P(),
            P(),
        ),
        out_specs=(P(None, "energy", None, "mom", None), P("energy", "mom", None, None)),
        check_vma=False,
    )
```

```python
import functools

import jax
import jax.numpy as jnp
from jax import lax
from jax.experimental import pallas as pl
from jax.experimental.pallas import tpu as pltpu
from jax.sharding import PartitionSpec as P


SHIFT_MAX = 2
F32 = jnp.float32
BF16 = jnp.bfloat16


def params(**kw):
    return pltpu.CompilerParams(vmem_limit_bytes=56 * 1024 * 1024, **kw)


def cost(flops, nbytes):
    return pl.CostEstimate(flops=int(flops), bytes_accessed=int(nbytes), transcendentals=0)


def dot_nt(a, b):
    return lax.dot_general(a, b, (((1,), (1,)), ((), ())), preferred_element_type=F32)


def dot_nn(a, b):
    return lax.dot_general(a, b, (((1,), (0,)), ((), ())), preferred_element_type=F32)


def row_col(rows, cols):
    return lax.broadcasted_iota(jnp.int32, (rows, cols), 0), lax.broadcasted_iota(jnp.int32, (rows, cols), 1)


def lesser_kernel(sel, g_ref, gamma_ref, out_ref):
    n = g_ref.shape[-1]
    half = n // 2
    e = pl.program_id(0)
    gamma = gamma_ref[0, pl.ds(e, 1), :]
    g_re, g_im = g_ref[0, 0, 0], g_ref[0, 0, 1]
    s_re = (g_re.astype(F32) * gamma).astype(BF16)
    s_im = (g_im.astype(F32) * gamma).astype(BF16)
    row, col = row_col(half, half)

    def real(i, j):
        i, j = slice(i * half, (i + 1) * half), slice(j * half, (j + 1) * half)
        return dot_nt(s_re[i], g_re[j]) + dot_nt(s_im[i], g_im[j])

    def imag(i, j):
        i, j = slice(i * half, (i + 1) * half), slice(j * half, (j + 1) * half)
        return dot_nt(s_im[i], g_re[j]) - dot_nt(s_re[i], g_im[j])

    for d in range(2):
        out_ref[0, d * half:(d + 1) * half, d * half:(d + 1) * half] = jnp.where(
            col >= row, real(d, d), imag(d, d)).astype(BF16)
    out_ref[0, :half, half:] = real(0, 1).astype(BF16)
    out_ref[0, half:, :half] = imag(1, 0).astype(BF16)


def lesser_packed(which, green, broadening):
    _, le, _, n, _ = green.shape
    return pl.pallas_call(
        lesser_kernel,
        out_shape=jax.ShapeDtypeStruct((le, n, n), BF16),
        grid_spec=pltpu.PrefetchScalarGridSpec(
            num_scalar_prefetch=1,
            grid=(le,),
            in_specs=[
                pl.BlockSpec((1, 1, 2, n, n), lambda e, sel: (sel[0], e, 0, 0, 0)),
                pl.BlockSpec((1, le, n), lambda e, sel: (sel[0], 0, 0)),
            ],
            out_specs=pl.BlockSpec((1, n, n), lambda e, sel: (e, 0, 0)),
        ),
        compiler_params=params(),
        cost_estimate=cost(le * 6 * n**3, le * n * n * 6),
        name="lesser",
    )(which[None], green, broadening)


def place_kernel(where, c_ref, *refs):
    full_ref, turned_ref = refs[-2:]
    full_ref[...] = c_ref[...]
    for q in range(c_ref.shape[0]):
        turned_ref[q] = c_ref[q].T


def place_coupling(where, piece, held):
    nk, rows, n = piece.shape
    each = 4
    alias = [] if held is None else list(held)
    return pl.pallas_call(
        place_kernel,
        out_shape=[jax.ShapeDtypeStruct((nk, n, n), BF16)] * 2,
        grid_spec=pltpu.PrefetchScalarGridSpec(
            num_scalar_prefetch=1,
            grid=(nk // each,),
            in_specs=[pl.BlockSpec((each, rows, n), lambda q, w: (q, 0, 0))]
            + [pl.BlockSpec(memory_space=pl.ANY)] * len(alias),
            out_specs=[
                pl.BlockSpec((each, rows, n), lambda q, w: (q, w[0], 0)),
                pl.BlockSpec((each, n, rows), lambda q, w: (q, 0, w[0])),
            ],
        ),
        input_output_aliases={2: 0, 3: 1} if alias else {},
        compiler_params=params(),
        cost_estimate=cost(nk * rows * n * 4, nk * rows * n * 6),
        name="place",
    )(where[None], piece, *alias)


def source_kernel(odd, w_ref, keep, recv, kz, rz, *refs):
    le = keep.shape[0]
    outs = refs[-2 * le:]

    def emit(order):
        line = [(ref, e) for ref in order for e in range(le)]
        for e in range(le):
            for ref, target in ((keep, outs[e]), (recv, outs[le + e])):
                at = [i for i, held in enumerate(order) if held is ref][0] * le + e
                total = None
                for s in range(1, SHIFT_MAX + 1):
                    for j, sign in ((0, s), (1, -s)):
                        source, index = line[at + sign]
                        term = w_ref[2 * (s - 1) + j] * source[index].astype(F32)
                        total = term if total is None else total + term
                target[0] = total.astype(BF16)

    @pl.when(odd[0] == 0)
    def _():
        emit((rz, keep, recv, kz))

    @pl.when(odd[0] == 1)
    def _():
        emit((kz, recv, keep, rz))


def sources(odd, weights, j, hk, keep, recv, kz, rz, held):
    le, n, _ = keep.shape
    rows = n // 4
    big = pl.BlockSpec((le, rows, n), lambda r, *_: (0, r, 0))
    first = pl.BlockSpec((1, rows, n), lambda r, *_: (0, r, 0))
    later = pl.BlockSpec((1, rows, n), lambda r, *_: (j, r, 0))
    shapes = [(1 if e == 0 else hk, n, n) for e in range(le)] * 2
    specs = [first if e == 0 else later for e in range(le)] * 2
    alias = {}
    extra = []
    if held is not None:
        for at, value in enumerate(held):
            if at % le:
                alias[6 + len(extra)] = at
                extra.append(value)
    return pl.pallas_call(
        source_kernel,
        out_shape=[jax.ShapeDtypeStruct(shape, BF16) for shape in shapes],
        grid_spec=pltpu.PrefetchScalarGridSpec(
            num_scalar_prefetch=2,
            grid=(n // rows,),
            in_specs=[big] * 4 + [pl.BlockSpec(memory_space=pl.ANY)] * len(extra),
            out_specs=specs,
        ),
        input_output_aliases=alias,
        compiler_params=params(),
        cost_estimate=cost(le * n * n * 16, le * n * n * 12),
        name="source",
    )(odd[None], weights, keep, recv, kz, rz, *extra)


def home_kernel(lk, pieces, slots, *refs):
    ins, (c_ref, ct_ref, x_ref, y_ref, q_ref) = refs[:pieces], refs[pieces:]
    each, rows, n = ins[0].shape
    count = pieces * each
    for s in range(pieces):
        for j in range(each):
            q_ref[s * each + j] = ins[s][j]
    tr, tc = 16, 256

    def tile(index, _):
        r = pl.ds(pl.multiple_of((index // (n // tc)) * tr, tr), tr)
        m = pl.ds(pl.multiple_of((index % (n // tc)) * tc, tc), tc)
        xs, ys = [None] * lk, [None] * lk
        for q in range(0, count, 4):
            px, py = [None] * lk, [None] * lk
            for p in (q, q + 2):
                c, ct = [c_ref[p + i, r, m] for i in range(2)], [ct_ref[p + i, r, m] for i in range(2)]
                for k in range(lk):
                    v = [q_ref[slots[k * count + p + i], r, m] for i in range(2)]
                    x, y = c[0] * v[0] + c[1] * v[1], ct[0] * v[0] + ct[1] * v[1]
                    px[k] = x if p == q else px[k] + x
                    py[k] = y if p == q else py[k] + y
            for k in range(lk):
                xs[k] = px[k] if q == 0 else xs[k] + px[k]
                ys[k] = py[k] if q == 0 else ys[k] + py[k]
        for k in range(lk):
            x_ref[k, r, m] = xs[k]
            y_ref[k, r, m] = ys[k]
        return 0

    lax.fori_loop(0, (rows // tr) * (n // tc), tile, 0)


def home_blocks(slots, pieces, full, turned, lk):
    each, n, _ = pieces[0].shape
    count = each * len(pieces)
    rows = n // 8
    block = lambda lead: pl.BlockSpec((lead, rows, n), lambda g, s: (0, g, 0))
    return pl.pallas_call(
        functools.partial(home_kernel, lk, len(pieces)),
        out_shape=[jax.ShapeDtypeStruct((lk, n, n), BF16)] * 2,
        grid_spec=pltpu.PrefetchScalarGridSpec(
            num_scalar_prefetch=1,
            grid=(n // rows,),
            in_specs=[block(each)] * len(pieces) + [block(count), block(count)],
            out_specs=[block(lk), block(lk)],
            scratch_shapes=[pltpu.VMEM((count, rows, n), BF16)],
        ),
        compiler_params=params(),
        cost_estimate=cost(4 * lk * count * n * n, n * n * (6 * count + 4 * lk)),
        name="home",
    )(slots, *pieces, full, turned)


def rows_kernel(pieces, mine, slots, *refs):
    a_refs, b_refs, refs = refs[:pieces], refs[pieces:2 * pieces], refs[2 * pieces:]
    c_ref, out_ref, re_ref, im_ref = (refs[0],) + refs[-3:]
    each, rows, cols = a_refs[0].shape
    count = pieces * each
    row, col = row_col(rows, cols)
    above = (col - row) + (pl.program_id(0) * cols - mine[0] * rows)
    for s in range(pieces):
        for j in range(each):
            a, b = a_refs[s][j].astype(F32), b_refs[s][j].astype(F32).T
            re_ref[s * each + j] = jnp.where(above >= 0, a, b).astype(BF16)
            im_ref[s * each + j] = jnp.where(above < 0, a, jnp.where(above > 0, -b, 0.0)).astype(BF16)
    tr, kg, tc = 16, 4, 256
    wide = cols // tc

    def tile(index, _):
        r = pl.ds(pl.multiple_of(((index // wide) % (rows // tr)) * tr, tr), tr)
        m = pl.ds(pl.multiple_of((index % wide) * tc, tc), tc)
        k0 = (index // (wide * (rows // tr))) * kg
        us, vs = [None] * kg, [None] * kg
        for q in range(0, count, 4):
            pu, pv = [None] * kg, [None] * kg
            for p in (q, q + 2):
                c = [c_ref[p + i, r, m] for i in range(2)]
                for k in range(kg):
                    slot = [slots[(k0 + k) * count + p + i] for i in range(2)]
                    u = c[0] * re_ref[slot[0], r, m] + c[1] * re_ref[slot[1], r, m]
                    v = c[0] * im_ref[slot[0], r, m] + c[1] * im_ref[slot[1], r, m]
                    pu[k] = u if p == q else pu[k] + u
                    pv[k] = v if p == q else pv[k] + v
            for k in range(kg):
                us[k] = pu[k] if q == 0 else us[k] + pu[k]
                vs[k] = pv[k] if q == 0 else vs[k] + pv[k]
        for k in range(kg):
            out_ref[k0 + k, 0, 0, r, m] = us[k]
            out_ref[k0 + k, 0, 1, r, m] = vs[k]
        return 0

    lax.fori_loop(0, wide * (rows // tr) * (count // kg), tile, 0)


def own_rows(mine, slots, pieces, coupling, energy, le, held):
    each, n, _ = pieces[0].shape
    count, rows, _ = coupling.shape
    cols = n // 2
    alias = [] if held is None else [held]
    in_specs = (
        [pl.BlockSpec((each, rows, cols), lambda t, mine, slots: (0, mine[0], t))] * len(pieces)
        + [pl.BlockSpec((each, cols, rows), lambda t, mine, slots: (0, t, mine[0]))] * len(pieces)
        + [pl.BlockSpec((count, rows, cols), lambda t, mine, slots: (0, 0, t))]
        + [pl.BlockSpec(memory_space=pl.ANY)] * len(alias)
    )
    return pl.pallas_call(
        functools.partial(rows_kernel, len(pieces)),
        out_shape=jax.ShapeDtypeStruct((count, le, 2, rows, n), BF16),
        grid_spec=pltpu.PrefetchScalarGridSpec(
            num_scalar_prefetch=2,
            grid=(n // cols,),
            in_specs=in_specs,
            out_specs=pl.BlockSpec((count, 1, 2, rows, cols), lambda t, mine, slots: (0, energy, 0, 0, t)),
            scratch_shapes=[pltpu.VMEM((count, rows, cols), BF16)] * 2,
        ),
        input_output_aliases={2 + len(in_specs) - 1: 0} if alias else {},
        compiler_params=params(),
        cost_estimate=cost(4 * count * count * rows * n, rows * n * count * 10),
        name="rows",
    )(mine[None], slots, *pieces, *pieces, coupling, *alias)


def density_terms(energy, g_ref, gamma_ref, x_ref, y_ref):
    n = g_ref.shape[-1]
    gamma = gamma_ref[0, energy:energy + 1, :]
    g_re, g_im = g_ref[0, 0, 0], g_ref[0, 0, 1]
    row, col = row_col(n, n)
    x, yt = x_ref[0].astype(F32), y_ref[0].astype(F32).T
    s_re = jnp.where(col >= row, x, yt).astype(BF16)
    s_im = jnp.where(col < row, x, jnp.where(col > row, -yt, 0.0)).astype(BF16)
    scaled_re = (g_re.astype(F32) * gamma).astype(BF16).astype(F32)
    scaled_im = (g_im.astype(F32) * gamma).astype(BF16).astype(F32)
    m_re = (dot_nn(g_re, s_re) - dot_nn(g_im, s_im) + scaled_re).astype(BF16)
    m_im = (dot_nn(g_re, s_im) + dot_nn(g_im, s_re) + scaled_im).astype(BF16)
    return dot_nt(m_re, g_re) + dot_nt(m_im, g_im), dot_nt(m_im, g_re) - dot_nt(m_re, g_im)


def first_density_kernel(energy, first, g_ref, gamma_ref, x_ref, y_ref, *refs):
    for c, d in enumerate(density_terms(energy, g_ref, gamma_ref, x_ref, y_ref)):
        refs[-1][0, c] = d if first else d + refs[0][0, c]


def first_density(energy, green, broadening, x, y, held):
    lk, le, _, n, _ = green.shape
    alias = [] if held is None else [held]
    pair = pl.BlockSpec((1, 2, n, n), lambda k: (k, 0, 0, 0))
    one = pl.BlockSpec((1, n, n), lambda k: (k, 0, 0))
    return pl.pallas_call(
        functools.partial(first_density_kernel, energy, held is None),
        out_shape=jax.ShapeDtypeStruct((lk, 2, n, n), F32),
        grid=(lk,),
        in_specs=[
            pl.BlockSpec((1, 1, 2, n, n), lambda k: (k, energy, 0, 0, 0)),
            pl.BlockSpec((1, le, n), lambda k: (k, 0, 0)),
            one,
            one,
        ] + [pair] * len(alias),
        out_specs=pair,
        compiler_params=params(),
        cost_estimate=cost(16 * lk * n**3, lk * n * n * 20),
        name="density",
    )(green, broadening, x, y, *alias)


def last_density_kernel(scale, energy, odd, g_ref, gamma_ref, x_ref, y_ref, held_ref, keep_ref, send_ref, d_ref):
    groups, _, rows, _ = keep_ref.shape
    for c, d in enumerate(density_terms(energy, g_ref, gamma_ref, x_ref, y_ref)):
        d_ref[c] = (d + held_ref[0, c]) * scale
        for g in range(groups):
            mine = pl.multiple_of((2 * g + odd[0]) * rows, rows)
            other = pl.multiple_of((2 * g + 1 - odd[0]) * rows, rows)
            keep_ref[g, c] = d_ref[c, pl.ds(mine, rows), :].astype(BF16)
            send_ref[g, c] = d_ref[c, pl.ds(other, rows), :].astype(BF16)


def last_density(scale, energy, k, groups, odd, green, broadening, x, y, held):
    _, le, _, n, _ = green.shape
    rows = n // (2 * groups)
    one = pl.BlockSpec((1, n, n), lambda i, odd: (k, 0, 0))
    out = pl.BlockSpec((groups, 2, rows, n), lambda i, odd: (0, 0, 0, 0))
    return pl.pallas_call(
        functools.partial(last_density_kernel, scale, energy),
        out_shape=[jax.ShapeDtypeStruct((groups, 2, rows, n), BF16)] * 2,
        grid_spec=pltpu.PrefetchScalarGridSpec(
            num_scalar_prefetch=1,
            grid=(1,),
            in_specs=[
                pl.BlockSpec((1, 1, 2, n, n), lambda i, odd: (k, energy, 0, 0, 0)),
                pl.BlockSpec((1, le, n), lambda i, odd: (k, 0, 0)),
                one,
                one,
                pl.BlockSpec((1, 2, n, n), lambda i, odd: (k, 0, 0, 0)),
            ],
            out_specs=[out, out],
            scratch_shapes=[pltpu.VMEM((2, n, n), F32)],
        ),
        compiler_params=params(),
        cost_estimate=cost(16 * n**3, n * n * 20),
        name="density",
    )(odd[None], green, broadening, x, y, held)


def pair_sum_kernel(group, keep_ref, recv_ref, *outs):
    groups = len(outs)
    for d in range(groups):
        at = lax.rem(group[0] + d, groups)
        outs[d][...] = (keep_ref[at].astype(F32) + recv_ref[at].astype(F32)).astype(BF16)


def pair_sum(group, keep, recv):
    groups = keep.shape[0]
    vmem = pl.BlockSpec(memory_space=pltpu.VMEM)
    return pl.pallas_call(
        pair_sum_kernel,
        out_shape=[jax.ShapeDtypeStruct(keep.shape[1:], BF16)] * groups,
        in_specs=[pl.BlockSpec(memory_space=pltpu.SMEM), vmem, vmem],
        out_specs=[vmem] * groups,
        compiler_params=params(),
        cost_estimate=cost(keep.size, keep.size * 6),
        name="pairsum",
    )(group[None], keep, recv)


def staged(green_ret, broadening, coupling, shift_steps, mode_weight, occupation, momentum_map):
    lk, le, _, _, _ = green_ret.shape
    ne, nm = lax.axis_size("energy"), lax.axis_size("mom")
    if le != SHIFT_MAX or lk % 2 or ne % 2 or nm & (nm - 1):
        raise ValueError("unsupported sizes")
    hk, groups = lk // 2, ne // 2
    me, mine = lax.axis_index("energy").astype(jnp.int32), lax.axis_index("mom").astype(jnp.int32)
    odd, group = me & 1, me >> 1
    pairs = [(i, i ^ 1) for i in range(ne)]
    away = [(i, i + (2 if i % 2 else -2)) for i in range(ne) if 0 <= i + (2 if i % 2 else -2) < ne]
    across = [(i, i + (-2 if i % 2 else 2)) for i in range(ne) if 0 <= i + (-2 if i % 2 else 2) < ne]
    strides = []
    while (nm >> (len(strides) + 1)) > 0:
        strides.append(nm >> (len(strides) + 1))

    def over_energy(x, perm):
        return lax.ppermute(x, "energy", perm)

    def swap(x, stride):
        return lax.ppermute(x, "mom", [(i, i ^ stride) for i in range(nm)])

    def spread(x):
        held = [x]
        for s in strides:
            held = held + [swap(piece, s) for piece in held]
        return held

    order = [0]
    for s in strides:
        order = order + [o ^ s for o in order]

    weights = []
    for s in range(1, SHIFT_MAX + 1):
        held = shift_steps == s
        weights.append(jnp.sum(jnp.where(held, mode_weight * (occupation + 1.0), 0.0)))
        weights.append(jnp.sum(jnp.where(held, mode_weight * occupation, 0.0)))
    weights = jnp.stack(weights)

    owner, inner = momentum_map // lk, momentum_map % lk
    place = jnp.zeros_like(owner)
    for at, o in enumerate(order):
        place = jnp.where((owner ^ mine) == o, at, place)
    slots = (place * lk + ((inner // hk) ^ odd) * hk + inner % hk).astype(jnp.int32)
    own_slots = lax.dynamic_slice_in_dim(slots, mine * lk, lk, 0).reshape(-1)
    all_slots = slots.reshape(-1)

    coupling_pieces = spread(coupling)

    send = [lesser_packed((1 - odd) * hk + j, green_ret, broadening) for j in range(hk)]
    recv = [over_energy(send[j], pairs) for j in range(hk)]
    keep = [lesser_packed(odd * hk + j, green_ret, broadening) for j in range(hk)]
    kz = [over_energy(keep[j], away) for j in range(hk)]
    rz = [over_energy(recv[j], across) for j in range(hk)]
    got, last = [], None
    for j in range(hk):
        last = sources(odd, weights, j, hk, keep[j], recv[j], kz[j], rz[j], last)
        got.append(last)

    placed = None
    for at in sorted(range(nm), key=lambda a: (a & 1, a)):
        placed = place_coupling(mine ^ order[at], coupling_pieces[at], placed)
    full, turned = placed

    held_rows, held_density = None, None
    scale = 1.0 / (le * ne)
    late = []
    for e in range(le):
        use = [got[j] for j in range(hk)] if e == 0 else [last]
        fresh = [spread(part[e]) for part in use]
        back = [spread(over_energy(part[le + e], pairs)) for part in use]
        pieces = [part[at] for at in range(nm) for part in fresh + back]
        x, y = home_blocks(own_slots, pieces, full, turned, lk)
        if e < le - 1:
            held_density = first_density(e, green_ret, broadening, x, y, held_density)
        else:
            for k in range(lk):
                kept, sent = last_density(
                    scale, e, k, groups, odd, green_ret, broadening, x, y, held_density)
                other = over_energy(sent, pairs)
                parts = pair_sum(group, kept, other)
                total = parts[0].astype(F32)
                for d in range(1, groups):
                    perm = [(i, (i + 2 * d) % ne) for i in range(ne)]
                    total = total + over_energy(parts[d], perm).astype(F32)
                late.append(total)
        held_rows = own_rows(mine, all_slots, pieces, coupling, e, le, held_rows)
    density = jnp.transpose(jnp.stack(late), (2, 0, 1, 3))
    return held_rows, density


def solution(mesh):
    return jax.shard_map(
        staged,
        mesh=mesh,
        in_specs=(
            P("mom", "energy", None, None, None),
            P("mom", "energy", None),
            P(None, "mom", None),
            P(),
            P(),
            P(),
            P(),
        ),
        out_specs=(P(None, "energy", None, "mom", None), P("energy", "mom", None, None)),
        check_vma=False,
    )
```

```python
import functools

import jax
import jax.numpy as jnp
from jax import lax
from jax.experimental import pallas as pl
from jax.experimental.pallas import tpu as pltpu
from jax.sharding import PartitionSpec as P


SHIFT_MAX = 2
F32 = jnp.float32
BF16 = jnp.bfloat16


def params(mib):
    return pltpu.CompilerParams(vmem_limit_bytes=mib * 1024 * 1024)


def cost(flops, nbytes):
    return pl.CostEstimate(flops=int(flops), bytes_accessed=int(nbytes), transcendentals=0)


def dot_nt(a, b):
    return lax.dot_general(a, b, (((1,), (1,)), ((), ())), preferred_element_type=F32)


def dot_nn(a, b):
    return lax.dot_general(a, b, (((1,), (0,)), ((), ())), preferred_element_type=F32)


def row_col(rows, cols):
    return lax.broadcasted_iota(jnp.int32, (rows, cols), 0), lax.broadcasted_iota(jnp.int32, (rows, cols), 1)


def lesser_kernel(sel, g_ref, gamma_ref, *outs):
    n = g_ref.shape[-1]
    half = n // 2
    e = pl.program_id(0)
    gamma = gamma_ref[0, pl.ds(e, 1), :]
    g_re, g_im = g_ref[0, 0, 0], g_ref[0, 0, 1]
    s_re = (g_re.astype(F32) * gamma).astype(BF16)
    s_im = (g_im.astype(F32) * gamma).astype(BF16)
    row, col = row_col(half, half)

    def real(i, j):
        i, j = slice(i * half, (i + 1) * half), slice(j * half, (j + 1) * half)
        return dot_nt(s_re[i], g_re[j]) + dot_nt(s_im[i], g_im[j])

    def imag(i, j):
        i, j = slice(i * half, (i + 1) * half), slice(j * half, (j + 1) * half)
        return dot_nt(s_im[i], g_re[j]) - dot_nt(s_re[i], g_im[j])

    for d in range(2):
        outs[d][0, :, d * half:(d + 1) * half] = jnp.where(col >= row, real(d, d), imag(d, d)).astype(BF16)
    outs[0][0, :, half:] = real(0, 1).astype(BF16)
    outs[1][0, :, :half] = imag(1, 0).astype(BF16)


def lesser_packed(which, green, broadening):
    _, le, _, n, _ = green.shape
    return pl.pallas_call(
        lesser_kernel,
        out_shape=[jax.ShapeDtypeStruct((le, n // 2, n), BF16)] * 2,
        grid_spec=pltpu.PrefetchScalarGridSpec(
            num_scalar_prefetch=1,
            grid=(le,),
            in_specs=[
                pl.BlockSpec((1, 1, 2, n, n), lambda e, sel: (sel[0], e, 0, 0, 0)),
                pl.BlockSpec((1, le, n), lambda e, sel: (sel[0], 0, 0)),
            ],
            out_specs=[pl.BlockSpec((1, n // 2, n), lambda e, sel: (e, 0, 0))] * 2,
        ),
        compiler_params=params(56),
        cost_estimate=cost(le * 6 * n**3, le * n * n * 6),
        name="lesser",
    )(which[None], green, broadening)


def place_kernel(where, c_ref, *refs):
    full_ref, turned_ref = refs[-2:]
    full_ref[...] = c_ref[...]
    for q in range(c_ref.shape[0]):
        turned_ref[q] = c_ref[q].T


def place_coupling(where, piece, held):
    nk, rows, n = piece.shape
    each = 4
    alias = [] if held is None else list(held)
    return pl.pallas_call(
        place_kernel,
        out_shape=[jax.ShapeDtypeStruct((nk, n, n), BF16)] * 2,
        grid_spec=pltpu.PrefetchScalarGridSpec(
            num_scalar_prefetch=1,
            grid=(nk // each,),
            in_specs=[pl.BlockSpec((each, rows, n), lambda q, w: (q, 0, 0))]
            + [pl.BlockSpec(memory_space=pl.ANY)] * len(alias),
            out_specs=[
                pl.BlockSpec((each, rows, n), lambda q, w: (q, w[0], 0)),
                pl.BlockSpec((each, n, rows), lambda q, w: (q, 0, w[0])),
            ],
        ),
        input_output_aliases={2: 0, 3: 1} if alias else {},
        compiler_params=params(56),
        cost_estimate=cost(nk * rows * n * 4, nk * rows * n * 6),
        name="place",
    )(where[None], piece, *alias)


def source_kernel(odd, w_ref, keep, recv, kz, rz, *refs):
    le = keep.shape[0]
    outs = refs[-2 * le:]

    def emit(order):
        line = [(ref, e) for ref in order for e in range(le)]
        for e in range(le):
            for ref, target in ((keep, outs[e]), (recv, outs[le + e])):
                at = [i for i, held in enumerate(order) if held is ref][0] * le + e
                total = None
                for s in range(1, SHIFT_MAX + 1):
                    for j, sign in ((0, s), (1, -s)):
                        source, index = line[at + sign]
                        term = w_ref[2 * (s - 1) + j] * source[index].astype(F32)
                        total = term if total is None else total + term
                target[0] = total.astype(BF16)

    @pl.when(odd[0] == 0)
    def _():
        emit((rz, keep, recv, kz))

    @pl.when(odd[0] == 1)
    def _():
        emit((kz, recv, keep, rz))


def sources(odd, weights, j, h, hk, keep, recv, kz, rz, held):
    le, half, n = keep.shape
    rows = half // 2
    at = h * (half // rows)
    big = pl.BlockSpec((le, rows, n), lambda r, *_: (0, r, 0))
    first = pl.BlockSpec((1, rows, n), lambda r, *_: (0, at + r, 0))
    later = pl.BlockSpec((1, rows, n), lambda r, *_: (j, at + r, 0))
    shapes = [(1 if e == 0 else hk, n, n) for e in range(le)] * 2
    specs = [first if e == 0 else later for e in range(le)] * 2
    alias, extra = {}, []
    if held is not None:
        for i, value in enumerate(held):
            if i % le or h:
                alias[6 + len(extra)] = i
                extra.append(value)
    return pl.pallas_call(
        source_kernel,
        out_shape=[jax.ShapeDtypeStruct(shape, BF16) for shape in shapes],
        grid_spec=pltpu.PrefetchScalarGridSpec(
            num_scalar_prefetch=2,
            grid=(half // rows,),
            in_specs=[big] * 4 + [pl.BlockSpec(memory_space=pl.ANY)] * len(extra),
            out_specs=specs,
        ),
        input_output_aliases=alias,
        compiler_params=params(56),
        cost_estimate=cost(le * half * n * 16, le * half * n * 12),
        name="source",
    )(odd[None], weights, keep, recv, kz, rz, *extra)


def home_kernel(lk, pieces, slots, *refs):
    ins, (c_ref, ct_ref, x_ref, y_ref, q_ref) = refs[:pieces], refs[pieces:]
    each, rows, n = ins[0].shape
    count = pieces * each
    for s in range(pieces):
        for j in range(each):
            q_ref[s * each + j] = ins[s][j]
    tr, tc = 16, 256

    def tile(index, _):
        r = pl.ds(pl.multiple_of((index // (n // tc)) * tr, tr), tr)
        m = pl.ds(pl.multiple_of((index % (n // tc)) * tc, tc), tc)
        xs, ys = [None] * lk, [None] * lk
        for q in range(0, count, 4):
            px, py = [None] * lk, [None] * lk
            for p in (q, q + 2):
                c, ct = [c_ref[p + i, r, m] for i in range(2)], [ct_ref[p + i, r, m] for i in range(2)]
                for k in range(lk):
                    v = [q_ref[slots[k * count + p + i], r, m] for i in range(2)]
                    x, y = c[0] * v[0] + c[1] * v[1], ct[0] * v[0] + ct[1] * v[1]
                    px[k] = x if p == q else px[k] + x
                    py[k] = y if p == q else py[k] + y
            for k in range(lk):
                xs[k] = px[k] if q == 0 else xs[k] + px[k]
                ys[k] = py[k] if q == 0 else ys[k] + py[k]
        for k in range(lk):
            x_ref[k, r, m] = xs[k]
            y_ref[k, r, m] = ys[k]
        return 0

    lax.fori_loop(0, (rows // tr) * (n // tc), tile, 0)


def home_blocks(slots, pieces, full, turned, lk):
    each, n, _ = pieces[0].shape
    count = each * len(pieces)
    rows = n // 8
    block = lambda lead: pl.BlockSpec((lead, rows, n), lambda g, s: (0, g, 0))
    return pl.pallas_call(
        functools.partial(home_kernel, lk, len(pieces)),
        out_shape=[jax.ShapeDtypeStruct((lk, n, n), BF16)] * 2,
        grid_spec=pltpu.PrefetchScalarGridSpec(
            num_scalar_prefetch=1,
            grid=(n // rows,),
            in_specs=[block(each)] * len(pieces) + [block(count), block(count)],
            out_specs=[block(lk), block(lk)],
            scratch_shapes=[pltpu.VMEM((count, rows, n), BF16)],
        ),
        compiler_params=params(56),
        cost_estimate=cost(4 * lk * count * n * n, n * n * (6 * count + 4 * lk)),
        name="home",
    )(slots, *pieces, full, turned)


def rows_kernel(pieces, mine, slots, *refs):
    a_refs, b_refs, refs = refs[:pieces], refs[pieces:2 * pieces], refs[2 * pieces:]
    c_ref, out_ref, re_ref, im_ref = (refs[0],) + refs[-3:]
    each, rows, cols = a_refs[0].shape
    count = pieces * each
    row, col = row_col(rows, cols)
    above = (col - row) + (pl.program_id(0) * cols - mine[0] * rows)
    for s in range(pieces):
        for j in range(each):
            a, b = a_refs[s][j].astype(F32), b_refs[s][j].astype(F32).T
            re_ref[s * each + j] = jnp.where(above >= 0, a, b).astype(BF16)
            im_ref[s * each + j] = jnp.where(above < 0, a, jnp.where(above > 0, -b, 0.0)).astype(BF16)
    tr, kg, tc = 16, 4, 256
    wide = cols // tc

    def tile(index, _):
        r = pl.ds(pl.multiple_of(((index // wide) % (rows // tr)) * tr, tr), tr)
        m = pl.ds(pl.multiple_of((index % wide) * tc, tc), tc)
        k0 = (index // (wide * (rows // tr))) * kg
        us, vs = [None] * kg, [None] * kg
        for q in range(0, count, 4):
            pu, pv = [None] * kg, [None] * kg
            for p in (q, q + 2):
                c = [c_ref[p + i, r, m] for i in range(2)]
                for k in range(kg):
                    slot = [slots[(k0 + k) * count + p + i] for i in range(2)]
                    u = c[0] * re_ref[slot[0], r, m] + c[1] * re_ref[slot[1], r, m]
                    v = c[0] * im_ref[slot[0], r, m] + c[1] * im_ref[slot[1], r, m]
                    pu[k] = u if p == q else pu[k] + u
                    pv[k] = v if p == q else pv[k] + v
            for k in range(kg):
                us[k] = pu[k] if q == 0 else us[k] + pu[k]
                vs[k] = pv[k] if q == 0 else vs[k] + pv[k]
        for k in range(kg):
            out_ref[k0 + k, 0, 0, r, m] = us[k]
            out_ref[k0 + k, 0, 1, r, m] = vs[k]
        return 0

    lax.fori_loop(0, wide * (rows // tr) * (count // kg), tile, 0)


def own_rows(mine, slots, pieces, coupling, energy, le, held):
    each, n, _ = pieces[0].shape
    count, rows, _ = coupling.shape
    cols = n // 2
    alias = [] if held is None else [held]
    in_specs = (
        [pl.BlockSpec((each, rows, cols), lambda t, mine, slots: (0, mine[0], t))] * len(pieces)
        + [pl.BlockSpec((each, cols, rows), lambda t, mine, slots: (0, t, mine[0]))] * len(pieces)
        + [pl.BlockSpec((count, rows, cols), lambda t, mine, slots: (0, 0, t))]
        + [pl.BlockSpec(memory_space=pl.ANY)] * len(alias)
    )
    return pl.pallas_call(
        functools.partial(rows_kernel, len(pieces)),
        out_shape=jax.ShapeDtypeStruct((count, le, 2, rows, n), BF16),
        grid_spec=pltpu.PrefetchScalarGridSpec(
            num_scalar_prefetch=2,
            grid=(n // cols,),
            in_specs=in_specs,
            out_specs=pl.BlockSpec((count, 1, 2, rows, cols), lambda t, mine, slots: (0, energy, 0, 0, t)),
            scratch_shapes=[pltpu.VMEM((count, rows, cols), BF16)] * 2,
        ),
        input_output_aliases={2 + len(in_specs) - 1: 0} if alias else {},
        compiler_params=params(56),
        cost_estimate=cost(4 * count * count * rows * n, rows * n * count * 10),
        name="rows",
    )(mine[None], slots, *pieces, *pieces, coupling, *alias)


def density_terms(energy, g_ref, gamma_ref, x_ref, y_ref):
    n = g_ref.shape[-1]
    gamma = gamma_ref[0, energy:energy + 1, :]
    g_re, g_im = g_ref[0, 0, 0], g_ref[0, 0, 1]
    row, col = row_col(n, n)
    x, yt = x_ref[0].astype(F32), y_ref[0].astype(F32).T
    s_re = jnp.where(col >= row, x, yt).astype(BF16)
    s_im = jnp.where(col < row, x, jnp.where(col > row, -yt, 0.0)).astype(BF16)
    scaled_re = (g_re.astype(F32) * gamma).astype(BF16).astype(F32)
    scaled_im = (g_im.astype(F32) * gamma).astype(BF16).astype(F32)
    m_re = (dot_nn(g_re, s_re) - dot_nn(g_im, s_im) + scaled_re).astype(BF16)
    m_im = (dot_nn(g_re, s_im) + dot_nn(g_im, s_re) + scaled_im).astype(BF16)
    return dot_nt(m_re, g_re) + dot_nt(m_im, g_im), dot_nt(m_im, g_re) - dot_nt(m_re, g_im)


def first_density_kernel(energy, first, g_ref, gamma_ref, x_ref, y_ref, *refs):
    for c, d in enumerate(density_terms(energy, g_ref, gamma_ref, x_ref, y_ref)):
        refs[-1][0, c] = d if first else d + refs[0][0, c]


def first_density(energy, green, broadening, x, y, held):
    lk, le, _, n, _ = green.shape
    alias = [] if held is None else [held]
    pair = pl.BlockSpec((1, 2, n, n), lambda k: (k, 0, 0, 0))
    one = pl.BlockSpec((1, n, n), lambda k: (k, 0, 0))
    return pl.pallas_call(
        functools.partial(first_density_kernel, energy, held is None),
        out_shape=jax.ShapeDtypeStruct((lk, 2, n, n), F32),
        grid=(lk,),
        in_specs=[
            pl.BlockSpec((1, 1, 2, n, n), lambda k: (k, energy, 0, 0, 0)),
            pl.BlockSpec((1, le, n), lambda k: (k, 0, 0)),
            one,
            one,
        ] + [pair] * len(alias),
        out_specs=pair,
        compiler_params=params(56),
        cost_estimate=cost(16 * lk * n**3, lk * n * n * 20),
        name="density",
    )(green, broadening, x, y, *alias)


def last_density_kernel(scale, energy, odd, g_ref, gamma_ref, x_ref, y_ref, held_ref, keep_ref, send_ref, d_ref):
    groups, _, rows, _ = keep_ref.shape
    for c, d in enumerate(density_terms(energy, g_ref, gamma_ref, x_ref, y_ref)):
        d_ref[c] = (d + held_ref[0, c]) * scale
        for g in range(groups):
            mine = pl.multiple_of((2 * g + odd[0]) * rows, rows)
            other = pl.multiple_of((2 * g + 1 - odd[0]) * rows, rows)
            keep_ref[g, c] = d_ref[c, pl.ds(mine, rows), :].astype(BF16)
            send_ref[g, c] = d_ref[c, pl.ds(other, rows), :].astype(BF16)


def last_density(scale, energy, k, groups, odd, green, broadening, x, y, held):
    _, le, _, n, _ = green.shape
    rows = n // (2 * groups)
    one = pl.BlockSpec((1, n, n), lambda i, odd: (k, 0, 0))
    out = pl.BlockSpec((groups, 2, rows, n), lambda i, odd: (0, 0, 0, 0))
    return pl.pallas_call(
        functools.partial(last_density_kernel, scale, energy),
        out_shape=[jax.ShapeDtypeStruct((groups, 2, rows, n), BF16)] * 2,
        grid_spec=pltpu.PrefetchScalarGridSpec(
            num_scalar_prefetch=1,
            grid=(1,),
            in_specs=[
                pl.BlockSpec((1, 1, 2, n, n), lambda i, odd: (k, energy, 0, 0, 0)),
                pl.BlockSpec((1, le, n), lambda i, odd: (k, 0, 0)),
                one,
                one,
                pl.BlockSpec((1, 2, n, n), lambda i, odd: (k, 0, 0, 0)),
            ],
            out_specs=[out, out],
            scratch_shapes=[pltpu.VMEM((2, n, n), F32)],
        ),
        compiler_params=params(56),
        cost_estimate=cost(16 * n**3, n * n * 20),
        name="density",
    )(odd[None], green, broadening, x, y, held)


def pair_sum_kernel(group, keep_ref, recv_ref, *outs):
    groups = len(outs)
    for d in range(groups):
        at = lax.rem(group[0] + d, groups)
        outs[d][...] = (keep_ref[at].astype(F32) + recv_ref[at].astype(F32)).astype(BF16)


def pair_sum(group, keep, recv):
    groups = keep.shape[0]
    vmem = pl.BlockSpec(memory_space=pltpu.VMEM)
    return pl.pallas_call(
        pair_sum_kernel,
        out_shape=[jax.ShapeDtypeStruct(keep.shape[1:], BF16)] * groups,
        in_specs=[pl.BlockSpec(memory_space=pltpu.SMEM), vmem, vmem],
        out_specs=[vmem] * groups,
        compiler_params=params(56),
        cost_estimate=cost(keep.size, keep.size * 6),
        name="pairsum",
    )(group[None], keep, recv)


def staged(green_ret, broadening, coupling, shift_steps, mode_weight, occupation, momentum_map):
    lk, le, _, _, _ = green_ret.shape
    ne, nm = lax.axis_size("energy"), lax.axis_size("mom")
    if le != SHIFT_MAX or lk % 2 or ne % 2 or nm & (nm - 1):
        raise ValueError("unsupported sizes")
    hk, groups = lk // 2, ne // 2
    me, mine = lax.axis_index("energy").astype(jnp.int32), lax.axis_index("mom").astype(jnp.int32)
    odd, group = me & 1, me >> 1
    pairs = [(i, i ^ 1) for i in range(ne)]
    away = [(i, i + (2 if i % 2 else -2)) for i in range(ne) if 0 <= i + (2 if i % 2 else -2) < ne]
    across = [(i, i + (-2 if i % 2 else 2)) for i in range(ne) if 0 <= i + (-2 if i % 2 else 2) < ne]
    strides = []
    while (nm >> (len(strides) + 1)) > 0:
        strides.append(nm >> (len(strides) + 1))

    def over_energy(x, perm):
        return lax.ppermute(x, "energy", perm)

    def swap(x, stride):
        return lax.ppermute(x, "mom", [(i, i ^ stride) for i in range(nm)])

    def spread(x):
        held = [x]
        for s in strides:
            held = held + [swap(piece, s) for piece in held]
        return held

    order = [0]
    for s in strides:
        order = order + [o ^ s for o in order]

    weights = []
    for s in range(1, SHIFT_MAX + 1):
        held = shift_steps == s
        weights.append(jnp.sum(jnp.where(held, mode_weight * (occupation + 1.0), 0.0)))
        weights.append(jnp.sum(jnp.where(held, mode_weight * occupation, 0.0)))
    weights = jnp.stack(weights)

    owner, inner = momentum_map // lk, momentum_map % lk
    place = jnp.zeros_like(owner)
    for at, o in enumerate(order):
        place = jnp.where((owner ^ mine) == o, at, place)
    slots = (place * lk + ((inner // hk) ^ odd) * hk + inner % hk).astype(jnp.int32)
    own_slots = lax.dynamic_slice_in_dim(slots, mine * lk, lk, 0).reshape(-1)
    all_slots = slots.reshape(-1)

    coupling_pieces = spread(coupling)

    send = [lesser_packed((1 - odd) * hk + j, green_ret, broadening) for j in range(hk)]
    recv = [[over_energy(send[j][h], pairs) for h in range(2)] for j in range(hk)]
    keep = [lesser_packed(odd * hk + j, green_ret, broadening) for j in range(hk)]
    kz = [[over_energy(keep[j][h], away) for h in range(2)] for j in range(hk)]
    rz = [[over_energy(recv[j][h], across) for h in range(2)] for j in range(hk)]
    got, last = [], None
    for j in range(hk):
        for h in range(2):
            last = sources(
                odd, weights, j, h, hk, keep[j][h], recv[j][h], kz[j][h], rz[j][h], last)
        got.append(last)

    placed = None
    for at in sorted(range(nm), key=lambda a: (a & 1, a)):
        placed = place_coupling(mine ^ order[at], coupling_pieces[at], placed)
    full, turned = placed

    held_rows, held_density = None, None
    scale = 1.0 / (le * ne)
    late = []
    for e in range(le):
        use = [got[j] for j in range(hk)] if e == 0 else [last]
        fresh = [spread(part[e]) for part in use]
        back = [spread(over_energy(part[le + e], pairs)) for part in use]
        pieces = [part[at] for at in range(nm) for part in fresh + back]
        x, y = home_blocks(own_slots, pieces, full, turned, lk)
        if e < le - 1:
            held_density = first_density(e, green_ret, broadening, x, y, held_density)
        else:
            for k in range(lk):
                kept, sent = last_density(
                    scale, e, k, groups, odd, green_ret, broadening, x, y, held_density)
                other = over_energy(sent, pairs)
                parts = pair_sum(group, kept, other)
                total = parts[0].astype(F32)
                for d in range(1, groups):
                    perm = [(i, (i + 2 * d) % ne) for i in range(ne)]
                    total = total + over_energy(parts[d], perm).astype(F32)
                late.append(total)
        held_rows = own_rows(mine, all_slots, pieces, coupling, e, le, held_rows)
    density = jnp.transpose(jnp.stack(late), (2, 0, 1, 3))
    return held_rows, density


def solution(mesh):
    return jax.shard_map(
        staged,
        mesh=mesh,
        in_specs=(
            P("mom", "energy", None, None, None),
            P("mom", "energy", None),
            P(None, "mom", None),
            P(),
            P(),
            P(),
            P(),
        ),
        out_specs=(P(None, "energy", None, "mom", None), P("energy", "mom", None, None)),
        check_vma=False,
    )
```

```python
import functools

import jax
import jax.numpy as jnp
from jax import lax
from jax.experimental import pallas as pl
from jax.experimental.pallas import tpu as pltpu
from jax.sharding import PartitionSpec as P


SHIFT_MAX = 2
F32 = jnp.float32
BF16 = jnp.bfloat16


def params(mib):
    return pltpu.CompilerParams(vmem_limit_bytes=mib * 1024 * 1024)


def cost(flops, nbytes):
    return pl.CostEstimate(flops=int(flops), bytes_accessed=int(nbytes), transcendentals=0)


def dot_nt(a, b):
    return lax.dot_general(a, b, (((1,), (1,)), ((), ())), preferred_element_type=F32)


def dot_nn(a, b):
    return lax.dot_general(a, b, (((1,), (0,)), ((), ())), preferred_element_type=F32)


def row_col(rows, cols):
    return lax.broadcasted_iota(jnp.int32, (rows, cols), 0), lax.broadcasted_iota(jnp.int32, (rows, cols), 1)


def lesser_kernel(sel, g_ref, gamma_ref, *outs):
    n = g_ref.shape[-1]
    half = n // 2
    e = pl.program_id(0)
    gamma = gamma_ref[0, pl.ds(e, 1), :]
    g_re, g_im = g_ref[0, 0, 0], g_ref[0, 0, 1]
    s_re = (g_re.astype(F32) * gamma).astype(BF16)
    s_im = (g_im.astype(F32) * gamma).astype(BF16)
    row, col = row_col(half, half)

    def real(i, j):
        i, j = slice(i * half, (i + 1) * half), slice(j * half, (j + 1) * half)
        return dot_nt(s_re[i], g_re[j]) + dot_nt(s_im[i], g_im[j])

    def imag(i, j):
        i, j = slice(i * half, (i + 1) * half), slice(j * half, (j + 1) * half)
        return dot_nt(s_im[i], g_re[j]) - dot_nt(s_re[i], g_im[j])

    for d in range(2):
        outs[d][0, :, d * half:(d + 1) * half] = jnp.where(col >= row, real(d, d), imag(d, d)).astype(BF16)
    outs[0][0, :, half:] = real(0, 1).astype(BF16)
    outs[1][0, :, :half] = imag(1, 0).astype(BF16)


def lesser_packed(which, green, broadening):
    _, le, _, n, _ = green.shape
    return pl.pallas_call(
        lesser_kernel,
        out_shape=[jax.ShapeDtypeStruct((le, n // 2, n), BF16)] * 2,
        grid_spec=pltpu.PrefetchScalarGridSpec(
            num_scalar_prefetch=1,
            grid=(le,),
            in_specs=[
                pl.BlockSpec((1, 1, 2, n, n), lambda e, sel: (sel[0], e, 0, 0, 0)),
                pl.BlockSpec((1, le, n), lambda e, sel: (sel[0], 0, 0)),
            ],
            out_specs=[pl.BlockSpec((1, n // 2, n), lambda e, sel: (e, 0, 0))] * 2,
        ),
        compiler_params=params(40),
        cost_estimate=cost(le * 6 * n**3, le * n * n * 6),
        name="lesser",
    )(which[None], green, broadening)


def place_kernel(where, *refs):
    pieces, (full_ref, turned_ref) = refs[:-2], refs[-2:]
    rows = pieces[0].shape[1]
    for at, c_ref in enumerate(pieces):
        start = pl.ds(pl.multiple_of(where[at] * rows, rows), rows)
        for q in range(c_ref.shape[0]):
            full_ref[q, start, :] = c_ref[q]
            turned_ref[q, :, start] = c_ref[q].T


def place_coupling(where, pieces):
    nk, rows, n = pieces[0].shape
    each = 2
    return pl.pallas_call(
        place_kernel,
        out_shape=[pltpu.VMEM((nk, n, n), BF16)] * 2,
        grid_spec=pltpu.PrefetchScalarGridSpec(
            num_scalar_prefetch=1,
            grid=(nk // each,),
            in_specs=[pl.BlockSpec((each, rows, n), lambda q, w: (q, 0, 0))] * len(pieces),
            out_specs=[pl.BlockSpec((each, n, n), lambda q, w: (q, 0, 0))] * 2,
        ),
        compiler_params=params(40),
        cost_estimate=cost(nk * n * n * 4, nk * n * n * 6),
        name="place",
    )(where, *pieces)


def source_kernel(odd, w_ref, keep, recv, kz, rz, *refs):
    le = keep.shape[0]
    outs = refs[-2 * le:]

    def emit(order):
        line = [(ref, e) for ref in order for e in range(le)]
        for e in range(le):
            for ref, target in ((keep, outs[e]), (recv, outs[le + e])):
                at = [i for i, held in enumerate(order) if held is ref][0] * le + e
                total = None
                for s in range(1, SHIFT_MAX + 1):
                    for j, sign in ((0, s), (1, -s)):
                        source, index = line[at + sign]
                        term = w_ref[2 * (s - 1) + j] * source[index].astype(F32)
                        total = term if total is None else total + term
                target[0] = total.astype(BF16)

    @pl.when(odd[0] == 0)
    def _():
        emit((rz, keep, recv, kz))

    @pl.when(odd[0] == 1)
    def _():
        emit((kz, recv, keep, rz))


def sources(odd, weights, j, h, hk, keep, recv, kz, rz, held):
    le, half, n = keep.shape
    rows = half // 2
    at = h * (half // rows)
    big = pl.BlockSpec((le, rows, n), lambda r, *_: (0, r, 0))
    first = pl.BlockSpec((1, rows, n), lambda r, *_: (0, at + r, 0))
    later = pl.BlockSpec((1, rows, n), lambda r, *_: (j, at + r, 0))
    shapes = [(1 if e == 0 else hk, n, n) for e in range(le)] * 2
    specs = [first if e == 0 else later for e in range(le)] * 2
    alias, extra = {}, []
    if held is not None:
        for i, value in enumerate(held):
            if i % le or h:
                alias[6 + len(extra)] = i
                extra.append(value)
    return pl.pallas_call(
        source_kernel,
        out_shape=[jax.ShapeDtypeStruct(shape, BF16) for shape in shapes],
        grid_spec=pltpu.PrefetchScalarGridSpec(
            num_scalar_prefetch=2,
            grid=(half // rows,),
            in_specs=[big] * 4 + [pl.BlockSpec(memory_space=pl.ANY)] * len(extra),
            out_specs=specs,
        ),
        input_output_aliases=alias,
        compiler_params=params(40),
        cost_estimate=cost(le * half * n * 16, le * half * n * 12),
        name="source",
    )(odd[None], weights, keep, recv, kz, rz, *extra)


def home_kernel(lk, pieces, slots, *refs):
    ins, (c_ref, ct_ref, x_ref, y_ref, q_ref) = refs[:pieces], refs[pieces:]
    each, rows, n = ins[0].shape
    count = pieces * each
    for s in range(pieces):
        for j in range(each):
            q_ref[s * each + j] = ins[s][j]
    tr, tc = 16, 256

    def tile(index, _):
        r = pl.ds(pl.multiple_of((index // (n // tc)) * tr, tr), tr)
        m = pl.ds(pl.multiple_of((index % (n // tc)) * tc, tc), tc)
        xs, ys = [None] * lk, [None] * lk
        for q in range(0, count, 4):
            px, py = [None] * lk, [None] * lk
            for p in (q, q + 2):
                c, ct = [c_ref[p + i, r, m] for i in range(2)], [ct_ref[p + i, r, m] for i in range(2)]
                for k in range(lk):
                    v = [q_ref[slots[k * count + p + i], r, m] for i in range(2)]
                    x, y = c[0] * v[0] + c[1] * v[1], ct[0] * v[0] + ct[1] * v[1]
                    px[k] = x if p == q else px[k] + x
                    py[k] = y if p == q else py[k] + y
            for k in range(lk):
                xs[k] = px[k] if q == 0 else xs[k] + px[k]
                ys[k] = py[k] if q == 0 else ys[k] + py[k]
        for k in range(lk):
            x_ref[k, r, m] = xs[k]
            y_ref[k, r, m] = ys[k]
        return 0

    lax.fori_loop(0, (rows // tr) * (n // tc), tile, 0)


def home_blocks(slots, pieces, full, turned, lk):
    each, n, _ = pieces[0].shape
    count = each * len(pieces)
    rows = n // 8
    block = lambda lead: pl.BlockSpec((lead, rows, n), lambda g, s: (0, g, 0))
    return pl.pallas_call(
        functools.partial(home_kernel, lk, len(pieces)),
        out_shape=[jax.ShapeDtypeStruct((lk, n, n), BF16)] * 2,
        grid_spec=pltpu.PrefetchScalarGridSpec(
            num_scalar_prefetch=1,
            grid=(n // rows,),
            in_specs=[block(each)] * len(pieces) + [block(count), block(count)],
            out_specs=[block(lk), block(lk)],
            scratch_shapes=[pltpu.VMEM((count, rows, n), BF16)],
        ),
        compiler_params=params(40),
        cost_estimate=cost(4 * lk * count * n * n, n * n * (6 * count + 4 * lk)),
        name="home",
    )(slots, *pieces, full, turned)


def rows_kernel(pieces, mine, slots, *refs):
    a_refs, b_refs, refs = refs[:pieces], refs[pieces:2 * pieces], refs[2 * pieces:]
    c_ref, out_ref, re_ref, im_ref = (refs[0],) + refs[-3:]
    each, rows, cols = a_refs[0].shape
    count = pieces * each
    row, col = row_col(rows, cols)
    above = (col - row) + (pl.program_id(0) * cols - mine[0] * rows)
    for s in range(pieces):
        for j in range(each):
            a, b = a_refs[s][j].astype(F32), b_refs[s][j].astype(F32).T
            re_ref[s * each + j] = jnp.where(above >= 0, a, b).astype(BF16)
            im_ref[s * each + j] = jnp.where(above < 0, a, jnp.where(above > 0, -b, 0.0)).astype(BF16)
    tr, kg, tc = 16, 4, 256
    wide = cols // tc

    def tile(index, _):
        r = pl.ds(pl.multiple_of(((index // wide) % (rows // tr)) * tr, tr), tr)
        m = pl.ds(pl.multiple_of((index % wide) * tc, tc), tc)
        k0 = (index // (wide * (rows // tr))) * kg
        us, vs = [None] * kg, [None] * kg
        for q in range(0, count, 4):
            pu, pv = [None] * kg, [None] * kg
            for p in (q, q + 2):
                c = [c_ref[p + i, r, m] for i in range(2)]
                for k in range(kg):
                    slot = [slots[(k0 + k) * count + p + i] for i in range(2)]
                    u = c[0] * re_ref[slot[0], r, m] + c[1] * re_ref[slot[1], r, m]
                    v = c[0] * im_ref[slot[0], r, m] + c[1] * im_ref[slot[1], r, m]
                    pu[k] = u if p == q else pu[k] + u
                    pv[k] = v if p == q else pv[k] + v
            for k in range(kg):
                us[k] = pu[k] if q == 0 else us[k] + pu[k]
                vs[k] = pv[k] if q == 0 else vs[k] + pv[k]
        for k in range(kg):
            out_ref[k0 + k, 0, 0, r, m] = us[k]
            out_ref[k0 + k, 0, 1, r, m] = vs[k]
        return 0

    lax.fori_loop(0, wide * (rows // tr) * (count // kg), tile, 0)


def own_rows(mine, slots, pieces, coupling, energy, le, held):
    each, n, _ = pieces[0].shape
    count, rows, _ = coupling.shape
    cols = n // 2
    alias = [] if held is None else [held]
    in_specs = (
        [pl.BlockSpec((each, rows, cols), lambda t, mine, slots: (0, mine[0], t))] * len(pieces)
        + [pl.BlockSpec((each, cols, rows), lambda t, mine, slots: (0, t, mine[0]))] * len(pieces)
        + [pl.BlockSpec((count, rows, cols), lambda t, mine, slots: (0, 0, t))]
        + [pl.BlockSpec(memory_space=pl.ANY)] * len(alias)
    )
    return pl.pallas_call(
        functools.partial(rows_kernel, len(pieces)),
        out_shape=jax.ShapeDtypeStruct((count, le, 2, rows, n), BF16),
        grid_spec=pltpu.PrefetchScalarGridSpec(
            num_scalar_prefetch=2,
            grid=(n // cols,),
            in_specs=in_specs,
            out_specs=pl.BlockSpec((count, 1, 2, rows, cols), lambda t, mine, slots: (0, energy, 0, 0, t)),
            scratch_shapes=[pltpu.VMEM((count, rows, cols), BF16)] * 2,
        ),
        input_output_aliases={2 + len(in_specs) - 1: 0} if alias else {},
        compiler_params=params(40),
        cost_estimate=cost(4 * count * count * rows * n, rows * n * count * 10),
        name="rows",
    )(mine[None], slots, *pieces, *pieces, coupling, *alias)


def density_terms(energy, g_ref, gamma_ref, x_ref, y_ref):
    n = g_ref.shape[-1]
    gamma = gamma_ref[0, energy:energy + 1, :]
    g_re, g_im = g_ref[0, 0, 0], g_ref[0, 0, 1]
    row, col = row_col(n, n)
    x, yt = x_ref[0].astype(F32), y_ref[0].astype(F32).T
    s_re = jnp.where(col >= row, x, yt).astype(BF16)
    s_im = jnp.where(col < row, x, jnp.where(col > row, -yt, 0.0)).astype(BF16)
    scaled_re = (g_re.astype(F32) * gamma).astype(BF16).astype(F32)
    scaled_im = (g_im.astype(F32) * gamma).astype(BF16).astype(F32)
    m_re = (dot_nn(g_re, s_re) - dot_nn(g_im, s_im) + scaled_re).astype(BF16)
    m_im = (dot_nn(g_re, s_im) + dot_nn(g_im, s_re) + scaled_im).astype(BF16)
    return dot_nt(m_re, g_re) + dot_nt(m_im, g_im), dot_nt(m_im, g_re) - dot_nt(m_re, g_im)


def first_density_kernel(energy, first, g_ref, gamma_ref, x_ref, y_ref, *refs):
    for c, d in enumerate(density_terms(energy, g_ref, gamma_ref, x_ref, y_ref)):
        refs[-1][0, c] = d if first else d + refs[0][0, c]


def first_density(energy, green, broadening, x, y, held):
    lk, le, _, n, _ = green.shape
    alias = [] if held is None else [held]
    pair = pl.BlockSpec((1, 2, n, n), lambda k: (k, 0, 0, 0))
    one = pl.BlockSpec((1, n, n), lambda k: (k, 0, 0))
    return pl.pallas_call(
        functools.partial(first_density_kernel, energy, held is None),
        out_shape=jax.ShapeDtypeStruct((lk, 2, n, n), F32),
        grid=(lk,),
        in_specs=[
            pl.BlockSpec((1, 1, 2, n, n), lambda k: (k, energy, 0, 0, 0)),
            pl.BlockSpec((1, le, n), lambda k: (k, 0, 0)),
            one,
            one,
        ] + [pair] * len(alias),
        out_specs=pair,
        compiler_params=params(40),
        cost_estimate=cost(16 * lk * n**3, lk * n * n * 20),
        name="density",
    )(green, broadening, x, y, *alias)


def last_density_kernel(scale, energy, odd, g_ref, gamma_ref, x_ref, y_ref, held_ref, *refs):
    d_ref, outs = refs[-1], refs[:-1]
    groups, _, rows, _ = outs[0].shape
    for c, d in enumerate(density_terms(energy, g_ref, gamma_ref, x_ref, y_ref)):
        d_ref[c] = (d + held_ref[0, c]) * scale
    for i in range(len(outs) // 2):
        keep_ref, send_ref = outs[2 * i], outs[2 * i + 1]

        @pl.when(pl.program_id(0) == i)
        def _():
            for c in range(2):
                for g in range(groups):
                    mine = pl.multiple_of((2 * g + odd[0]) * rows, rows)
                    other = pl.multiple_of((2 * g + 1 - odd[0]) * rows, rows)
                    keep_ref[g, c] = d_ref[c, pl.ds(mine, rows), :].astype(BF16)
                    send_ref[g, c] = d_ref[c, pl.ds(other, rows), :].astype(BF16)


def last_density(scale, energy, start, stop, groups, odd, green, broadening, x, y, held):
    _, le, _, n, _ = green.shape
    rows = n // (2 * groups)
    count = stop - start
    one = pl.BlockSpec((1, n, n), lambda i, odd: (start + i, 0, 0))
    out = pl.BlockSpec((groups, 2, rows, n), lambda i, odd: (0, 0, 0, 0))
    return pl.pallas_call(
        functools.partial(last_density_kernel, scale, energy),
        out_shape=[jax.ShapeDtypeStruct((groups, 2, rows, n), BF16)] * (2 * count),
        grid_spec=pltpu.PrefetchScalarGridSpec(
            num_scalar_prefetch=1,
            grid=(count,),
            in_specs=[
                pl.BlockSpec((1, 1, 2, n, n), lambda i, odd: (start + i, energy, 0, 0, 0)),
                pl.BlockSpec((1, le, n), lambda i, odd: (start + i, 0, 0)),
                one,
                one,
                pl.BlockSpec((1, 2, n, n), lambda i, odd: (start + i, 0, 0, 0)),
            ],
            out_specs=[out] * (2 * count),
            scratch_shapes=[pltpu.VMEM((2, n, n), F32)],
        ),
        compiler_params=params(40),
        cost_estimate=cost(count * 16 * n**3, count * n * n * 20),
        name="density",
    )(odd[None], green, broadening, x, y, held)


def pair_sum_kernel(group, keep_ref, recv_ref, *outs):
    groups = len(outs)
    for d in range(groups):
        at = lax.rem(group[0] + d, groups)
        outs[d][...] = (keep_ref[at].astype(F32) + recv_ref[at].astype(F32)).astype(BF16)


def pair_sum(group, keep, recv):
    groups = keep.shape[0]
    vmem = pl.BlockSpec(memory_space=pltpu.VMEM)
    return pl.pallas_call(
        pair_sum_kernel,
        out_shape=[jax.ShapeDtypeStruct(keep.shape[1:], BF16)] * groups,
        in_specs=[pl.BlockSpec(memory_space=pltpu.SMEM), vmem, vmem],
        out_specs=[vmem] * groups,
        compiler_params=params(40),
        cost_estimate=cost(keep.size, keep.size * 6),
        name="pairsum",
    )(group[None], keep, recv)


def staged(green_ret, broadening, coupling, shift_steps, mode_weight, occupation, momentum_map):
    lk, le, _, _, _ = green_ret.shape
    ne, nm = lax.axis_size("energy"), lax.axis_size("mom")
    if le != SHIFT_MAX or lk % 2 or ne % 2 or nm & (nm - 1):
        raise ValueError("unsupported sizes")
    hk, groups = lk // 2, ne // 2
    me, mine = lax.axis_index("energy").astype(jnp.int32), lax.axis_index("mom").astype(jnp.int32)
    odd, group = me & 1, me >> 1
    pairs = [(i, i ^ 1) for i in range(ne)]
    away = [(i, i + (2 if i % 2 else -2)) for i in range(ne) if 0 <= i + (2 if i % 2 else -2) < ne]
    across = [(i, i + (-2 if i % 2 else 2)) for i in range(ne) if 0 <= i + (-2 if i % 2 else 2) < ne]
    strides = []
    while (nm >> (len(strides) + 1)) > 0:
        strides.append(nm >> (len(strides) + 1))

    def over_energy(x, perm):
        return lax.ppermute(x, "energy", perm)

    def swap(x, stride):
        return lax.ppermute(x, "mom", [(i, i ^ stride) for i in range(nm)])

    def spread(x):
        held = [x]
        for s in strides:
            held = held + [swap(piece, s) for piece in held]
        return held

    order = [0]
    for s in strides:
        order = order + [o ^ s for o in order]

    weights = []
    for s in range(1, SHIFT_MAX + 1):
        held = shift_steps == s
        weights.append(jnp.sum(jnp.where(held, mode_weight * (occupation + 1.0), 0.0)))
        weights.append(jnp.sum(jnp.where(held, mode_weight * occupation, 0.0)))
    weights = jnp.stack(weights)

    owner, inner = momentum_map // lk, momentum_map % lk
    place = jnp.zeros_like(owner)
    for at, o in enumerate(order):
        place = jnp.where((owner ^ mine) == o, at, place)
    slots = (place * lk + ((inner // hk) ^ odd) * hk + inner % hk).astype(jnp.int32)
    own_slots = lax.dynamic_slice_in_dim(slots, mine * lk, lk, 0).reshape(-1)
    all_slots = slots.reshape(-1)

    green_ret = pltpu.with_memory_space_constraint(green_ret, pltpu.HBM)
    coupling_pieces = spread(coupling)

    send = [lesser_packed((1 - odd) * hk + j, green_ret, broadening) for j in range(hk)]
    recv = [[over_energy(send[j][h], pairs) for h in range(2)] for j in range(hk)]
    keep = [lesser_packed(odd * hk + j, green_ret, broadening) for j in range(hk)]
    kz = [[over_energy(keep[j][h], away) for h in range(2)] for j in range(hk)]
    rz = [[over_energy(recv[j][h], across) for h in range(2)] for j in range(hk)]
    got, last = [], None
    for j in range(hk):
        for h in range(2):
            last = sources(
                odd, weights, j, h, hk, keep[j][h], recv[j][h], kz[j][h], rz[j][h], last)
        got.append(last)

    full, turned = place_coupling(jnp.stack([mine ^ o for o in order]), coupling_pieces)

    held_rows, held_density = None, None
    scale = 1.0 / (le * ne)
    late = []
    for e in range(le):
        use = [got[j] for j in range(hk)] if e == 0 else [last]
        fresh = [spread(part[e]) for part in use]
        back = [spread(over_energy(part[le + e], pairs)) for part in use]
        pieces = [part[at] for at in range(nm) for part in fresh + back]
        x, y = home_blocks(own_slots, pieces, full, turned, lk)
        if e < le - 1:
            held_density = first_density(e, green_ret, broadening, x, y, held_density)
        else:
            shares = []
            for start, stop in ((0, 1), (1, lk)):
                shares = shares + list(last_density(
                    scale, e, start, stop, groups, odd,
                    green_ret, broadening, x, y, held_density))
            for k in range(lk):
                kept, sent = shares[2 * k], shares[2 * k + 1]
                other = over_energy(sent, pairs)
                parts = pair_sum(group, kept, other)
                total = parts[0].astype(F32)
                for d in range(1, groups):
                    perm = [(i, (i + 2 * d) % ne) for i in range(ne)]
                    total = total + over_energy(parts[d], perm).astype(F32)
                late.append(total)
        held_rows = own_rows(mine, all_slots, pieces, coupling, e, le, held_rows)
    density = jnp.transpose(jnp.stack(late), (2, 0, 1, 3))
    return held_rows, density


def solution(mesh):
    return jax.shard_map(
        staged,
        mesh=mesh,
        in_specs=(
            P("mom", "energy", None, None, None),
            P("mom", "energy", None),
            P(None, "mom", None),
            P(),
            P(),
            P(),
            P(),
        ),
        out_specs=(P(None, "energy", None, "mom", None), P("energy", "mom", None, None)),
        check_vma=False,
    )
```

```python
import functools

import jax
import jax.numpy as jnp
from jax import lax
from jax.experimental import pallas as pl
from jax.experimental.pallas import tpu as pltpu
from jax.sharding import PartitionSpec as P


SHIFT_MAX = 2
F32 = jnp.float32
BF16 = jnp.bfloat16


def params(mib):
    return pltpu.CompilerParams(vmem_limit_bytes=mib * 1024 * 1024)


def cost(flops, nbytes):
    return pl.CostEstimate(flops=int(flops), bytes_accessed=int(nbytes), transcendentals=0)


def dot_nt(a, b):
    return lax.dot_general(a, b, (((1,), (1,)), ((), ())), preferred_element_type=F32)


def dot_nn(a, b):
    return lax.dot_general(a, b, (((1,), (0,)), ((), ())), preferred_element_type=F32)


def row_col(rows, cols):
    return lax.broadcasted_iota(jnp.int32, (rows, cols), 0), lax.broadcasted_iota(jnp.int32, (rows, cols), 1)


def lesser_kernel(sel, g_ref, gamma_ref, *outs):
    n = g_ref.shape[-1]
    half = n // 2
    e = pl.program_id(0)
    gamma = gamma_ref[0, pl.ds(e, 1), :]
    g_re, g_im = g_ref[0, 0, 0], g_ref[0, 0, 1]
    s_re = (g_re.astype(F32) * gamma).astype(BF16)
    s_im = (g_im.astype(F32) * gamma).astype(BF16)
    row, col = row_col(half, half)

    def real(i, j):
        i, j = slice(i * half, (i + 1) * half), slice(j * half, (j + 1) * half)
        return dot_nt(s_re[i], g_re[j]) + dot_nt(s_im[i], g_im[j])

    def imag(i, j):
        i, j = slice(i * half, (i + 1) * half), slice(j * half, (j + 1) * half)
        return dot_nt(s_im[i], g_re[j]) - dot_nt(s_re[i], g_im[j])

    for d in range(2):
        outs[d][0, :, d * half:(d + 1) * half] = jnp.where(col >= row, real(d, d), imag(d, d)).astype(BF16)
    outs[0][0, :, half:] = real(0, 1).astype(BF16)
    outs[1][0, :, :half] = imag(1, 0).astype(BF16)


def lesser_packed(which, green, broadening):
    _, le, _, n, _ = green.shape
    return pl.pallas_call(
        lesser_kernel,
        out_shape=[jax.ShapeDtypeStruct((le, n // 2, n), BF16)] * 2,
        grid_spec=pltpu.PrefetchScalarGridSpec(
            num_scalar_prefetch=1,
            grid=(le,),
            in_specs=[
                pl.BlockSpec((1, 1, 2, n, n), lambda e, sel: (sel[0], e, 0, 0, 0)),
                pl.BlockSpec((1, le, n), lambda e, sel: (sel[0], 0, 0)),
            ],
            out_specs=[pl.BlockSpec((1, n // 2, n), lambda e, sel: (e, 0, 0))] * 2,
        ),
        compiler_params=params(56),
        cost_estimate=cost(le * 6 * n**3, le * n * n * 6),
        name="lesser",
    )(which[None], green, broadening)


def place_kernel(where, *refs):
    pieces, (full_ref, turned_ref) = refs[:-2], refs[-2:]
    rows = pieces[0].shape[1]
    for at, c_ref in enumerate(pieces):
        start = pl.ds(pl.multiple_of(where[at] * rows, rows), rows)
        for q in range(c_ref.shape[0]):
            full_ref[q, start, :] = c_ref[q]
            turned_ref[q, :, start] = c_ref[q].T


def place_coupling(where, pieces):
    nk, rows, n = pieces[0].shape
    each = 2
    return pl.pallas_call(
        place_kernel,
        out_shape=[pltpu.VMEM((nk, n, n), BF16)] * 2,
        grid_spec=pltpu.PrefetchScalarGridSpec(
            num_scalar_prefetch=1,
            grid=(nk // each,),
            in_specs=[pl.BlockSpec((each, rows, n), lambda q, w: (q, 0, 0))] * len(pieces),
            out_specs=[pl.BlockSpec((each, n, n), lambda q, w: (q, 0, 0))] * 2,
        ),
        compiler_params=params(42),
        cost_estimate=cost(nk * n * n * 4, nk * n * n * 6),
        name="place",
    )(where, *pieces)


def source_kernel(odd, w_ref, keep, recv, kz, rz, *refs):
    le = keep.shape[0]
    outs = refs[-2 * le:]

    def emit(order):
        line = [(ref, e) for ref in order for e in range(le)]
        for e in range(le):
            for ref, target in ((keep, outs[e]), (recv, outs[le + e])):
                at = [i for i, held in enumerate(order) if held is ref][0] * le + e
                total = None
                for s in range(1, SHIFT_MAX + 1):
                    for j, sign in ((0, s), (1, -s)):
                        source, index = line[at + sign]
                        term = w_ref[2 * (s - 1) + j] * source[index].astype(F32)
                        total = term if total is None else total + term
                target[0] = total.astype(BF16)

    @pl.when(odd[0] == 0)
    def _():
        emit((rz, keep, recv, kz))

    @pl.when(odd[0] == 1)
    def _():
        emit((kz, recv, keep, rz))


def sources(odd, weights, j, h, hk, keep, recv, kz, rz, held):
    le, half, n = keep.shape
    rows = half // 2
    at = h * (half // rows)
    big = pl.BlockSpec((le, rows, n), lambda r, *_: (0, r, 0))
    first = pl.BlockSpec((1, rows, n), lambda r, *_: (0, at + r, 0))
    later = pl.BlockSpec((1, rows, n), lambda r, *_: (j, at + r, 0))
    shapes = [(1 if e == 0 else hk, n, n) for e in range(le)] * 2
    specs = [first if e == 0 else later for e in range(le)] * 2
    alias, extra = {}, []
    if held is not None:
        for i, value in enumerate(held):
            if i % le or h:
                alias[6 + len(extra)] = i
                extra.append(value)
    return pl.pallas_call(
        source_kernel,
        out_shape=[jax.ShapeDtypeStruct(shape, BF16) for shape in shapes],
        grid_spec=pltpu.PrefetchScalarGridSpec(
            num_scalar_prefetch=2,
            grid=(half // rows,),
            in_specs=[big] * 4 + [pl.BlockSpec(memory_space=pl.ANY)] * len(extra),
            out_specs=specs,
        ),
        input_output_aliases=alias,
        compiler_params=params(56),
        cost_estimate=cost(le * half * n * 16, le * half * n * 12),
        name="source",
    )(odd[None], weights, keep, recv, kz, rz, *extra)


def home_kernel(lk, pieces, slots, *refs):
    ins, (c_ref, ct_ref, x_ref, y_ref, q_ref, sems) = refs[:pieces], refs[pieces:]
    each, n, _ = ins[0].shape
    _, count, rows, _ = q_ref.shape
    steps = n // rows
    tr, tc = 16, 256

    def fetch(g, slot):
        at = pl.ds(pl.multiple_of(g * rows, rows), rows)
        return [
            pltpu.make_async_copy(
                ins[s].at[j, at, :], q_ref.at[slot, s * each + j], sems.at[slot, s * each + j])
            for s in range(pieces) for j in range(each)
        ]

    for copy in fetch(0, 0):
        copy.start()

    def step(g, _):
        slot = lax.rem(g, 2)

        @pl.when(g + 1 < steps)
        def _():
            for copy in fetch(g + 1, 1 - slot):
                copy.start()

        for copy in fetch(g, slot):
            copy.wait()

        def tile(index, _):
            within = pl.multiple_of((index // (n // tc)) * tr, tr)
            r = pl.ds(within, tr)
            w = pl.ds(pl.multiple_of(g * rows + within, tr), tr)
            m = pl.ds(pl.multiple_of((index % (n // tc)) * tc, tc), tc)
            xs, ys = [None] * lk, [None] * lk
            for q in range(0, count, 4):
                px, py = [None] * lk, [None] * lk
                for p in (q, q + 2):
                    c, ct = [c_ref[p + i, w, m] for i in range(2)], [ct_ref[p + i, w, m] for i in range(2)]
                    for k in range(lk):
                        v = [q_ref[slot, slots[k * count + p + i], r, m] for i in range(2)]
                        x, y = c[0] * v[0] + c[1] * v[1], ct[0] * v[0] + ct[1] * v[1]
                        px[k] = x if p == q else px[k] + x
                        py[k] = y if p == q else py[k] + y
                for k in range(lk):
                    xs[k] = px[k] if q == 0 else xs[k] + px[k]
                    ys[k] = py[k] if q == 0 else ys[k] + py[k]
            for k in range(lk):
                x_ref[k, w, m] = xs[k]
                y_ref[k, w, m] = ys[k]
            return 0

        return lax.fori_loop(0, (rows // tr) * (n // tc), tile, 0)

    lax.fori_loop(0, steps, step, 0)


def home_blocks(slots, pieces, full, turned, lk):
    each, n, _ = pieces[0].shape
    count = each * len(pieces)
    rows = n // 8
    vmem = pl.BlockSpec(memory_space=pltpu.VMEM)
    return pl.pallas_call(
        functools.partial(home_kernel, lk, len(pieces)),
        out_shape=[jax.ShapeDtypeStruct((lk, n, n), BF16)] * 2,
        in_specs=[pl.BlockSpec(memory_space=pltpu.SMEM)]
        + [pl.BlockSpec(memory_space=pl.ANY)] * len(pieces) + [vmem, vmem],
        out_specs=[vmem, vmem],
        scratch_shapes=[pltpu.VMEM((2, count, rows, n), BF16), pltpu.SemaphoreType.DMA((2, count))],
        compiler_params=params(38),
        cost_estimate=cost(4 * lk * count * n * n, n * n * (6 * count + 4 * lk)),
        name="home",
    )(slots, *pieces, full, turned)


def rows_kernel(pieces, mine, slots, *refs):
    a_refs, b_refs, refs = refs[:pieces], refs[pieces:2 * pieces], refs[2 * pieces:]
    c_ref, out_ref, re_ref, im_ref = (refs[0],) + refs[-3:]
    each, rows, cols = a_refs[0].shape
    count = pieces * each
    row, col = row_col(rows, cols)
    above = (col - row) + (pl.program_id(0) * cols - mine[0] * rows)
    for s in range(pieces):
        for j in range(each):
            a, b = a_refs[s][j].astype(F32), b_refs[s][j].astype(F32).T
            re_ref[s * each + j] = jnp.where(above >= 0, a, b).astype(BF16)
            im_ref[s * each + j] = jnp.where(above < 0, a, jnp.where(above > 0, -b, 0.0)).astype(BF16)
    tr, kg, tc = 16, 4, 256
    wide = cols // tc

    def tile(index, _):
        r = pl.ds(pl.multiple_of(((index // wide) % (rows // tr)) * tr, tr), tr)
        m = pl.ds(pl.multiple_of((index % wide) * tc, tc), tc)
        k0 = (index // (wide * (rows // tr))) * kg
        us, vs = [None] * kg, [None] * kg
        for q in range(0, count, 4):
            pu, pv = [None] * kg, [None] * kg
            for p in (q, q + 2):
                c = [c_ref[p + i, r, m] for i in range(2)]
                for k in range(kg):
                    slot = [slots[(k0 + k) * count + p + i] for i in range(2)]
                    u = c[0] * re_ref[slot[0], r, m] + c[1] * re_ref[slot[1], r, m]
                    v = c[0] * im_ref[slot[0], r, m] + c[1] * im_ref[slot[1], r, m]
                    pu[k] = u if p == q else pu[k] + u
                    pv[k] = v if p == q else pv[k] + v
            for k in range(kg):
                us[k] = pu[k] if q == 0 else us[k] + pu[k]
                vs[k] = pv[k] if q == 0 else vs[k] + pv[k]
        for k in range(kg):
            out_ref[k0 + k, 0, 0, r, m] = us[k]
            out_ref[k0 + k, 0, 1, r, m] = vs[k]
        return 0

    lax.fori_loop(0, wide * (rows // tr) * (count // kg), tile, 0)


def own_rows(mine, slots, pieces, coupling, energy, le, held):
    each, n, _ = pieces[0].shape
    count, rows, _ = coupling.shape
    cols = n // 2
    alias = [] if held is None else [held]
    in_specs = (
        [pl.BlockSpec((each, rows, cols), lambda t, mine, slots: (0, mine[0], t))] * len(pieces)
        + [pl.BlockSpec((each, cols, rows), lambda t, mine, slots: (0, t, mine[0]))] * len(pieces)
        + [pl.BlockSpec((count, rows, cols), lambda t, mine, slots: (0, 0, t))]
        + [pl.BlockSpec(memory_space=pl.ANY)] * len(alias)
    )
    return pl.pallas_call(
        functools.partial(rows_kernel, len(pieces)),
        out_shape=jax.ShapeDtypeStruct((count, le, 2, rows, n), BF16),
        grid_spec=pltpu.PrefetchScalarGridSpec(
            num_scalar_prefetch=2,
            grid=(n // cols,),
            in_specs=in_specs,
            out_specs=pl.BlockSpec((count, 1, 2, rows, cols), lambda t, mine, slots: (0, energy, 0, 0, t)),
            scratch_shapes=[pltpu.VMEM((count, rows, cols), BF16)] * 2,
        ),
        input_output_aliases={2 + len(in_specs) - 1: 0} if alias else {},
        compiler_params=params(42),
        cost_estimate=cost(4 * count * count * rows * n, rows * n * count * 10),
        name="rows",
    )(mine[None], slots, *pieces, *pieces, coupling, *alias)


def density_terms(energy, g_ref, gamma_ref, x_ref, y_ref):
    n = g_ref.shape[-1]
    gamma = gamma_ref[0, energy:energy + 1, :]
    g_re, g_im = g_ref[0, 0, 0], g_ref[0, 0, 1]
    row, col = row_col(n, n)
    x, yt = x_ref[0].astype(F32), y_ref[0].astype(F32).T
    s_re = jnp.where(col >= row, x, yt).astype(BF16)
    s_im = jnp.where(col < row, x, jnp.where(col > row, -yt, 0.0)).astype(BF16)
    scaled_re = (g_re.astype(F32) * gamma).astype(BF16).astype(F32)
    scaled_im = (g_im.astype(F32) * gamma).astype(BF16).astype(F32)
    m_re = (dot_nn(g_re, s_re) - dot_nn(g_im, s_im) + scaled_re).astype(BF16)
    m_im = (dot_nn(g_re, s_im) + dot_nn(g_im, s_re) + scaled_im).astype(BF16)
    return dot_nt(m_re, g_re) + dot_nt(m_im, g_im), dot_nt(m_im, g_re) - dot_nt(m_re, g_im)


def first_density_kernel(energy, first, g_ref, gamma_ref, x_ref, y_ref, *refs):
    for c, d in enumerate(density_terms(energy, g_ref, gamma_ref, x_ref, y_ref)):
        refs[-1][0, c] = d if first else d + refs[0][0, c]


def first_density(energy, green, broadening, x, y, held):
    lk, le, _, n, _ = green.shape
    alias = [] if held is None else [held]
    pair = pl.BlockSpec((1, 2, n, n), lambda k: (k, 0, 0, 0))
    one = pl.BlockSpec((1, n, n), lambda k: (k, 0, 0))
    return pl.pallas_call(
        functools.partial(first_density_kernel, energy, held is None),
        out_shape=pltpu.HBM((lk, 2, n, n), F32),
        grid=(lk,),
        in_specs=[
            pl.BlockSpec((1, 1, 2, n, n), lambda k: (k, energy, 0, 0, 0)),
            pl.BlockSpec((1, le, n), lambda k: (k, 0, 0)),
            one,
            one,
        ] + [pair] * len(alias),
        out_specs=pair,
        compiler_params=params(38),
        cost_estimate=cost(16 * lk * n**3, lk * n * n * 20),
        name="density",
    )(green, broadening, x, y, *alias)


def last_density_kernel(scale, energy, odd, g_ref, gamma_ref, x_ref, y_ref, held_ref, *refs):
    d_ref, outs = refs[-1], refs[:-1]
    groups, _, rows, _ = outs[0].shape
    for c, d in enumerate(density_terms(energy, g_ref, gamma_ref, x_ref, y_ref)):
        d_ref[c] = (d + held_ref[0, c]) * scale
    for i in range(len(outs) // 2):
        keep_ref, send_ref = outs[2 * i], outs[2 * i + 1]

        @pl.when(pl.program_id(0) == i)
        def _():
            for c in range(2):
                for g in range(groups):
                    mine = pl.multiple_of((2 * g + odd[0]) * rows, rows)
                    other = pl.multiple_of((2 * g + 1 - odd[0]) * rows, rows)
                    keep_ref[g, c] = d_ref[c, pl.ds(mine, rows), :].astype(BF16)
                    send_ref[g, c] = d_ref[c, pl.ds(other, rows), :].astype(BF16)


def last_density(scale, energy, start, count, groups, odd, green, broadening, x, y, held):
    _, le, _, n, _ = green.shape
    rows = n // (2 * groups)
    one = pl.BlockSpec((1, n, n), lambda i, odd: (i, 0, 0))
    out = pl.BlockSpec((groups, 2, rows, n), lambda i, odd: (0, 0, 0, 0))
    return pl.pallas_call(
        functools.partial(last_density_kernel, scale, energy),
        out_shape=[jax.ShapeDtypeStruct((groups, 2, rows, n), BF16)] * (2 * count),
        grid_spec=pltpu.PrefetchScalarGridSpec(
            num_scalar_prefetch=1,
            grid=(count,),
            in_specs=[
                pl.BlockSpec((1, 1, 2, n, n), lambda i, odd: (start + i, energy, 0, 0, 0)),
                pl.BlockSpec((1, le, n), lambda i, odd: (start + i, 0, 0)),
                one,
                one,
                pl.BlockSpec((1, 2, n, n), lambda i, odd: (start + i, 0, 0, 0)),
            ],
            out_specs=[out] * (2 * count),
            scratch_shapes=[pltpu.VMEM((2, n, n), F32)],
        ),
        compiler_params=params(38),
        cost_estimate=cost(count * 16 * n**3, count * n * n * 20),
        name="density",
    )(odd[None], green, broadening, x, y, held)


def pair_sum_kernel(group, keep_ref, recv_ref, *outs):
    groups = len(outs)
    for d in range(groups):
        at = lax.rem(group[0] + d, groups)
        outs[d][...] = (keep_ref[at].astype(F32) + recv_ref[at].astype(F32)).astype(BF16)


def pair_sum(group, keep, recv):
    groups = keep.shape[0]
    vmem = pl.BlockSpec(memory_space=pltpu.VMEM)
    return pl.pallas_call(
        pair_sum_kernel,
        out_shape=[jax.ShapeDtypeStruct(keep.shape[1:], BF16)] * groups,
        in_specs=[pl.BlockSpec(memory_space=pltpu.SMEM), vmem, vmem],
        out_specs=[vmem] * groups,
        compiler_params=params(56),
        cost_estimate=cost(keep.size, keep.size * 6),
        name="pairsum",
    )(group[None], keep, recv)


def staged(green_ret, broadening, coupling, shift_steps, mode_weight, occupation, momentum_map):
    lk, le, _, _, _ = green_ret.shape
    ne, nm = lax.axis_size("energy"), lax.axis_size("mom")
    if le != SHIFT_MAX or lk % 2 or ne % 2 or nm & (nm - 1):
        raise ValueError("unsupported sizes")
    hk, groups = lk // 2, ne // 2
    me, mine = lax.axis_index("energy").astype(jnp.int32), lax.axis_index("mom").astype(jnp.int32)
    odd, group = me & 1, me >> 1
    pairs = [(i, i ^ 1) for i in range(ne)]
    away = [(i, i + (2 if i % 2 else -2)) for i in range(ne) if 0 <= i + (2 if i % 2 else -2) < ne]
    across = [(i, i + (-2 if i % 2 else 2)) for i in range(ne) if 0 <= i + (-2 if i % 2 else 2) < ne]
    strides = []
    while (nm >> (len(strides) + 1)) > 0:
        strides.append(nm >> (len(strides) + 1))

    def over_energy(x, perm):
        return lax.ppermute(x, "energy", perm)

    def swap(x, stride):
        return lax.ppermute(x, "mom", [(i, i ^ stride) for i in range(nm)])

    def spread(x):
        held = [x]
        for s in strides:
            held = held + [swap(piece, s) for piece in held]
        return held

    order = [0]
    for s in strides:
        order = order + [o ^ s for o in order]

    weights = []
    for s in range(1, SHIFT_MAX + 1):
        held = shift_steps == s
        weights.append(jnp.sum(jnp.where(held, mode_weight * (occupation + 1.0), 0.0)))
        weights.append(jnp.sum(jnp.where(held, mode_weight * occupation, 0.0)))
    weights = jnp.stack(weights)

    owner, inner = momentum_map // lk, momentum_map % lk
    place = jnp.zeros_like(owner)
    for at, o in enumerate(order):
        place = jnp.where((owner ^ mine) == o, at, place)
    slots = (place * lk + ((inner // hk) ^ odd) * hk + inner % hk).astype(jnp.int32)
    own_slots = lax.dynamic_slice_in_dim(slots, mine * lk, lk, 0).reshape(-1)
    all_slots = slots.reshape(-1)

    green_ret = pltpu.with_memory_space_constraint(green_ret, pltpu.HBM)
    coupling = pltpu.with_memory_space_constraint(coupling, pltpu.HBM)
    coupling_pieces = spread(coupling)

    send = [lesser_packed((1 - odd) * hk + j, green_ret, broadening) for j in range(hk)]
    recv = [[over_energy(send[j][h], pairs) for h in range(2)] for j in range(hk)]
    keep = [lesser_packed(odd * hk + j, green_ret, broadening) for j in range(hk)]
    kz = [[over_energy(keep[j][h], away) for h in range(2)] for j in range(hk)]
    rz = [[over_energy(recv[j][h], across) for h in range(2)] for j in range(hk)]
    got, last = [], None
    for j in range(hk):
        for h in range(2):
            last = sources(
                odd, weights, j, h, hk, keep[j][h], recv[j][h], kz[j][h], rz[j][h], last)
        got.append(last)

    full, turned = place_coupling(jnp.stack([mine ^ o for o in order]), coupling_pieces)

    held_rows, held_density = None, None
    scale = 1.0 / (le * ne)
    late = []
    for e in range(le):
        use = [got[j] for j in range(hk)] if e == 0 else [last]
        fresh = [spread(part[e]) for part in use]
        back = [spread(over_energy(part[le + e], pairs)) for part in use]
        pieces = [part[at] for at in range(nm) for part in fresh + back]
        if e < le - 1:
            x, y = home_blocks(own_slots, pieces, full, turned, lk)
            held_density = first_density(e, green_ret, broadening, x, y, held_density)
        else:
            shares = []
            nk = lk * nm
            for half in range(2):
                first = half * hk
                some = lax.slice_in_dim(own_slots, first * nk, (first + hk) * nk)
                x, y = home_blocks(some, pieces, full, turned, hk)
                shares = shares + list(last_density(
                    scale, e, first, hk, groups, odd,
                    green_ret, broadening, x, y, held_density))
            for k in range(lk):
                kept, sent = shares[2 * k], shares[2 * k + 1]
                other = over_energy(sent, pairs)
                parts = pair_sum(group, kept, other)
                total = parts[0].astype(F32)
                for d in range(1, groups):
                    perm = [(i, (i + 2 * d) % ne) for i in range(ne)]
                    total = total + over_energy(parts[d], perm).astype(F32)
                late.append(total)
        held_rows = own_rows(mine, all_slots, pieces, coupling, e, le, held_rows)
    density = jnp.transpose(jnp.stack(late), (2, 0, 1, 3))
    return held_rows, density


def solution(mesh):
    return jax.shard_map(
        staged,
        mesh=mesh,
        in_specs=(
            P("mom", "energy", None, None, None),
            P("mom", "energy", None),
            P(None, "mom", None),
            P(),
            P(),
            P(),
            P(),
        ),
        out_specs=(P(None, "energy", None, "mom", None), P("energy", "mom", None, None)),
        check_vma=False,
    )
```

```python
import functools

import jax
import jax.numpy as jnp
from jax import lax
from jax.experimental import pallas as pl
from jax.experimental.pallas import tpu as pltpu
from jax.sharding import PartitionSpec as P


SHIFT_MAX = 2
F32 = jnp.float32
BF16 = jnp.bfloat16


def params(mib):
    return pltpu.CompilerParams(vmem_limit_bytes=mib * 1024 * 1024)


def hbm(x):
    return pltpu.with_memory_space_constraint(x, pltpu.HBM)


def cost(flops, nbytes):
    return pl.CostEstimate(flops=int(flops), bytes_accessed=int(nbytes), transcendentals=0)


def dot_nt(a, b):
    return lax.dot_general(a, b, (((1,), (1,)), ((), ())), preferred_element_type=F32)


def dot_nn(a, b):
    return lax.dot_general(a, b, (((1,), (0,)), ((), ())), preferred_element_type=F32)


def row_col(rows, cols):
    return lax.broadcasted_iota(jnp.int32, (rows, cols), 0), lax.broadcasted_iota(jnp.int32, (rows, cols), 1)


def lesser_kernel(sel, g_ref, gamma_ref, *outs):
    n = g_ref.shape[-1]
    half = n // 2
    e = pl.program_id(0)
    gamma = gamma_ref[0, pl.ds(e, 1), :]
    g_re, g_im = g_ref[0, 0, 0], g_ref[0, 0, 1]
    s_re = (g_re.astype(F32) * gamma).astype(BF16)
    s_im = (g_im.astype(F32) * gamma).astype(BF16)
    row, col = row_col(half, half)

    def real(i, j):
        i, j = slice(i * half, (i + 1) * half), slice(j * half, (j + 1) * half)
        return dot_nt(s_re[i], g_re[j]) + dot_nt(s_im[i], g_im[j])

    def imag(i, j):
        i, j = slice(i * half, (i + 1) * half), slice(j * half, (j + 1) * half)
        return dot_nt(s_im[i], g_re[j]) - dot_nt(s_re[i], g_im[j])

    for d in range(2):
        outs[d][0, :, d * half:(d + 1) * half] = jnp.where(col >= row, real(d, d), imag(d, d)).astype(BF16)
    outs[0][0, :, half:] = real(0, 1).astype(BF16)
    outs[1][0, :, :half] = imag(1, 0).astype(BF16)


def lesser_packed(which, green, broadening):
    _, le, _, n, _ = green.shape
    return pl.pallas_call(
        lesser_kernel,
        out_shape=[pltpu.HBM((le, n // 2, n), BF16)] * 2,
        grid_spec=pltpu.PrefetchScalarGridSpec(
            num_scalar_prefetch=1,
            grid=(le,),
            in_specs=[
                pl.BlockSpec((1, 1, 2, n, n), lambda e, sel: (sel[0], e, 0, 0, 0)),
                pl.BlockSpec((1, le, n), lambda e, sel: (sel[0], 0, 0)),
            ],
            out_specs=[pl.BlockSpec((1, n // 2, n), lambda e, sel: (e, 0, 0))] * 2,
        ),
        compiler_params=params(56),
        cost_estimate=cost(le * 6 * n**3, le * n * n * 6),
        name="lesser",
    )(which[None], green, broadening)


def place_kernel(where, *refs):
    pieces, (full_ref, turned_ref) = refs[:-2], refs[-2:]
    rows = pieces[0].shape[1]
    for at, c_ref in enumerate(pieces):
        start = pl.ds(pl.multiple_of(where[at] * rows, rows), rows)
        for q in range(c_ref.shape[0]):
            full_ref[q, start, :] = c_ref[q]
            turned_ref[q, :, start] = c_ref[q].T


def place_coupling(where, pieces):
    nk, rows, n = pieces[0].shape
    each = 2
    return pl.pallas_call(
        place_kernel,
        out_shape=[pltpu.HBM((nk, n, n), BF16)] * 2,
        grid_spec=pltpu.PrefetchScalarGridSpec(
            num_scalar_prefetch=1,
            grid=(nk // each,),
            in_specs=[pl.BlockSpec((each, rows, n), lambda q, w: (q, 0, 0))] * len(pieces),
            out_specs=[pl.BlockSpec((each, n, n), lambda q, w: (q, 0, 0))] * 2,
        ),
        compiler_params=params(56),
        cost_estimate=cost(nk * n * n * 4, nk * n * n * 6),
        name="place",
    )(where, *pieces)


def source_kernel(odd, w_ref, keep, recv, kz, rz, *refs):
    le = keep.shape[0]
    outs = refs[-2 * le:]

    def emit(order):
        line = [(ref, e) for ref in order for e in range(le)]
        for e in range(le):
            for ref, target in ((keep, outs[e]), (recv, outs[le + e])):
                at = [i for i, held in enumerate(order) if held is ref][0] * le + e
                total = None
                for s in range(1, SHIFT_MAX + 1):
                    for j, sign in ((0, s), (1, -s)):
                        source, index = line[at + sign]
                        term = w_ref[2 * (s - 1) + j] * source[index].astype(F32)
                        total = term if total is None else total + term
                target[0] = total.astype(BF16)

    @pl.when(odd[0] == 0)
    def _():
        emit((rz, keep, recv, kz))

    @pl.when(odd[0] == 1)
    def _():
        emit((kz, recv, keep, rz))


def sources(odd, weights, j, h, hk, keep, recv, kz, rz, held):
    le, half, n = keep.shape
    rows = half // 2
    at = h * (half // rows)
    big = pl.BlockSpec((le, rows, n), lambda r, *_: (0, r, 0))
    first = pl.BlockSpec((1, rows, n), lambda r, *_: (0, at + r, 0))
    later = pl.BlockSpec((1, rows, n), lambda r, *_: (j, at + r, 0))
    shapes = [(1 if e == 0 else hk, n, n) for e in range(le)] * 2
    specs = [first if e == 0 else later for e in range(le)] * 2
    alias, extra = {}, []
    if held is not None:
        for i, value in enumerate(held):
            if i % le or h:
                alias[6 + len(extra)] = i
                extra.append(value)
    return pl.pallas_call(
        source_kernel,
        out_shape=[pltpu.HBM(shape, BF16) for shape in shapes],
        grid_spec=pltpu.PrefetchScalarGridSpec(
            num_scalar_prefetch=2,
            grid=(half // rows,),
            in_specs=[big] * 4 + [pl.BlockSpec(memory_space=pl.ANY)] * len(extra),
            out_specs=specs,
        ),
        input_output_aliases=alias,
        compiler_params=params(56),
        cost_estimate=cost(le * half * n * 16, le * half * n * 12),
        name="source",
    )(odd[None], weights, keep, recv, kz, rz, *extra)


def home_kernel(lk, pieces, slots, *refs):
    ins, (c_ref, ct_ref, x_ref, y_ref, q_ref) = refs[:pieces], refs[pieces:]
    each, rows, n = ins[0].shape
    count = pieces * each
    for s in range(pieces):
        for j in range(each):
            q_ref[s * each + j] = ins[s][j]
    tr, tc = 16, 256

    def tile(index, _):
        r = pl.ds(pl.multiple_of((index // (n // tc)) * tr, tr), tr)
        m = pl.ds(pl.multiple_of((index % (n // tc)) * tc, tc), tc)
        xs, ys = [None] * lk, [None] * lk
        for q in range(0, count, 4):
            px, py = [None] * lk, [None] * lk
            for p in (q, q + 2):
                c, ct = [c_ref[p + i, r, m] for i in range(2)], [ct_ref[p + i, r, m] for i in range(2)]
                for k in range(lk):
                    v = [q_ref[slots[k * count + p + i], r, m] for i in range(2)]
                    x, y = c[0] * v[0] + c[1] * v[1], ct[0] * v[0] + ct[1] * v[1]
                    px[k] = x if p == q else px[k] + x
                    py[k] = y if p == q else py[k] + y
            for k in range(lk):
                xs[k] = px[k] if q == 0 else xs[k] + px[k]
                ys[k] = py[k] if q == 0 else ys[k] + py[k]
        for k in range(lk):
            x_ref[k, r, m] = xs[k]
            y_ref[k, r, m] = ys[k]
        return 0

    lax.fori_loop(0, (rows // tr) * (n // tc), tile, 0)


def home_blocks(slots, pieces, full, turned, lk):
    each, n, _ = pieces[0].shape
    count = each * len(pieces)
    rows = n // 8
    block = lambda lead: pl.BlockSpec((lead, rows, n), lambda g, s: (0, g, 0))
    return pl.pallas_call(
        functools.partial(home_kernel, lk, len(pieces)),
        out_shape=[pltpu.HBM((lk, n, n), BF16)] * 2,
        grid_spec=pltpu.PrefetchScalarGridSpec(
            num_scalar_prefetch=1,
            grid=(n // rows,),
            in_specs=[block(each)] * len(pieces) + [block(count), block(count)],
            out_specs=[block(lk), block(lk)],
            scratch_shapes=[pltpu.VMEM((count, rows, n), BF16)],
        ),
        compiler_params=params(56),
        cost_estimate=cost(4 * lk * count * n * n, n * n * (6 * count + 4 * lk)),
        name="home",
    )(slots, *pieces, full, turned)


def rows_kernel(pieces, mine, slots, *refs):
    a_refs, b_refs, refs = refs[:pieces], refs[pieces:2 * pieces], refs[2 * pieces:]
    c_ref, out_ref, re_ref, im_ref = (refs[0],) + refs[-3:]
    each, rows, cols = a_refs[0].shape
    count = pieces * each
    row, col = row_col(rows, cols)
    above = (col - row) + (pl.program_id(0) * cols - mine[0] * rows)
    for s in range(pieces):
        for j in range(each):
            a, b = a_refs[s][j].astype(F32), b_refs[s][j].astype(F32).T
            re_ref[s * each + j] = jnp.where(above >= 0, a, b).astype(BF16)
            im_ref[s * each + j] = jnp.where(above < 0, a, jnp.where(above > 0, -b, 0.0)).astype(BF16)
    tr, kg, tc = 16, 4, 256
    wide = cols // tc

    def tile(index, _):
        r = pl.ds(pl.multiple_of(((index // wide) % (rows // tr)) * tr, tr), tr)
        m = pl.ds(pl.multiple_of((index % wide) * tc, tc), tc)
        k0 = (index // (wide * (rows // tr))) * kg
        us, vs = [None] * kg, [None] * kg
        for q in range(0, count, 4):
            pu, pv = [None] * kg, [None] * kg
            for p in (q, q + 2):
                c = [c_ref[p + i, r, m] for i in range(2)]
                for k in range(kg):
                    slot = [slots[(k0 + k) * count + p + i] for i in range(2)]
                    u = c[0] * re_ref[slot[0], r, m] + c[1] * re_ref[slot[1], r, m]
                    v = c[0] * im_ref[slot[0], r, m] + c[1] * im_ref[slot[1], r, m]
                    pu[k] = u if p == q else pu[k] + u
                    pv[k] = v if p == q else pv[k] + v
            for k in range(kg):
                us[k] = pu[k] if q == 0 else us[k] + pu[k]
                vs[k] = pv[k] if q == 0 else vs[k] + pv[k]
        for k in range(kg):
            out_ref[k0 + k, 0, 0, r, m] = us[k]
            out_ref[k0 + k, 0, 1, r, m] = vs[k]
        return 0

    lax.fori_loop(0, wide * (rows // tr) * (count // kg), tile, 0)


def own_rows(mine, slots, pieces, coupling, energy, le, held):
    each, n, _ = pieces[0].shape
    count, rows, _ = coupling.shape
    cols = n // 2
    alias = [] if held is None else [held]
    in_specs = (
        [pl.BlockSpec((each, rows, cols), lambda t, mine, slots: (0, mine[0], t))] * len(pieces)
        + [pl.BlockSpec((each, cols, rows), lambda t, mine, slots: (0, t, mine[0]))] * len(pieces)
        + [pl.BlockSpec((count, rows, cols), lambda t, mine, slots: (0, 0, t))]
        + [pl.BlockSpec(memory_space=pl.ANY)] * len(alias)
    )
    return pl.pallas_call(
        functools.partial(rows_kernel, len(pieces)),
        out_shape=jax.ShapeDtypeStruct((count, le, 2, rows, n), BF16),
        grid_spec=pltpu.PrefetchScalarGridSpec(
            num_scalar_prefetch=2,
            grid=(n // cols,),
            in_specs=in_specs,
            out_specs=pl.BlockSpec((count, 1, 2, rows, cols), lambda t, mine, slots: (0, energy, 0, 0, t)),
            scratch_shapes=[pltpu.VMEM((count, rows, cols), BF16)] * 2,
        ),
        input_output_aliases={2 + len(in_specs) - 1: 0} if alias else {},
        compiler_params=params(56),
        cost_estimate=cost(4 * count * count * rows * n, rows * n * count * 10),
        name="rows",
    )(mine[None], slots, *pieces, *pieces, coupling, *alias)


def density_terms(energy, g_ref, gamma_ref, x_ref, y_ref):
    n = g_ref.shape[-1]
    gamma = gamma_ref[0, energy:energy + 1, :]
    g_re, g_im = g_ref[0, 0, 0], g_ref[0, 0, 1]
    row, col = row_col(n, n)
    x, yt = x_ref[0].astype(F32), y_ref[0].astype(F32).T
    s_re = jnp.where(col >= row, x, yt).astype(BF16)
    s_im = jnp.where(col < row, x, jnp.where(col > row, -yt, 0.0)).astype(BF16)
    scaled_re = (g_re.astype(F32) * gamma).astype(BF16).astype(F32)
    scaled_im = (g_im.astype(F32) * gamma).astype(BF16).astype(F32)
    m_re = (dot_nn(g_re, s_re) - dot_nn(g_im, s_im) + scaled_re).astype(BF16)
    m_im = (dot_nn(g_re, s_im) + dot_nn(g_im, s_re) + scaled_im).astype(BF16)
    return dot_nt(m_re, g_re) + dot_nt(m_im, g_im), dot_nt(m_im, g_re) - dot_nt(m_re, g_im)


def first_density_kernel(energy, first, g_ref, gamma_ref, x_ref, y_ref, *refs):
    for c, d in enumerate(density_terms(energy, g_ref, gamma_ref, x_ref, y_ref)):
        refs[-1][0, c] = d if first else d + refs[0][0, c]


def first_density(energy, green, broadening, x, y, held):
    lk, le, _, n, _ = green.shape
    alias = [] if held is None else [held]
    pair = pl.BlockSpec((1, 2, n, n), lambda k: (k, 0, 0, 0))
    one = pl.BlockSpec((1, n, n), lambda k: (k, 0, 0))
    return pl.pallas_call(
        functools.partial(first_density_kernel, energy, held is None),
        out_shape=pltpu.HBM((lk, 2, n, n), F32),
        grid=(lk,),
        in_specs=[
            pl.BlockSpec((1, 1, 2, n, n), lambda k: (k, energy, 0, 0, 0)),
            pl.BlockSpec((1, le, n), lambda k: (k, 0, 0)),
            one,
            one,
        ] + [pair] * len(alias),
        out_specs=pair,
        compiler_params=params(56),
        cost_estimate=cost(16 * lk * n**3, lk * n * n * 20),
        name="density",
    )(green, broadening, x, y, *alias)


def last_density_kernel(scale, energy, odd, g_ref, gamma_ref, x_ref, y_ref, held_ref, *refs):
    d_ref, outs = refs[-1], refs[:-1]
    groups, _, rows, _ = outs[0].shape
    for c, d in enumerate(density_terms(energy, g_ref, gamma_ref, x_ref, y_ref)):
        d_ref[c] = (d + held_ref[0, c]) * scale
    for i in range(len(outs) // 2):
        keep_ref, send_ref = outs[2 * i], outs[2 * i + 1]

        @pl.when(pl.program_id(0) == i)
        def _():
            for c in range(2):
                for g in range(groups):
                    mine = pl.multiple_of((2 * g + odd[0]) * rows, rows)
                    other = pl.multiple_of((2 * g + 1 - odd[0]) * rows, rows)
                    keep_ref[g, c] = d_ref[c, pl.ds(mine, rows), :].astype(BF16)
                    send_ref[g, c] = d_ref[c, pl.ds(other, rows), :].astype(BF16)


def last_density(scale, energy, start, count, groups, odd, green, broadening, x, y, held):
    _, le, _, n, _ = green.shape
    rows = n // (2 * groups)
    one = pl.BlockSpec((1, n, n), lambda i, odd: (start + i, 0, 0))
    out = pl.BlockSpec((groups, 2, rows, n), lambda i, odd: (0, 0, 0, 0))
    return pl.pallas_call(
        functools.partial(last_density_kernel, scale, energy),
        out_shape=[jax.ShapeDtypeStruct((groups, 2, rows, n), BF16)] * (2 * count),
        grid_spec=pltpu.PrefetchScalarGridSpec(
            num_scalar_prefetch=1,
            grid=(count,),
            in_specs=[
                pl.BlockSpec((1, 1, 2, n, n), lambda i, odd: (start + i, energy, 0, 0, 0)),
                pl.BlockSpec((1, le, n), lambda i, odd: (start + i, 0, 0)),
                one,
                one,
                pl.BlockSpec((1, 2, n, n), lambda i, odd: (start + i, 0, 0, 0)),
            ],
            out_specs=[out] * (2 * count),
            scratch_shapes=[pltpu.VMEM((2, n, n), F32)],
        ),
        compiler_params=params(56),
        cost_estimate=cost(count * 16 * n**3, count * n * n * 20),
        name="density",
    )(odd[None], green, broadening, x, y, held)


def pair_sum_kernel(group, keep_ref, recv_ref, *outs):
    groups = len(outs)
    for d in range(groups):
        at = lax.rem(group[0] + d, groups)
        outs[d][...] = (keep_ref[at].astype(F32) + recv_ref[at].astype(F32)).astype(BF16)


def pair_sum(group, keep, recv):
    groups = keep.shape[0]
    vmem = pl.BlockSpec(memory_space=pltpu.VMEM)
    return pl.pallas_call(
        pair_sum_kernel,
        out_shape=[jax.ShapeDtypeStruct(keep.shape[1:], BF16)] * groups,
        in_specs=[pl.BlockSpec(memory_space=pltpu.SMEM), vmem, vmem],
        out_specs=[vmem] * groups,
        compiler_params=params(56),
        cost_estimate=cost(keep.size, keep.size * 6),
        name="pairsum",
    )(group[None], keep, recv)


def staged(green_ret, broadening, coupling, shift_steps, mode_weight, occupation, momentum_map):
    lk, le, _, _, _ = green_ret.shape
    ne, nm = lax.axis_size("energy"), lax.axis_size("mom")
    if le != SHIFT_MAX or lk % 2 or ne % 2 or nm & (nm - 1):
        raise ValueError("unsupported sizes")
    hk, groups = lk // 2, ne // 2
    me, mine = lax.axis_index("energy").astype(jnp.int32), lax.axis_index("mom").astype(jnp.int32)
    odd, group = me & 1, me >> 1
    pairs = [(i, i ^ 1) for i in range(ne)]
    away = [(i, i + (2 if i % 2 else -2)) for i in range(ne) if 0 <= i + (2 if i % 2 else -2) < ne]
    across = [(i, i + (-2 if i % 2 else 2)) for i in range(ne) if 0 <= i + (-2 if i % 2 else 2) < ne]
    strides = []
    while (nm >> (len(strides) + 1)) > 0:
        strides.append(nm >> (len(strides) + 1))

    def permuted(x, perm):
        return lax.ppermute(x, "energy", perm)

    def over_energy(x, perm):
        return hbm(permuted(x, perm))

    def swap(x, stride):
        moved = lax.ppermute(x, "mom", [(i, i ^ stride) for i in range(nm)])
        return hbm(moved)

    def spread(x):
        held = [x]
        for s in strides:
            held = held + [swap(piece, s) for piece in held]
        return held

    order = [0]
    for s in strides:
        order = order + [o ^ s for o in order]

    weights = []
    for s in range(1, SHIFT_MAX + 1):
        held = shift_steps == s
        weights.append(jnp.sum(jnp.where(held, mode_weight * (occupation + 1.0), 0.0)))
        weights.append(jnp.sum(jnp.where(held, mode_weight * occupation, 0.0)))
    weights = jnp.stack(weights)

    owner, inner = momentum_map // lk, momentum_map % lk
    place = jnp.zeros_like(owner)
    for at, o in enumerate(order):
        place = jnp.where((owner ^ mine) == o, at, place)
    slots = (place * lk + ((inner // hk) ^ odd) * hk + inner % hk).astype(jnp.int32)
    own_slots = lax.dynamic_slice_in_dim(slots, mine * lk, lk, 0).reshape(-1)
    all_slots = slots.reshape(-1)

    green_ret = hbm(green_ret)
    coupling = hbm(coupling)
    coupling_pieces = spread(coupling)

    send = [lesser_packed((1 - odd) * hk + j, green_ret, broadening) for j in range(hk)]
    recv = [[over_energy(send[j][h], pairs) for h in range(2)] for j in range(hk)]
    keep = [lesser_packed(odd * hk + j, green_ret, broadening) for j in range(hk)]
    kz = [[over_energy(keep[j][h], away) for h in range(2)] for j in range(hk)]
    rz = [[over_energy(recv[j][h], across) for h in range(2)] for j in range(hk)]
    got, last = [], None
    for j in range(hk):
        for h in range(2):
            last = sources(
                odd, weights, j, h, hk, keep[j][h], recv[j][h], kz[j][h], rz[j][h], last)
        got.append(last)

    full, turned = place_coupling(jnp.stack([mine ^ o for o in order]), coupling_pieces)

    held_rows, held_density = None, None
    scale = 1.0 / (le * ne)
    late = []
    for e in range(le):
        use = [got[j] for j in range(hk)] if e == 0 else [last]
        fresh = [spread(part[e]) for part in use]
        back = [spread(over_energy(part[le + e], pairs)) for part in use]
        pieces = [part[at] for at in range(nm) for part in fresh + back]
        if e < le - 1:
            x, y = home_blocks(own_slots, pieces, full, turned, lk)
            held_density = first_density(e, green_ret, broadening, x, y, held_density)
        else:
            shares = []
            x, y = home_blocks(own_slots, pieces, full, turned, lk)
            for first, count in ((0, 1), (1, lk - 1)):
                shares = shares + list(last_density(
                    scale, e, first, count, groups, odd,
                    green_ret, broadening, x, y, held_density))
            for k in range(lk):
                kept, sent = shares[2 * k], shares[2 * k + 1]
                other = permuted(sent, pairs)
                parts = pair_sum(group, kept, other)
                total = parts[0].astype(F32)
                for d in range(1, groups):
                    perm = [(i, (i + 2 * d) % ne) for i in range(ne)]
                    total = total + permuted(parts[d], perm).astype(F32)
                late.append(total)
        held_rows = own_rows(mine, all_slots, pieces, coupling, e, le, held_rows)
    density = jnp.transpose(jnp.stack(late), (2, 0, 1, 3))
    return held_rows, density


def solution(mesh):
    return jax.shard_map(
        staged,
        mesh=mesh,
        in_specs=(
            P("mom", "energy", None, None, None),
            P("mom", "energy", None),
            P(None, "mom", None),
            P(),
            P(),
            P(),
            P(),
        ),
        out_specs=(P(None, "energy", None, "mom", None), P("energy", "mom", None, None)),
        check_vma=False,
    )
```

```python
import functools

import jax
import jax.numpy as jnp
from jax import lax
from jax.experimental import pallas as pl
from jax.experimental.pallas import tpu as pltpu
from jax.sharding import PartitionSpec as P


SHIFT_MAX = 2
F32 = jnp.float32
BF16 = jnp.bfloat16


def params(mib):
    return pltpu.CompilerParams(vmem_limit_bytes=mib * 1024 * 1024)


def hbm(x):
    return pltpu.with_memory_space_constraint(x, pltpu.HBM)


def cost(flops, nbytes):
    return pl.CostEstimate(flops=int(flops), bytes_accessed=int(nbytes), transcendentals=0)


def dot_nt(a, b):
    return lax.dot_general(a, b, (((1,), (1,)), ((), ())), preferred_element_type=F32)


def dot_nn(a, b):
    return lax.dot_general(a, b, (((1,), (0,)), ((), ())), preferred_element_type=F32)


def row_col(rows, cols):
    return lax.broadcasted_iota(jnp.int32, (rows, cols), 0), lax.broadcasted_iota(jnp.int32, (rows, cols), 1)


def lesser_kernel(sel, g_ref, gamma_ref, *outs):
    n = g_ref.shape[-1]
    half = n // 2
    e = pl.program_id(0)
    gamma = gamma_ref[0, pl.ds(e, 1), :]
    g_re, g_im = g_ref[0, 0, 0], g_ref[0, 0, 1]
    s_re = (g_re.astype(F32) * gamma).astype(BF16)
    s_im = (g_im.astype(F32) * gamma).astype(BF16)
    row, col = row_col(half, half)

    def real(i, j):
        i, j = slice(i * half, (i + 1) * half), slice(j * half, (j + 1) * half)
        return dot_nt(s_re[i], g_re[j]) + dot_nt(s_im[i], g_im[j])

    def imag(i, j):
        i, j = slice(i * half, (i + 1) * half), slice(j * half, (j + 1) * half)
        return dot_nt(s_im[i], g_re[j]) - dot_nt(s_re[i], g_im[j])

    for d in range(2):
        outs[d][0, :, d * half:(d + 1) * half] = jnp.where(col >= row, real(d, d), imag(d, d)).astype(BF16)
    outs[0][0, :, half:] = real(0, 1).astype(BF16)
    outs[1][0, :, :half] = imag(1, 0).astype(BF16)


def lesser_packed(which, green, broadening):
    _, le, _, n, _ = green.shape
    return pl.pallas_call(
        lesser_kernel,
        out_shape=[pltpu.HBM((le, n // 2, n), BF16)] * 2,
        grid_spec=pltpu.PrefetchScalarGridSpec(
            num_scalar_prefetch=1,
            grid=(le,),
            in_specs=[
                pl.BlockSpec((1, 1, 2, n, n), lambda e, sel: (sel[0], e, 0, 0, 0)),
                pl.BlockSpec((1, le, n), lambda e, sel: (sel[0], 0, 0)),
            ],
            out_specs=[pl.BlockSpec((1, n // 2, n), lambda e, sel: (e, 0, 0))] * 2,
        ),
        compiler_params=params(56),
        cost_estimate=cost(le * 6 * n**3, le * n * n * 6),
        name="lesser",
    )(which[None], green, broadening)


def place_kernel(where, *refs):
    pieces, (full_ref, turned_ref) = refs[:-2], refs[-2:]
    rows = pieces[0].shape[1]
    for at, c_ref in enumerate(pieces):
        start = pl.ds(pl.multiple_of(where[at] * rows, rows), rows)
        for q in range(c_ref.shape[0]):
            full_ref[q, start, :] = c_ref[q]
            turned_ref[q, :, start] = c_ref[q].T


def place_coupling(where, pieces):
    nk, rows, n = pieces[0].shape
    each = 2
    return pl.pallas_call(
        place_kernel,
        out_shape=[pltpu.HBM((nk, n, n), BF16)] * 2,
        grid_spec=pltpu.PrefetchScalarGridSpec(
            num_scalar_prefetch=1,
            grid=(nk // each,),
            in_specs=[pl.BlockSpec((each, rows, n), lambda q, w: (q, 0, 0))] * len(pieces),
            out_specs=[pl.BlockSpec((each, n, n), lambda q, w: (q, 0, 0))] * 2,
        ),
        compiler_params=params(56),
        cost_estimate=cost(nk * n * n * 4, nk * n * n * 6),
        name="place",
    )(where, *pieces)


def source_kernel(odd, w_ref, keep, recv, kz, rz, *refs):
    le = keep.shape[0]
    outs = refs[-2 * le:]

    def emit(order):
        line = [(ref, e) for ref in order for e in range(le)]
        for e in range(le):
            for ref, target in ((keep, outs[e]), (recv, outs[le + e])):
                at = [i for i, held in enumerate(order) if held is ref][0] * le + e
                total = None
                for s in range(1, SHIFT_MAX + 1):
                    for j, sign in ((0, s), (1, -s)):
                        source, index = line[at + sign]
                        term = w_ref[2 * (s - 1) + j] * source[index].astype(F32)
                        total = term if total is None else total + term
                target[0] = total.astype(BF16)

    @pl.when(odd[0] == 0)
    def _():
        emit((rz, keep, recv, kz))

    @pl.when(odd[0] == 1)
    def _():
        emit((kz, recv, keep, rz))


def sources(odd, weights, j, h, hk, keep, recv, kz, rz, held):
    le, half, n = keep.shape
    rows = half // 2
    at = h * (half // rows)
    big = pl.BlockSpec((le, rows, n), lambda r, *_: (0, r, 0))
    first = pl.BlockSpec((1, rows, n), lambda r, *_: (0, at + r, 0))
    later = pl.BlockSpec((1, rows, n), lambda r, *_: (j, at + r, 0))
    shapes = [(1 if e == 0 else hk, n, n) for e in range(le)] * 2
    specs = [first if e == 0 else later for e in range(le)] * 2
    alias, extra = {}, []
    if held is not None:
        for i, value in enumerate(held):
            if i % le or h:
                alias[6 + len(extra)] = i
                extra.append(value)
    return pl.pallas_call(
        source_kernel,
        out_shape=[pltpu.HBM(shape, BF16) for shape in shapes],
        grid_spec=pltpu.PrefetchScalarGridSpec(
            num_scalar_prefetch=2,
            grid=(half // rows,),
            in_specs=[big] * 4 + [pl.BlockSpec(memory_space=pl.ANY)] * len(extra),
            out_specs=specs,
        ),
        input_output_aliases=alias,
        compiler_params=params(56),
        cost_estimate=cost(le * half * n * 16, le * half * n * 12),
        name="source",
    )(odd[None], weights, keep, recv, kz, rz, *extra)


def home_kernel(lk, pieces, slots, *refs):
    ins, (c_ref, ct_ref, x_ref, y_ref, q_ref) = refs[:pieces], refs[pieces:]
    each, rows, n = ins[0].shape
    count = pieces * each
    for s in range(pieces):
        for j in range(each):
            q_ref[s * each + j] = ins[s][j]
    tr, tc = 16, 256

    def tile(index, _):
        r = pl.ds(pl.multiple_of((index // (n // tc)) * tr, tr), tr)
        m = pl.ds(pl.multiple_of((index % (n // tc)) * tc, tc), tc)
        xs, ys = [None] * lk, [None] * lk
        for q in range(0, count, 4):
            px, py = [None] * lk, [None] * lk
            for p in (q, q + 2):
                c, ct = [c_ref[p + i, r, m] for i in range(2)], [ct_ref[p + i, r, m] for i in range(2)]
                for k in range(lk):
                    v = [q_ref[slots[k * count + p + i], r, m] for i in range(2)]
                    x, y = c[0] * v[0] + c[1] * v[1], ct[0] * v[0] + ct[1] * v[1]
                    px[k] = x if p == q else px[k] + x
                    py[k] = y if p == q else py[k] + y
            for k in range(lk):
                xs[k] = px[k] if q == 0 else xs[k] + px[k]
                ys[k] = py[k] if q == 0 else ys[k] + py[k]
        for k in range(lk):
            x_ref[k, r, m] = xs[k]
            y_ref[k, r, m] = ys[k]
        return 0

    lax.fori_loop(0, (rows // tr) * (n // tc), tile, 0)


def home_blocks(slots, pieces, full, turned, lk):
    each, n, _ = pieces[0].shape
    count = each * len(pieces)
    rows = n // 4
    block = lambda lead: pl.BlockSpec((lead, rows, n), lambda g, s: (0, g, 0))
    return pl.pallas_call(
        functools.partial(home_kernel, lk, len(pieces)),
        out_shape=[pltpu.VMEM((lk, n, n), BF16)] * 2,
        grid_spec=pltpu.PrefetchScalarGridSpec(
            num_scalar_prefetch=1,
            grid=(n // rows,),
            in_specs=[block(each)] * len(pieces) + [block(count), block(count)],
            out_specs=[block(lk), block(lk)],
            scratch_shapes=[pltpu.VMEM((count, rows, n), BF16)],
        ),
        compiler_params=params(44),
        cost_estimate=cost(4 * lk * count * n * n, n * n * (6 * count + 4 * lk)),
        name="home",
    )(slots, *pieces, full, turned)


def rows_kernel(pieces, mine, slots, *refs):
    a_refs, b_refs, refs = refs[:pieces], refs[pieces:2 * pieces], refs[2 * pieces:]
    c_ref, out_ref, d_ref = (refs[0],) + refs[-2:]
    each, rows, cols = a_refs[0].shape
    count = pieces * each
    row, col = row_col(rows, cols)
    above = (col - row) + (pl.program_id(0) * cols - mine[0] * rows)
    for s in range(pieces):
        for j in range(each):
            a, b = a_refs[s][j].astype(F32), b_refs[s][j].astype(F32).T
            d_ref[s * each + j, 0] = jnp.where(above >= 0, a, b).astype(BF16)
            d_ref[s * each + j, 1] = jnp.where(above < 0, a, jnp.where(above > 0, -b, 0.0)).astype(BF16)
    tr, kg, tc = 32, 2, 256
    wide = cols // tc

    def tile(index, _):
        r = pl.ds(pl.multiple_of(((index // wide) % (rows // tr)) * tr, tr), tr)
        m = pl.ds(pl.multiple_of((index % wide) * tc, tc), tc)
        k0 = (index // (wide * (rows // tr))) * kg
        us, vs = [None] * kg, [None] * kg
        for q in range(0, count, 4):
            pu, pv = [None] * kg, [None] * kg
            for p in (q, q + 2):
                c = [c_ref[p + i, r, m] for i in range(2)]
                for k in range(kg):
                    slot = [slots[(k0 + k) * count + p + i] for i in range(2)]
                    u = c[0] * d_ref[slot[0], 0, r, m] + c[1] * d_ref[slot[1], 0, r, m]
                    v = c[0] * d_ref[slot[0], 1, r, m] + c[1] * d_ref[slot[1], 1, r, m]
                    pu[k] = u if p == q else pu[k] + u
                    pv[k] = v if p == q else pv[k] + v
            for k in range(kg):
                us[k] = pu[k] if q == 0 else us[k] + pu[k]
                vs[k] = pv[k] if q == 0 else vs[k] + pv[k]
        for k in range(kg):
            out_ref[k0 + k, 0, 0, r, m] = us[k]
            out_ref[k0 + k, 0, 1, r, m] = vs[k]
        return 0

    lax.fori_loop(0, wide * (rows // tr) * (count // kg), tile, 0)


def own_rows(mine, slots, pieces, coupling, energy, le, held):
    each, n, _ = pieces[0].shape
    count, rows, _ = coupling.shape
    cols = n // 2
    alias = [] if held is None else [held]
    in_specs = (
        [pl.BlockSpec((each, rows, cols), lambda t, mine, slots: (0, mine[0], t))] * len(pieces)
        + [pl.BlockSpec((each, cols, rows), lambda t, mine, slots: (0, t, mine[0]))] * len(pieces)
        + [pl.BlockSpec((count, rows, cols), lambda t, mine, slots: (0, 0, t))]
        + [pl.BlockSpec(memory_space=pl.ANY)] * len(alias)
    )
    return pl.pallas_call(
        functools.partial(rows_kernel, len(pieces)),
        out_shape=jax.ShapeDtypeStruct((count, le, 2, rows, n), BF16),
        grid_spec=pltpu.PrefetchScalarGridSpec(
            num_scalar_prefetch=2,
            grid=(n // cols,),
            in_specs=in_specs,
            out_specs=pl.BlockSpec((count, 1, 2, rows, cols), lambda t, mine, slots: (0, energy, 0, 0, t)),
            scratch_shapes=[pltpu.VMEM((count, 2, rows, cols), BF16)],
        ),
        input_output_aliases={2 + len(in_specs) - 1: 0} if alias else {},
        compiler_params=params(56),
        cost_estimate=cost(4 * count * count * rows * n, rows * n * count * 10),
        name="rows",
    )(mine[None], slots, *pieces, *pieces, coupling, *alias)


def density_terms(energy, g_ref, gamma_ref, x_ref, y_ref):
    n = g_ref.shape[-1]
    gamma = gamma_ref[0, energy:energy + 1, :]
    g_re, g_im = g_ref[0, 0, 0], g_ref[0, 0, 1]
    row, col = row_col(n, n)
    x, yt = x_ref[0].astype(F32), y_ref[0].astype(F32).T
    s_re = jnp.where(col >= row, x, yt).astype(BF16)
    s_im = jnp.where(col < row, x, jnp.where(col > row, -yt, 0.0)).astype(BF16)
    scaled_re = (g_re.astype(F32) * gamma).astype(BF16).astype(F32)
    scaled_im = (g_im.astype(F32) * gamma).astype(BF16).astype(F32)
    m_re = (dot_nn(g_re, s_re) - dot_nn(g_im, s_im) + scaled_re).astype(BF16)
    m_im = (dot_nn(g_re, s_im) + dot_nn(g_im, s_re) + scaled_im).astype(BF16)
    return dot_nt(m_re, g_re) + dot_nt(m_im, g_im), dot_nt(m_im, g_re) - dot_nt(m_re, g_im)


def first_density_kernel(energy, first, g_ref, gamma_ref, x_ref, y_ref, *refs):
    for c, d in enumerate(density_terms(energy, g_ref, gamma_ref, x_ref, y_ref)):
        refs[-1][0, c] = d if first else d + refs[0][0, c]


def first_density(energy, green, broadening, x, y, held):
    lk, le, _, n, _ = green.shape
    alias = [] if held is None else [held]
    pair = pl.BlockSpec((1, 2, n, n), lambda k: (k, 0, 0, 0))
    one = pl.BlockSpec((1, n, n), lambda k: (k, 0, 0))
    return pl.pallas_call(
        functools.partial(first_density_kernel, energy, held is None),
        out_shape=pltpu.HBM((lk, 2, n, n), F32),
        grid=(lk,),
        in_specs=[
            pl.BlockSpec((1, 1, 2, n, n), lambda k: (k, energy, 0, 0, 0)),
            pl.BlockSpec((1, le, n), lambda k: (k, 0, 0)),
            one,
            one,
        ] + [pair] * len(alias),
        out_specs=pair,
        compiler_params=params(44),
        cost_estimate=cost(16 * lk * n**3, lk * n * n * 20),
        name="density",
    )(green, broadening, x, y, *alias)


def last_density_kernel(scale, energy, odd, g_ref, gamma_ref, x_ref, y_ref, held_ref, *refs):
    d_ref, outs = refs[-1], refs[:-1]
    groups, _, rows, _ = outs[0].shape
    for c, d in enumerate(density_terms(energy, g_ref, gamma_ref, x_ref, y_ref)):
        d_ref[c] = (d + held_ref[0, c]) * scale
    for i in range(len(outs) // 2):
        keep_ref, send_ref = outs[2 * i], outs[2 * i + 1]

        @pl.when(pl.program_id(0) == i)
        def _():
            for c in range(2):
                for g in range(groups):
                    mine = pl.multiple_of((2 * g + odd[0]) * rows, rows)
                    other = pl.multiple_of((2 * g + 1 - odd[0]) * rows, rows)
                    keep_ref[g, c] = d_ref[c, pl.ds(mine, rows), :].astype(BF16)
                    send_ref[g, c] = d_ref[c, pl.ds(other, rows), :].astype(BF16)


def last_density(scale, energy, start, count, groups, odd, green, broadening, x, y, held):
    _, le, _, n, _ = green.shape
    rows = n // (2 * groups)
    one = pl.BlockSpec((1, n, n), lambda i, odd: (start + i, 0, 0))
    out = pl.BlockSpec((groups, 2, rows, n), lambda i, odd: (0, 0, 0, 0))
    return pl.pallas_call(
        functools.partial(last_density_kernel, scale, energy),
        out_shape=[jax.ShapeDtypeStruct((groups, 2, rows, n), BF16)] * (2 * count),
        grid_spec=pltpu.PrefetchScalarGridSpec(
            num_scalar_prefetch=1,
            grid=(count,),
            in_specs=[
                pl.BlockSpec((1, 1, 2, n, n), lambda i, odd: (start + i, energy, 0, 0, 0)),
                pl.BlockSpec((1, le, n), lambda i, odd: (start + i, 0, 0)),
                one,
                one,
                pl.BlockSpec((1, 2, n, n), lambda i, odd: (start + i, 0, 0, 0)),
            ],
            out_specs=[out] * (2 * count),
            scratch_shapes=[pltpu.VMEM((2, n, n), F32)],
        ),
        compiler_params=params(44),
        cost_estimate=cost(count * 16 * n**3, count * n * n * 20),
        name="density",
    )(odd[None], green, broadening, x, y, held)


def pair_sum_kernel(group, keep_ref, recv_ref, *outs):
    groups = len(outs)
    for d in range(groups):
        at = lax.rem(group[0] + d, groups)
        outs[d][...] = (keep_ref[at].astype(F32) + recv_ref[at].astype(F32)).astype(BF16)


def pair_sum(group, keep, recv):
    groups = keep.shape[0]
    vmem = pl.BlockSpec(memory_space=pltpu.VMEM)
    return pl.pallas_call(
        pair_sum_kernel,
        out_shape=[jax.ShapeDtypeStruct(keep.shape[1:], BF16)] * groups,
        in_specs=[pl.BlockSpec(memory_space=pltpu.SMEM), vmem, vmem],
        out_specs=[vmem] * groups,
        compiler_params=params(16),
        cost_estimate=cost(keep.size, keep.size * 6),
        name="pairsum",
    )(group[None], keep, recv)


def staged(green_ret, broadening, coupling, shift_steps, mode_weight, occupation, momentum_map):
    lk, le, _, _, _ = green_ret.shape
    ne, nm = lax.axis_size("energy"), lax.axis_size("mom")
    if le != SHIFT_MAX or lk % 2 or ne % 2 or nm & (nm - 1):
        raise ValueError("unsupported sizes")
    hk, groups = lk // 2, ne // 2
    me, mine = lax.axis_index("energy").astype(jnp.int32), lax.axis_index("mom").astype(jnp.int32)
    odd, group = me & 1, me >> 1
    pairs = [(i, i ^ 1) for i in range(ne)]
    away = [(i, i + (2 if i % 2 else -2)) for i in range(ne) if 0 <= i + (2 if i % 2 else -2) < ne]
    across = [(i, i + (-2 if i % 2 else 2)) for i in range(ne) if 0 <= i + (-2 if i % 2 else 2) < ne]
    strides = []
    while (nm >> (len(strides) + 1)) > 0:
        strides.append(nm >> (len(strides) + 1))

    def permuted(x, perm):
        return lax.ppermute(x, "energy", perm)

    def over_energy(x, perm):
        return hbm(permuted(x, perm))

    def swap(x, stride):
        moved = lax.ppermute(x, "mom", [(i, i ^ stride) for i in range(nm)])
        return hbm(moved)

    def spread(x):
        held = [x]
        for s in strides:
            held = held + [swap(piece, s) for piece in held]
        return held

    order = [0]
    for s in strides:
        order = order + [o ^ s for o in order]

    weights = []
    for s in range(1, SHIFT_MAX + 1):
        held = shift_steps == s
        weights.append(jnp.sum(jnp.where(held, mode_weight * (occupation + 1.0), 0.0)))
        weights.append(jnp.sum(jnp.where(held, mode_weight * occupation, 0.0)))
    weights = jnp.stack(weights)

    owner, inner = momentum_map // lk, momentum_map % lk
    place = jnp.zeros_like(owner)
    for at, o in enumerate(order):
        place = jnp.where((owner ^ mine) == o, at, place)
    slots = (place * lk + ((inner // hk) ^ odd) * hk + inner % hk).astype(jnp.int32)
    own_slots = lax.dynamic_slice_in_dim(slots, mine * lk, lk, 0).reshape(-1)
    all_slots = slots.reshape(-1)

    green_ret = hbm(green_ret)
    coupling = hbm(coupling)
    coupling_pieces = spread(coupling)

    send = [lesser_packed((1 - odd) * hk + j, green_ret, broadening) for j in range(hk)]
    recv = [[over_energy(send[j][h], pairs) for h in range(2)] for j in range(hk)]
    keep = [lesser_packed(odd * hk + j, green_ret, broadening) for j in range(hk)]
    kz = [[over_energy(keep[j][h], away) for h in range(2)] for j in range(hk)]
    rz = [[over_energy(recv[j][h], across) for h in range(2)] for j in range(hk)]
    got, last = [], None
    for j in range(hk):
        for h in range(2):
            last = sources(
                odd, weights, j, h, hk, keep[j][h], recv[j][h], kz[j][h], rz[j][h], last)
        got.append(last)

    full, turned = place_coupling(jnp.stack([mine ^ o for o in order]), coupling_pieces)

    held_rows, held_density = None, None
    scale = 1.0 / (le * ne)
    late = []
    for e in range(le):
        use = [got[j] for j in range(hk)] if e == 0 else [last]
        fresh = [spread(part[e]) for part in use]
        back = [spread(over_energy(part[le + e], pairs)) for part in use]
        pieces = [part[at] for at in range(nm) for part in fresh + back]
        if e < le - 1:
            x, y = home_blocks(own_slots, pieces, full, turned, lk)
            held_density = first_density(e, green_ret, broadening, x, y, held_density)
        else:
            shares = []
            x, y = home_blocks(own_slots, pieces, full, turned, lk)
            for first, count in ((0, 1), (1, lk - 1)):
                shares = shares + list(last_density(
                    scale, e, first, count, groups, odd,
                    green_ret, broadening, x, y, held_density))
            for k in range(lk):
                kept, sent = shares[2 * k], shares[2 * k + 1]
                other = permuted(sent, pairs)
                parts = pair_sum(group, kept, other)
                total = parts[0].astype(F32)
                for d in range(1, groups):
                    perm = [(i, (i + 2 * d) % ne) for i in range(ne)]
                    total = total + permuted(parts[d], perm).astype(F32)
                late.append(total)
        held_rows = own_rows(mine, all_slots, pieces, coupling, e, le, held_rows)
    density = jnp.transpose(jnp.stack(late), (2, 0, 1, 3))
    return held_rows, density


def solution(mesh):
    return jax.shard_map(
        staged,
        mesh=mesh,
        in_specs=(
            P("mom", "energy", None, None, None),
            P("mom", "energy", None),
            P(None, "mom", None),
            P(),
            P(),
            P(),
            P(),
        ),
        out_specs=(P(None, "energy", None, "mom", None), P("energy", "mom", None, None)),
        check_vma=False,
    )
```

```python
import functools

import jax
import jax.numpy as jnp
from jax import lax
from jax.experimental import pallas as pl
from jax.experimental.pallas import tpu as pltpu
from jax.sharding import PartitionSpec as P


SHIFT_MAX = 2
F32 = jnp.float32
BF16 = jnp.bfloat16


def params(mib):
    return pltpu.CompilerParams(vmem_limit_bytes=mib * 1024 * 1024)


def hbm(x):
    return pltpu.with_memory_space_constraint(x, pltpu.HBM)


def cost(flops, nbytes):
    return pl.CostEstimate(flops=int(flops), bytes_accessed=int(nbytes), transcendentals=0)


def dot_nt(a, b):
    return lax.dot_general(a, b, (((1,), (1,)), ((), ())), preferred_element_type=F32)


def dot_nn(a, b):
    return lax.dot_general(a, b, (((1,), (0,)), ((), ())), preferred_element_type=F32)


def row_col(rows, cols):
    return lax.broadcasted_iota(jnp.int32, (rows, cols), 0), lax.broadcasted_iota(jnp.int32, (rows, cols), 1)


def lesser_kernel(sel, g_ref, gamma_ref, *outs):
    n = g_ref.shape[-1]
    half = n // 2
    e = pl.program_id(0)
    gamma = gamma_ref[0, pl.ds(e, 1), :]
    g_re, g_im = g_ref[0, 0, 0], g_ref[0, 0, 1]
    s_re = (g_re.astype(F32) * gamma).astype(BF16)
    s_im = (g_im.astype(F32) * gamma).astype(BF16)
    row, col = row_col(half, half)

    def real(i, j):
        i, j = slice(i * half, (i + 1) * half), slice(j * half, (j + 1) * half)
        return dot_nt(s_re[i], g_re[j]) + dot_nt(s_im[i], g_im[j])

    def imag(i, j):
        i, j = slice(i * half, (i + 1) * half), slice(j * half, (j + 1) * half)
        return dot_nt(s_im[i], g_re[j]) - dot_nt(s_re[i], g_im[j])

    for d in range(2):
        outs[d][0, :, d * half:(d + 1) * half] = jnp.where(col >= row, real(d, d), imag(d, d)).astype(BF16)
    outs[0][0, :, half:] = real(0, 1).astype(BF16)
    outs[1][0, :, :half] = imag(1, 0).astype(BF16)


def lesser_packed(which, green, broadening):
    _, le, _, n, _ = green.shape
    return pl.pallas_call(
        lesser_kernel,
        out_shape=[pltpu.HBM((le, n // 2, n), BF16)] * 2,
        grid_spec=pltpu.PrefetchScalarGridSpec(
            num_scalar_prefetch=1,
            grid=(le,),
            in_specs=[
                pl.BlockSpec((1, 1, 2, n, n), lambda e, sel: (sel[0], e, 0, 0, 0)),
                pl.BlockSpec((1, le, n), lambda e, sel: (sel[0], 0, 0)),
            ],
            out_specs=[pl.BlockSpec((1, n // 2, n), lambda e, sel: (e, 0, 0))] * 2,
        ),
        compiler_params=params(56),
        cost_estimate=cost(le * 6 * n**3, le * n * n * 6),
        name="lesser",
    )(which[None], green, broadening)


def place_kernel(where, *refs):
    pieces, (full_ref, turned_ref) = refs[:-2], refs[-2:]
    rows = pieces[0].shape[1]
    for at, c_ref in enumerate(pieces):
        start = pl.ds(pl.multiple_of(where[at] * rows, rows), rows)
        for q in range(c_ref.shape[0]):
            full_ref[q, start, :] = c_ref[q]
            turned_ref[q, :, start] = c_ref[q].T


def place_coupling(where, pieces):
    nk, rows, n = pieces[0].shape
    each = 2
    return pl.pallas_call(
        place_kernel,
        out_shape=[pltpu.HBM((nk, n, n), BF16)] * 2,
        grid_spec=pltpu.PrefetchScalarGridSpec(
            num_scalar_prefetch=1,
            grid=(nk // each,),
            in_specs=[pl.BlockSpec((each, rows, n), lambda q, w: (q, 0, 0))] * len(pieces),
            out_specs=[pl.BlockSpec((each, n, n), lambda q, w: (q, 0, 0))] * 2,
        ),
        compiler_params=params(56),
        cost_estimate=cost(nk * n * n * 4, nk * n * n * 6),
        name="place",
    )(where, *pieces)


def source_kernel(odd, steps, strength, boson, keep, recv, kz, rz, *refs):
    le = keep.shape[0]
    weights = []
    for s in range(1, SHIFT_MAX + 1):
        up, down = jnp.float32(0), jnp.float32(0)
        for m in range(steps.shape[0]):
            held = jnp.where(steps[m] == s, strength[m], 0.0)
            up, down = up + held * (boson[m] + 1.0), down + held * boson[m]
        weights = weights + [up, down]
    outs = refs[-2 * le:]

    def emit(order):
        line = [(ref, e) for ref in order for e in range(le)]
        for e in range(le):
            for ref, target in ((keep, outs[e]), (recv, outs[le + e])):
                at = [i for i, held in enumerate(order) if held is ref][0] * le + e
                total = None
                for s in range(1, SHIFT_MAX + 1):
                    for j, sign in ((0, s), (1, -s)):
                        source, index = line[at + sign]
                        term = weights[2 * (s - 1) + j] * source[index].astype(F32)
                        total = term if total is None else total + term
                target[0] = total.astype(BF16)

    @pl.when(odd[0] == 0)
    def _():
        emit((rz, keep, recv, kz))

    @pl.when(odd[0] == 1)
    def _():
        emit((kz, recv, keep, rz))


def sources(odd, modes, j, h, hk, keep, recv, kz, rz, held):
    le, half, n = keep.shape
    rows = half // 2
    at = h * (half // rows)
    big = pl.BlockSpec((le, rows, n), lambda r, *_: (0, r, 0))
    first = pl.BlockSpec((1, rows, n), lambda r, *_: (0, at + r, 0))
    later = pl.BlockSpec((1, rows, n), lambda r, *_: (j, at + r, 0))
    shapes = [(1 if e == 0 else hk, n, n) for e in range(le)] * 2
    specs = [first if e == 0 else later for e in range(le)] * 2
    alias, extra = {}, []
    if held is not None:
        for i, value in enumerate(held):
            if i % le or h:
                alias[5 + len(modes) + len(extra)] = i
                extra.append(value)
    return pl.pallas_call(
        source_kernel,
        out_shape=[pltpu.HBM(shape, BF16) for shape in shapes],
        grid_spec=pltpu.PrefetchScalarGridSpec(
            num_scalar_prefetch=1 + len(modes),
            grid=(half // rows,),
            in_specs=[big] * 4 + [pl.BlockSpec(memory_space=pl.ANY)] * len(extra),
            out_specs=specs,
        ),
        input_output_aliases=alias,
        compiler_params=params(16),
        cost_estimate=cost(le * half * n * 16, le * half * n * 12),
        name="source",
    )(odd[None], *modes, keep, recv, kz, rz, *extra)


def home_kernel(lk, pieces, mine, slots, *refs):
    first = mine[0] * lk
    ins, (c_ref, ct_ref, x_ref, y_ref, q_ref) = refs[:pieces], refs[pieces:]
    each, rows, n = ins[0].shape
    count = pieces * each
    for s in range(pieces):
        for j in range(each):
            q_ref[s * each + j] = ins[s][j]
    tr, tc = 16, 256

    def tile(index, _):
        r = pl.ds(pl.multiple_of((index // (n // tc)) * tr, tr), tr)
        m = pl.ds(pl.multiple_of((index % (n // tc)) * tc, tc), tc)
        xs, ys = [None] * lk, [None] * lk
        for q in range(0, count, 4):
            px, py = [None] * lk, [None] * lk
            for p in (q, q + 2):
                c, ct = [c_ref[p + i, r, m] for i in range(2)], [ct_ref[p + i, r, m] for i in range(2)]
                for k in range(lk):
                    v = [q_ref[slots[first + k, p + i], r, m] for i in range(2)]
                    x, y = c[0] * v[0] + c[1] * v[1], ct[0] * v[0] + ct[1] * v[1]
                    px[k] = x if p == q else px[k] + x
                    py[k] = y if p == q else py[k] + y
            for k in range(lk):
                xs[k] = px[k] if q == 0 else xs[k] + px[k]
                ys[k] = py[k] if q == 0 else ys[k] + py[k]
        for k in range(lk):
            x_ref[k, r, m] = xs[k]
            y_ref[k, r, m] = ys[k]
        return 0

    lax.fori_loop(0, (rows // tr) * (n // tc), tile, 0)


def home_blocks(mine, slots, pieces, full, turned, lk):
    each, n, _ = pieces[0].shape
    count = each * len(pieces)
    rows = n // 4
    block = lambda lead: pl.BlockSpec((lead, rows, n), lambda g, *_: (0, g, 0))
    return pl.pallas_call(
        functools.partial(home_kernel, lk, len(pieces)),
        out_shape=[pltpu.VMEM((lk, n, n), BF16)] * 2,
        grid_spec=pltpu.PrefetchScalarGridSpec(
            num_scalar_prefetch=2,
            grid=(n // rows,),
            in_specs=[block(each)] * len(pieces) + [block(count), block(count)],
            out_specs=[block(lk), block(lk)],
            scratch_shapes=[pltpu.VMEM((count, rows, n), BF16)],
        ),
        compiler_params=params(44),
        cost_estimate=cost(4 * lk * count * n * n, n * n * (6 * count + 4 * lk)),
        name="home",
    )(mine[None], slots, *pieces, full, turned)


def rows_kernel(pieces, mine, slots, *refs):
    a_refs, b_refs, refs = refs[:pieces], refs[pieces:2 * pieces], refs[2 * pieces:]
    c_ref, out_ref, d_ref = (refs[0],) + refs[-2:]
    each, rows, cols = a_refs[0].shape
    count = pieces * each
    row, col = row_col(rows, cols)
    above = (col - row) + (pl.program_id(0) * cols - mine[0] * rows)
    for s in range(pieces):
        for j in range(each):
            a, b = a_refs[s][j].astype(F32), b_refs[s][j].astype(F32).T
            d_ref[s * each + j, 0] = jnp.where(above >= 0, a, b).astype(BF16)
            d_ref[s * each + j, 1] = jnp.where(above < 0, a, jnp.where(above > 0, -b, 0.0)).astype(BF16)
    tr, kg, tc = 32, 2, 256
    wide = cols // tc

    def tile(index, _):
        r = pl.ds(pl.multiple_of(((index // wide) % (rows // tr)) * tr, tr), tr)
        m = pl.ds(pl.multiple_of((index % wide) * tc, tc), tc)
        k0 = (index // (wide * (rows // tr))) * kg
        us, vs = [None] * kg, [None] * kg
        for q in range(0, count, 4):
            pu, pv = [None] * kg, [None] * kg
            for p in (q, q + 2):
                c = [c_ref[p + i, r, m] for i in range(2)]
                for k in range(kg):
                    slot = [slots[k0 + k, p + i] for i in range(2)]
                    u = c[0] * d_ref[slot[0], 0, r, m] + c[1] * d_ref[slot[1], 0, r, m]
                    v = c[0] * d_ref[slot[0], 1, r, m] + c[1] * d_ref[slot[1], 1, r, m]
                    pu[k] = u if p == q else pu[k] + u
                    pv[k] = v if p == q else pv[k] + v
            for k in range(kg):
                us[k] = pu[k] if q == 0 else us[k] + pu[k]
                vs[k] = pv[k] if q == 0 else vs[k] + pv[k]
        for k in range(kg):
            out_ref[k0 + k, 0, 0, r, m] = us[k]
            out_ref[k0 + k, 0, 1, r, m] = vs[k]
        return 0

    lax.fori_loop(0, wide * (rows // tr) * (count // kg), tile, 0)


def own_rows(mine, slots, pieces, coupling, energy, le, held):
    each, n, _ = pieces[0].shape
    count, rows, _ = coupling.shape
    cols = n // 2
    alias = [] if held is None else [held]
    in_specs = (
        [pl.BlockSpec((each, rows, cols), lambda t, mine, slots: (0, mine[0], t))] * len(pieces)
        + [pl.BlockSpec((each, cols, rows), lambda t, mine, slots: (0, t, mine[0]))] * len(pieces)
        + [pl.BlockSpec((count, rows, cols), lambda t, mine, slots: (0, 0, t))]
        + [pl.BlockSpec(memory_space=pl.ANY)] * len(alias)
    )
    return pl.pallas_call(
        functools.partial(rows_kernel, len(pieces)),
        out_shape=jax.ShapeDtypeStruct((count, le, 2, rows, n), BF16),
        grid_spec=pltpu.PrefetchScalarGridSpec(
            num_scalar_prefetch=2,
            grid=(n // cols,),
            in_specs=in_specs,
            out_specs=pl.BlockSpec((count, 1, 2, rows, cols), lambda t, mine, slots: (0, energy, 0, 0, t)),
            scratch_shapes=[pltpu.VMEM((count, 2, rows, cols), BF16)],
        ),
        input_output_aliases={2 + len(in_specs) - 1: 0} if alias else {},
        compiler_params=params(56),
        cost_estimate=cost(4 * count * count * rows * n, rows * n * count * 10),
        name="rows",
    )(mine[None], slots, *pieces, *pieces, coupling, *alias)


def density_terms(energy, g_ref, gamma_ref, x_ref, y_ref):
    n = g_ref.shape[-1]
    gamma = gamma_ref[0, energy:energy + 1, :]
    g_re, g_im = g_ref[0, 0, 0], g_ref[0, 0, 1]
    row, col = row_col(n, n)
    x, yt = x_ref[0].astype(F32), y_ref[0].astype(F32).T
    s_re = jnp.where(col >= row, x, yt).astype(BF16)
    s_im = jnp.where(col < row, x, jnp.where(col > row, -yt, 0.0)).astype(BF16)
    scaled_re = (g_re.astype(F32) * gamma).astype(BF16).astype(F32)
    scaled_im = (g_im.astype(F32) * gamma).astype(BF16).astype(F32)
    m_re = (dot_nn(g_re, s_re) - dot_nn(g_im, s_im) + scaled_re).astype(BF16)
    m_im = (dot_nn(g_re, s_im) + dot_nn(g_im, s_re) + scaled_im).astype(BF16)
    return dot_nt(m_re, g_re) + dot_nt(m_im, g_im), dot_nt(m_im, g_re) - dot_nt(m_re, g_im)


def first_density_kernel(energy, first, g_ref, gamma_ref, x_ref, y_ref, *refs):
    for c, d in enumerate(density_terms(energy, g_ref, gamma_ref, x_ref, y_ref)):
        refs[-1][0, c] = d if first else d + refs[0][0, c]


def first_density(energy, green, broadening, x, y, held):
    lk, le, _, n, _ = green.shape
    alias = [] if held is None else [held]
    pair = pl.BlockSpec((1, 2, n, n), lambda k: (k, 0, 0, 0))
    one = pl.BlockSpec((1, n, n), lambda k: (k, 0, 0))
    return pl.pallas_call(
        functools.partial(first_density_kernel, energy, held is None),
        out_shape=pltpu.HBM((lk, 2, n, n), F32),
        grid=(lk,),
        in_specs=[
            pl.BlockSpec((1, 1, 2, n, n), lambda k: (k, energy, 0, 0, 0)),
            pl.BlockSpec((1, le, n), lambda k: (k, 0, 0)),
            one,
            one,
        ] + [pair] * len(alias),
        out_specs=pair,
        compiler_params=params(44),
        cost_estimate=cost(16 * lk * n**3, lk * n * n * 20),
        name="density",
    )(green, broadening, x, y, *alias)


def last_density_kernel(scale, energy, odd, g_ref, gamma_ref, x_ref, y_ref, held_ref, *refs):
    d_ref, outs = refs[-1], refs[:-1]
    groups, _, rows, _ = outs[0].shape
    for c, d in enumerate(density_terms(energy, g_ref, gamma_ref, x_ref, y_ref)):
        d_ref[c] = (d + held_ref[0, c]) * scale
    for i in range(len(outs) // 2):
        keep_ref, send_ref = outs[2 * i], outs[2 * i + 1]

        @pl.when(pl.program_id(0) == i)
        def _():
            for c in range(2):
                for g in range(groups):
                    mine = pl.multiple_of((2 * g + odd[0]) * rows, rows)
                    other = pl.multiple_of((2 * g + 1 - odd[0]) * rows, rows)
                    keep_ref[g, c] = d_ref[c, pl.ds(mine, rows), :].astype(BF16)
                    send_ref[g, c] = d_ref[c, pl.ds(other, rows), :].astype(BF16)


def last_density(scale, energy, start, count, groups, odd, green, broadening, x, y, held):
    _, le, _, n, _ = green.shape
    rows = n // (2 * groups)
    one = pl.BlockSpec((1, n, n), lambda i, odd: (start + i, 0, 0))
    out = pl.BlockSpec((groups, 2, rows, n), lambda i, odd: (0, 0, 0, 0))
    return pl.pallas_call(
        functools.partial(last_density_kernel, scale, energy),
        out_shape=[jax.ShapeDtypeStruct((groups, 2, rows, n), BF16)] * (2 * count),
        grid_spec=pltpu.PrefetchScalarGridSpec(
            num_scalar_prefetch=1,
            grid=(count,),
            in_specs=[
                pl.BlockSpec((1, 1, 2, n, n), lambda i, odd: (start + i, energy, 0, 0, 0)),
                pl.BlockSpec((1, le, n), lambda i, odd: (start + i, 0, 0)),
                one,
                one,
                pl.BlockSpec((1, 2, n, n), lambda i, odd: (start + i, 0, 0, 0)),
            ],
            out_specs=[out] * (2 * count),
            scratch_shapes=[pltpu.VMEM((2, n, n), F32)],
        ),
        compiler_params=params(44),
        cost_estimate=cost(count * 16 * n**3, count * n * n * 20),
        name="density",
    )(odd[None], green, broadening, x, y, held)


def pair_sum_kernel(group, keep_ref, recv_ref, *outs):
    groups = len(outs)
    for d in range(groups):
        at = lax.rem(group[0] + d, groups)
        outs[d][...] = (keep_ref[at].astype(F32) + recv_ref[at].astype(F32)).astype(BF16)


def pair_sum(group, keep, recv):
    groups = keep.shape[0]
    vmem = pl.BlockSpec(memory_space=pltpu.VMEM)
    return pl.pallas_call(
        pair_sum_kernel,
        out_shape=[jax.ShapeDtypeStruct(keep.shape[1:], BF16)] * groups,
        in_specs=[pl.BlockSpec(memory_space=pltpu.SMEM), vmem, vmem],
        out_specs=[vmem] * groups,
        compiler_params=params(16),
        cost_estimate=cost(keep.size, keep.size * 6),
        name="pairsum",
    )(group[None], keep, recv)


def staged(green_ret, broadening, coupling, shift_steps, mode_weight, occupation, momentum_map):
    lk, le, _, _, _ = green_ret.shape
    ne, nm = lax.axis_size("energy"), lax.axis_size("mom")
    if le != SHIFT_MAX or lk % 2 or ne % 2 or nm & (nm - 1):
        raise ValueError("unsupported sizes")
    hk, groups = lk // 2, ne // 2
    me, mine = lax.axis_index("energy").astype(jnp.int32), lax.axis_index("mom").astype(jnp.int32)
    odd, group = me & 1, me >> 1
    pairs = [(i, i ^ 1) for i in range(ne)]
    away = [(i, i + (2 if i % 2 else -2)) for i in range(ne) if 0 <= i + (2 if i % 2 else -2) < ne]
    across = [(i, i + (-2 if i % 2 else 2)) for i in range(ne) if 0 <= i + (-2 if i % 2 else 2) < ne]
    strides = []
    while (nm >> (len(strides) + 1)) > 0:
        strides.append(nm >> (len(strides) + 1))

    def permuted(x, perm):
        return lax.ppermute(x, "energy", perm)

    def over_energy(x, perm):
        return hbm(permuted(x, perm))

    def swap(x, stride):
        moved = lax.ppermute(x, "mom", [(i, i ^ stride) for i in range(nm)])
        return hbm(moved)

    def spread(x):
        held = [x]
        for s in strides:
            held = held + [swap(piece, s) for piece in held]
        return held

    order = [0]
    for s in strides:
        order = order + [o ^ s for o in order]

    modes = (shift_steps, mode_weight, occupation)

    owner, inner = momentum_map // lk, momentum_map % lk
    place = jnp.zeros_like(owner)
    for at, o in enumerate(order):
        place = jnp.where((owner ^ mine) == o, at, place)
    slots = (place * lk + ((inner // hk) ^ odd) * hk + inner % hk).astype(jnp.int32)

    green_ret = hbm(green_ret)
    coupling = hbm(coupling)
    coupling_pieces = spread(coupling)

    send = [lesser_packed((1 - odd) * hk + j, green_ret, broadening) for j in range(hk)]
    recv = [[over_energy(send[j][h], pairs) for h in range(2)] for j in range(hk)]
    keep = [lesser_packed(odd * hk + j, green_ret, broadening) for j in range(hk)]
    kz = [[permuted(keep[j][h], away) for h in range(2)] for j in range(hk)]
    rz = [[permuted(recv[j][h], across) for h in range(2)] for j in range(hk)]
    got, last = [], None
    for j in range(hk):
        for h in range(2):
            last = sources(
                odd, modes, j, h, hk, keep[j][h], recv[j][h], kz[j][h], rz[j][h], last)
        got.append(last)

    full, turned = place_coupling(jnp.stack([mine ^ o for o in order]), coupling_pieces)

    held_rows, held_density = None, None
    scale = 1.0 / (le * ne)
    late = []
    for e in range(le):
        use = [got[j] for j in range(hk)] if e == 0 else [last]
        fresh = [spread(part[e]) for part in use]
        back = [spread(over_energy(part[le + e], pairs)) for part in use]
        pieces = [part[at] for at in range(nm) for part in fresh + back]
        if e < le - 1:
            x, y = home_blocks(mine, slots, pieces, full, turned, lk)
            held_density = first_density(e, green_ret, broadening, x, y, held_density)
        else:
            shares = []
            x, y = home_blocks(mine, slots, pieces, full, turned, lk)
            for first, count in ((0, 1), (1, lk - 1)):
                shares = shares + list(last_density(
                    scale, e, first, count, groups, odd,
                    green_ret, broadening, x, y, held_density))
            for k in range(lk):
                kept, sent = shares[2 * k], shares[2 * k + 1]
                other = permuted(sent, pairs)
                parts = pair_sum(group, kept, other)
                total = parts[0].astype(F32)
                for d in range(1, groups):
                    perm = [(i, (i + 2 * d) % ne) for i in range(ne)]
                    total = total + permuted(parts[d], perm).astype(F32)
                late.append(total)
        held_rows = own_rows(mine, slots, pieces, coupling, e, le, held_rows)
    density = jnp.transpose(jnp.stack(late), (2, 0, 1, 3))
    return held_rows, density


def solution(mesh):
    return jax.shard_map(
        staged,
        mesh=mesh,
        in_specs=(
            P("mom", "energy", None, None, None),
            P("mom", "energy", None),
            P(None, "mom", None),
            P(),
            P(),
            P(),
            P(),
        ),
        out_specs=(P(None, "energy", None, "mom", None), P("energy", "mom", None, None)),
        check_vma=False,
    )
```

```python
import functools

import jax
import jax.numpy as jnp
from jax import lax
from jax.experimental import pallas as pl
from jax.experimental.pallas import tpu as pltpu
from jax.sharding import PartitionSpec as P


SHIFT_MAX = 2
F32 = jnp.float32
BF16 = jnp.bfloat16


def params(mib):
    return pltpu.CompilerParams(vmem_limit_bytes=mib * 1024 * 1024)


def hbm(x):
    return pltpu.with_memory_space_constraint(x, pltpu.HBM)


def cost(flops, nbytes):
    return pl.CostEstimate(flops=int(flops), bytes_accessed=int(nbytes), transcendentals=0)


def dot_nt(a, b):
    return lax.dot_general(a, b, (((1,), (1,)), ((), ())), preferred_element_type=F32)


def dot_nn(a, b):
    return lax.dot_general(a, b, (((1,), (0,)), ((), ())), preferred_element_type=F32)


def row_col(rows, cols):
    return lax.broadcasted_iota(jnp.int32, (rows, cols), 0), lax.broadcasted_iota(jnp.int32, (rows, cols), 1)


def lesser_kernel(sel, g_ref, gamma_ref, *outs):
    n = g_ref.shape[-1]
    half = n // 2
    e = pl.program_id(0)
    gamma = gamma_ref[0, pl.ds(e, 1), :]
    g_re, g_im = g_ref[0, 0, 0], g_ref[0, 0, 1]
    s_re = (g_re.astype(F32) * gamma).astype(BF16)
    s_im = (g_im.astype(F32) * gamma).astype(BF16)
    row, col = row_col(half, half)

    def real(i, j):
        i, j = slice(i * half, (i + 1) * half), slice(j * half, (j + 1) * half)
        return dot_nt(s_re[i], g_re[j]) + dot_nt(s_im[i], g_im[j])

    def imag(i, j):
        i, j = slice(i * half, (i + 1) * half), slice(j * half, (j + 1) * half)
        return dot_nt(s_im[i], g_re[j]) - dot_nt(s_re[i], g_im[j])

    for d in range(2):
        outs[d][0, :, d * half:(d + 1) * half] = jnp.where(col >= row, real(d, d), imag(d, d)).astype(BF16)
    outs[0][0, :, half:] = real(0, 1).astype(BF16)
    outs[1][0, :, :half] = imag(1, 0).astype(BF16)


def lesser_packed(which, green, broadening):
    _, le, _, n, _ = green.shape
    return pl.pallas_call(
        lesser_kernel,
        out_shape=[pltpu.HBM((le, n // 2, n), BF16)] * 2,
        grid_spec=pltpu.PrefetchScalarGridSpec(
            num_scalar_prefetch=1,
            grid=(le,),
            in_specs=[
                pl.BlockSpec((1, 1, 2, n, n), lambda e, sel: (sel[0], e, 0, 0, 0)),
                pl.BlockSpec((1, le, n), lambda e, sel: (sel[0], 0, 0)),
            ],
            out_specs=[pl.BlockSpec((1, n // 2, n), lambda e, sel: (e, 0, 0))] * 2,
        ),
        compiler_params=params(56),
        cost_estimate=cost(le * 6 * n**3, le * n * n * 6),
        name="lesser",
    )(which[None], green, broadening)


def place_kernel(order, where, *refs):
    pieces, (full_ref, turned_ref) = refs[:-2], refs[-2:]
    rows = pieces[0].shape[1]
    for at, c_ref in enumerate(pieces):
        start = pl.ds(pl.multiple_of((where[0] ^ order[at]) * rows, rows), rows)
        for q in range(c_ref.shape[0]):
            full_ref[q, start, :] = c_ref[q]
            turned_ref[q, :, start] = c_ref[q].T


def place_coupling(where, order, pieces):
    nk, rows, n = pieces[0].shape
    each = 2
    return pl.pallas_call(
        functools.partial(place_kernel, order),
        out_shape=[pltpu.HBM((nk, n, n), BF16)] * 2,
        grid_spec=pltpu.PrefetchScalarGridSpec(
            num_scalar_prefetch=1,
            grid=(nk // each,),
            in_specs=[pl.BlockSpec((each, rows, n), lambda q, w: (q, 0, 0))] * len(pieces),
            out_specs=[pl.BlockSpec((each, n, n), lambda q, w: (q, 0, 0))] * 2,
        ),
        compiler_params=params(56),
        cost_estimate=cost(nk * n * n * 4, nk * n * n * 6),
        name="place",
    )(where[None], *pieces)


def source_kernel(odd, steps, strength, boson, keep, recv, kz, rz, *refs):
    le = keep.shape[0]
    weights = []
    for s in range(1, SHIFT_MAX + 1):
        up, down = jnp.float32(0), jnp.float32(0)
        for m in range(steps.shape[0]):
            held = jnp.where(steps[m] == s, strength[m], 0.0)
            up, down = up + held * (boson[m] + 1.0), down + held * boson[m]
        weights = weights + [up, down]
    outs = refs[-2 * le:]

    def emit(order):
        line = [(ref, e) for ref in order for e in range(le)]
        for e in range(le):
            for ref, target in ((keep, outs[e]), (recv, outs[le + e])):
                at = [i for i, held in enumerate(order) if held is ref][0] * le + e
                total = None
                for s in range(1, SHIFT_MAX + 1):
                    for j, sign in ((0, s), (1, -s)):
                        source, index = line[at + sign]
                        term = weights[2 * (s - 1) + j] * source[index].astype(F32)
                        total = term if total is None else total + term
                target[0] = total.astype(BF16)

    @pl.when(odd[0] == 0)
    def _():
        emit((rz, keep, recv, kz))

    @pl.when(odd[0] == 1)
    def _():
        emit((kz, recv, keep, rz))


def sources(odd, modes, j, h, hk, keep, recv, kz, rz, held):
    le, half, n = keep.shape
    rows = half // 2
    at = h * (half // rows)
    big = pl.BlockSpec((le, rows, n), lambda r, *_: (0, r, 0))
    first = pl.BlockSpec((1, rows, n), lambda r, *_: (0, at + r, 0))
    later = pl.BlockSpec((1, rows, n), lambda r, *_: (j, at + r, 0))
    shapes = [(1 if e == 0 else hk, n, n) for e in range(le)] * 2
    specs = [first if e == 0 else later for e in range(le)] * 2
    alias, extra = {}, []
    if held is not None:
        for i, value in enumerate(held):
            if i % le or h:
                alias[5 + len(modes) + len(extra)] = i
                extra.append(value)
    return pl.pallas_call(
        source_kernel,
        out_shape=[pltpu.HBM(shape, BF16) for shape in shapes],
        grid_spec=pltpu.PrefetchScalarGridSpec(
            num_scalar_prefetch=1 + len(modes),
            grid=(half // rows,),
            in_specs=[big] * 4 + [pl.BlockSpec(memory_space=pl.ANY)] * len(extra),
            out_specs=specs,
        ),
        input_output_aliases=alias,
        compiler_params=params(16),
        cost_estimate=cost(le * half * n * 16, le * half * n * 12),
        name="source",
    )(odd[None], *modes, keep, recv, kz, rz, *extra)


def home_kernel(lk, pieces, mine, slots, *refs):
    first = mine[0] * lk
    ins, (c_ref, ct_ref, x_ref, y_ref, q_ref) = refs[:pieces], refs[pieces:]
    each, rows, n = ins[0].shape
    count = pieces * each
    for s in range(pieces):
        for j in range(each):
            q_ref[s * each + j] = ins[s][j]
    tr, tc = 16, 256

    def tile(index, _):
        r = pl.ds(pl.multiple_of((index // (n // tc)) * tr, tr), tr)
        m = pl.ds(pl.multiple_of((index % (n // tc)) * tc, tc), tc)
        xs, ys = [None] * lk, [None] * lk
        for q in range(0, count, 4):
            px, py = [None] * lk, [None] * lk
            for p in (q, q + 2):
                c, ct = [c_ref[p + i, r, m] for i in range(2)], [ct_ref[p + i, r, m] for i in range(2)]
                for k in range(lk):
                    v = [q_ref[slots[first + k, p + i], r, m] for i in range(2)]
                    x, y = c[0] * v[0] + c[1] * v[1], ct[0] * v[0] + ct[1] * v[1]
                    px[k] = x if p == q else px[k] + x
                    py[k] = y if p == q else py[k] + y
            for k in range(lk):
                xs[k] = px[k] if q == 0 else xs[k] + px[k]
                ys[k] = py[k] if q == 0 else ys[k] + py[k]
        for k in range(lk):
            x_ref[k, r, m] = xs[k]
            y_ref[k, r, m] = ys[k]
        return 0

    lax.fori_loop(0, (rows // tr) * (n // tc), tile, 0)


def home_blocks(mine, slots, pieces, full, turned, lk):
    each, n, _ = pieces[0].shape
    count = each * len(pieces)
    rows = n // 4
    block = lambda lead: pl.BlockSpec((lead, rows, n), lambda g, *_: (0, g, 0))
    return pl.pallas_call(
        functools.partial(home_kernel, lk, len(pieces)),
        out_shape=[pltpu.VMEM((lk, n, n), BF16)] * 2,
        grid_spec=pltpu.PrefetchScalarGridSpec(
            num_scalar_prefetch=2,
            grid=(n // rows,),
            in_specs=[block(each)] * len(pieces) + [block(count), block(count)],
            out_specs=[block(lk), block(lk)],
            scratch_shapes=[pltpu.VMEM((count, rows, n), BF16)],
        ),
        compiler_params=params(44),
        cost_estimate=cost(4 * lk * count * n * n, n * n * (6 * count + 4 * lk)),
        name="home",
    )(mine[None], slots, *pieces, full, turned)


def rows_kernel(pieces, mine, slots, *refs):
    a_refs, b_refs, refs = refs[:pieces], refs[pieces:2 * pieces], refs[2 * pieces:]
    c_ref, out_ref, d_ref = (refs[0],) + refs[-2:]
    each, rows, cols = a_refs[0].shape
    count = pieces * each
    row, col = row_col(rows, cols)
    above = (col - row) + (pl.program_id(0) * cols - mine[0] * rows)
    for s in range(pieces):
        for j in range(each):
            a, b = a_refs[s][j].astype(F32), b_refs[s][j].astype(F32).T
            d_ref[s * each + j, 0] = jnp.where(above >= 0, a, b).astype(BF16)
            d_ref[s * each + j, 1] = jnp.where(above < 0, a, jnp.where(above > 0, -b, 0.0)).astype(BF16)
    tr, kg, tc = 32, 2, 256
    wide = cols // tc

    def tile(index, _):
        r = pl.ds(pl.multiple_of(((index // wide) % (rows // tr)) * tr, tr), tr)
        m = pl.ds(pl.multiple_of((index % wide) * tc, tc), tc)
        k0 = (index // (wide * (rows // tr))) * kg
        us, vs = [None] * kg, [None] * kg
        for q in range(0, count, 4):
            pu, pv = [None] * kg, [None] * kg
            for p in (q, q + 2):
                c = [c_ref[p + i, r, m] for i in range(2)]
                for k in range(kg):
                    slot = [slots[k0 + k, p + i] for i in range(2)]
                    u = c[0] * d_ref[slot[0], 0, r, m] + c[1] * d_ref[slot[1], 0, r, m]
                    v = c[0] * d_ref[slot[0], 1, r, m] + c[1] * d_ref[slot[1], 1, r, m]
                    pu[k] = u if p == q else pu[k] + u
                    pv[k] = v if p == q else pv[k] + v
            for k in range(kg):
                us[k] = pu[k] if q == 0 else us[k] + pu[k]
                vs[k] = pv[k] if q == 0 else vs[k] + pv[k]
        for k in range(kg):
            out_ref[k0 + k, 0, 0, r, m] = us[k]
            out_ref[k0 + k, 0, 1, r, m] = vs[k]
        return 0

    lax.fori_loop(0, wide * (rows // tr) * (count // kg), tile, 0)


def own_rows(mine, slots, pieces, coupling, energy, le, held):
    each, n, _ = pieces[0].shape
    count, rows, _ = coupling.shape
    cols = n // 2
    alias = [] if held is None else [held]
    in_specs = (
        [pl.BlockSpec((each, rows, cols), lambda t, mine, slots: (0, mine[0], t))] * len(pieces)
        + [pl.BlockSpec((each, cols, rows), lambda t, mine, slots: (0, t, mine[0]))] * len(pieces)
        + [pl.BlockSpec((count, rows, cols), lambda t, mine, slots: (0, 0, t))]
        + [pl.BlockSpec(memory_space=pl.ANY)] * len(alias)
    )
    return pl.pallas_call(
        functools.partial(rows_kernel, len(pieces)),
        out_shape=jax.ShapeDtypeStruct((count, le, 2, rows, n), BF16),
        grid_spec=pltpu.PrefetchScalarGridSpec(
            num_scalar_prefetch=2,
            grid=(n // cols,),
            in_specs=in_specs,
            out_specs=pl.BlockSpec((count, 1, 2, rows, cols), lambda t, mine, slots: (0, energy, 0, 0, t)),
            scratch_shapes=[pltpu.VMEM((count, 2, rows, cols), BF16)],
        ),
        input_output_aliases={2 + len(in_specs) - 1: 0} if alias else {},
        compiler_params=params(56),
        cost_estimate=cost(4 * count * count * rows * n, rows * n * count * 10),
        name="rows",
    )(mine[None], slots, *pieces, *pieces, coupling, *alias)


def density_terms(energy, g_ref, gamma_ref, x_ref, y_ref):
    n = g_ref.shape[-1]
    gamma = gamma_ref[0, energy:energy + 1, :]
    g_re, g_im = g_ref[0, 0, 0], g_ref[0, 0, 1]
    row, col = row_col(n, n)
    x, yt = x_ref[0].astype(F32), y_ref[0].astype(F32).T
    s_re = jnp.where(col >= row, x, yt).astype(BF16)
    s_im = jnp.where(col < row, x, jnp.where(col > row, -yt, 0.0)).astype(BF16)
    scaled_re = (g_re.astype(F32) * gamma).astype(BF16).astype(F32)
    scaled_im = (g_im.astype(F32) * gamma).astype(BF16).astype(F32)
    m_re = (dot_nn(g_re, s_re) - dot_nn(g_im, s_im) + scaled_re).astype(BF16)
    m_im = (dot_nn(g_re, s_im) + dot_nn(g_im, s_re) + scaled_im).astype(BF16)
    return dot_nt(m_re, g_re) + dot_nt(m_im, g_im), dot_nt(m_im, g_re) - dot_nt(m_re, g_im)


def first_density_kernel(energy, first, g_ref, gamma_ref, x_ref, y_ref, *refs):
    for c, d in enumerate(density_terms(energy, g_ref, gamma_ref, x_ref, y_ref)):
        refs[-1][0, c] = d if first else d + refs[0][0, c]


def first_density(energy, green, broadening, x, y, held):
    lk, le, _, n, _ = green.shape
    alias = [] if held is None else [held]
    pair = pl.BlockSpec((1, 2, n, n), lambda k: (k, 0, 0, 0))
    one = pl.BlockSpec((1, n, n), lambda k: (k, 0, 0))
    return pl.pallas_call(
        functools.partial(first_density_kernel, energy, held is None),
        out_shape=pltpu.HBM((lk, 2, n, n), F32),
        grid=(lk,),
        in_specs=[
            pl.BlockSpec((1, 1, 2, n, n), lambda k: (k, energy, 0, 0, 0)),
            pl.BlockSpec((1, le, n), lambda k: (k, 0, 0)),
            one,
            one,
        ] + [pair] * len(alias),
        out_specs=pair,
        compiler_params=params(44),
        cost_estimate=cost(16 * lk * n**3, lk * n * n * 20),
        name="density",
    )(green, broadening, x, y, *alias)


def last_density_kernel(scale, energy, chunks, odd, g_ref, gamma_ref, x_ref, y_ref, held_ref, *refs):
    d_ref, outs = refs[-1], refs[:-1]
    groups, _, rows, _ = outs[0].shape
    for c, d in enumerate(density_terms(energy, g_ref, gamma_ref, x_ref, y_ref)):
        d_ref[c] = (d + held_ref[0, c]) * scale
    for at, (i, low, parts) in enumerate(chunks):
        keep_ref, send_ref = outs[2 * at], outs[2 * at + 1]

        @pl.when(pl.program_id(0) == i)
        def _():
            for c in range(parts):
                for g in range(groups):
                    mine = pl.multiple_of((2 * g + odd[0]) * rows, rows)
                    other = pl.multiple_of((2 * g + 1 - odd[0]) * rows, rows)
                    keep_ref[g, c] = d_ref[low + c, pl.ds(mine, rows), :].astype(BF16)
                    send_ref[g, c] = d_ref[low + c, pl.ds(other, rows), :].astype(BF16)


def last_density(scale, energy, start, count, chunks, groups, odd, green, broadening, x, y, held):
    _, le, _, n, _ = green.shape
    rows = n // (2 * groups)
    one = pl.BlockSpec((1, n, n), lambda i, odd: (start + i, 0, 0))
    shapes = [(groups, parts, rows, n) for _, _, parts in chunks for _ in range(2)]
    return pl.pallas_call(
        functools.partial(last_density_kernel, scale, energy, chunks),
        out_shape=[jax.ShapeDtypeStruct(shape, BF16) for shape in shapes],
        grid_spec=pltpu.PrefetchScalarGridSpec(
            num_scalar_prefetch=1,
            grid=(count,),
            in_specs=[
                pl.BlockSpec((1, 1, 2, n, n), lambda i, odd: (start + i, energy, 0, 0, 0)),
                pl.BlockSpec((1, le, n), lambda i, odd: (start + i, 0, 0)),
                one,
                one,
                pl.BlockSpec((1, 2, n, n), lambda i, odd: (start + i, 0, 0, 0)),
            ],
            out_specs=[pl.BlockSpec(shape, lambda i, odd: (0, 0, 0, 0)) for shape in shapes],
            scratch_shapes=[pltpu.VMEM((2, n, n), F32)],
        ),
        compiler_params=params(44),
        cost_estimate=cost(count * 16 * n**3, count * n * n * 20),
        name="density",
    )(odd[None], green, broadening, x, y, held)


def pair_sum_kernel(group, keep_ref, recv_ref, *outs):
    groups = len(outs)
    for d in range(groups):
        at = lax.rem(group[0] + d, groups)
        outs[d][...] = (keep_ref[at].astype(F32) + recv_ref[at].astype(F32)).astype(BF16)


def pair_sum(group, keep, recv):
    groups = keep.shape[0]
    vmem = pl.BlockSpec(memory_space=pltpu.VMEM)
    return pl.pallas_call(
        pair_sum_kernel,
        out_shape=[jax.ShapeDtypeStruct(keep.shape[1:], BF16)] * groups,
        in_specs=[pl.BlockSpec(memory_space=pltpu.SMEM), vmem, vmem],
        out_specs=[vmem] * groups,
        compiler_params=params(16),
        cost_estimate=cost(keep.size, keep.size * 6),
        name="pairsum",
    )(group[None], keep, recv)


def staged(green_ret, broadening, coupling, shift_steps, mode_weight, occupation, momentum_map):
    lk, le, _, _, _ = green_ret.shape
    ne, nm = lax.axis_size("energy"), lax.axis_size("mom")
    if le != SHIFT_MAX or lk % 2 or ne % 2 or nm & (nm - 1):
        raise ValueError("unsupported sizes")
    hk, groups = lk // 2, ne // 2
    me, mine = lax.axis_index("energy").astype(jnp.int32), lax.axis_index("mom").astype(jnp.int32)
    odd, group = me & 1, me >> 1
    pairs = [(i, i ^ 1) for i in range(ne)]
    away = [(i, i + (2 if i % 2 else -2)) for i in range(ne) if 0 <= i + (2 if i % 2 else -2) < ne]
    across = [(i, i + (-2 if i % 2 else 2)) for i in range(ne) if 0 <= i + (-2 if i % 2 else 2) < ne]
    strides = []
    while (nm >> (len(strides) + 1)) > 0:
        strides.append(nm >> (len(strides) + 1))

    def permuted(x, perm):
        return lax.ppermute(x, "energy", perm)

    def over_energy(x, perm):
        return hbm(permuted(x, perm))

    def swap(x, stride):
        moved = lax.ppermute(x, "mom", [(i, i ^ stride) for i in range(nm)])
        return hbm(moved)

    def spread(x):
        held = [x]
        for s in strides:
            held = held + [swap(piece, s) for piece in held]
        return held

    order = [0]
    for s in strides:
        order = order + [o ^ s for o in order]

    modes = (shift_steps, mode_weight, occupation)

    owner, inner = momentum_map // lk, momentum_map % lk
    place = jnp.zeros_like(owner)
    for at, o in enumerate(order):
        place = jnp.where((owner ^ mine) == o, at, place)
    slots = (place * lk + ((inner // hk) ^ odd) * hk + inner % hk).astype(jnp.int32)

    green_ret = hbm(green_ret)
    coupling = hbm(coupling)
    coupling_pieces = spread(coupling)

    send = [lesser_packed((1 - odd) * hk + j, green_ret, broadening) for j in range(hk)]
    recv = [[over_energy(send[j][h], pairs) for h in range(2)] for j in range(hk)]
    keep = [lesser_packed(odd * hk + j, green_ret, broadening) for j in range(hk)]
    kz = [[permuted(keep[j][h], away) for h in range(2)] for j in range(hk)]
    rz = [[permuted(recv[j][h], across) for h in range(2)] for j in range(hk)]
    got, last = [], None
    for j in range(hk):
        for h in range(2):
            last = sources(
                odd, modes, j, h, hk, keep[j][h], recv[j][h], kz[j][h], rz[j][h], last)
        got.append(last)

    full, turned = place_coupling(mine, tuple(order), coupling_pieces)

    held_rows, held_density = None, None
    scale = 1.0 / (le * ne)
    late = []
    for e in range(le):
        use = [got[j] for j in range(hk)] if e == 0 else [last]
        fresh = [spread(part[e]) for part in use]
        back = [spread(over_energy(part[le + e], pairs)) for part in use]
        pieces = [part[at] for at in range(nm) for part in fresh + back]
        if e < le - 1:
            x, y = home_blocks(mine, slots, pieces, full, turned, lk)
            held_density = first_density(e, green_ret, broadening, x, y, held_density)
        else:
            shares = []
            x, y = home_blocks(mine, slots, pieces, full, turned, lk)
            whole = [(i, 0, 2) for i in range(lk - 2)]
            calls = ((0, 1, ((0, 0, 2),)), (1, lk - 1, tuple(whole) + ((lk - 2, 0, 1), (lk - 2, 1, 1))))
            for first, count, chunks in calls:
                shares = shares + list(last_density(
                    scale, e, first, count, chunks, groups, odd,
                    green_ret, broadening, x, y, held_density))
            for k in range(len(shares) // 2):
                kept, sent = shares[2 * k], shares[2 * k + 1]
                other = permuted(sent, pairs)
                parts = pair_sum(group, kept, other)
                total = parts[0].astype(F32)
                for d in range(1, groups):
                    perm = [(i, (i + 2 * d) % ne) for i in range(ne)]
                    total = total + permuted(parts[d], perm).astype(F32)
                late.append(total)
            late = late[:-2] + [jnp.concatenate(late[-2:], axis=0)]
        held_rows = own_rows(mine, slots, pieces, coupling, e, le, held_rows)
    density = jnp.transpose(jnp.stack(late), (2, 0, 1, 3))
    return held_rows, density


def solution(mesh):
    return jax.shard_map(
        staged,
        mesh=mesh,
        in_specs=(
            P("mom", "energy", None, None, None),
            P("mom", "energy", None),
            P(None, "mom", None),
            P(),
            P(),
            P(),
            P(),
        ),
        out_specs=(P(None, "energy", None, "mom", None), P("energy", "mom", None, None)),
        check_vma=False,
    )
```

```python
import functools

import jax
import jax.numpy as jnp
from jax import lax
from jax.experimental import pallas as pl
from jax.experimental.pallas import tpu as pltpu
from jax.sharding import PartitionSpec as P


SHIFT_MAX = 2
F32 = jnp.float32
BF16 = jnp.bfloat16


def params(mib):
    return pltpu.CompilerParams(vmem_limit_bytes=mib * 1024 * 1024)


def hbm(x):
    return pltpu.with_memory_space_constraint(x, pltpu.HBM)


def cost(flops, nbytes):
    return pl.CostEstimate(flops=int(flops), bytes_accessed=int(nbytes), transcendentals=0)


def dot_nt(a, b):
    return lax.dot_general(a, b, (((1,), (1,)), ((), ())), preferred_element_type=F32)


def dot_nn(a, b):
    return lax.dot_general(a, b, (((1,), (0,)), ((), ())), preferred_element_type=F32)


def row_col(rows, cols):
    return lax.broadcasted_iota(jnp.int32, (rows, cols), 0), lax.broadcasted_iota(jnp.int32, (rows, cols), 1)


def lesser_kernel(sel, g_ref, gamma_ref, *outs):
    n = g_ref.shape[-1]
    half = n // 2
    e = pl.program_id(0)
    gamma = gamma_ref[0, pl.ds(e, 1), :]
    g_re, g_im = g_ref[0, 0, 0], g_ref[0, 0, 1]
    s_re = (g_re.astype(F32) * gamma).astype(BF16)
    s_im = (g_im.astype(F32) * gamma).astype(BF16)
    row, col = row_col(half, half)

    def real(i, j):
        i, j = slice(i * half, (i + 1) * half), slice(j * half, (j + 1) * half)
        return dot_nt(s_re[i], g_re[j]) + dot_nt(s_im[i], g_im[j])

    def imag(i, j):
        i, j = slice(i * half, (i + 1) * half), slice(j * half, (j + 1) * half)
        return dot_nt(s_im[i], g_re[j]) - dot_nt(s_re[i], g_im[j])

    for d in range(2):
        outs[d][0, :, d * half:(d + 1) * half] = jnp.where(col >= row, real(d, d), imag(d, d)).astype(BF16)
    outs[0][0, :, half:] = real(0, 1).astype(BF16)
    outs[1][0, :, :half] = imag(1, 0).astype(BF16)


def lesser_packed(which, green, broadening):
    _, le, _, n, _ = green.shape
    return pl.pallas_call(
        lesser_kernel,
        out_shape=[pltpu.HBM((le, n // 2, n), BF16)] * 2,
        grid_spec=pltpu.PrefetchScalarGridSpec(
            num_scalar_prefetch=1,
            grid=(le,),
            in_specs=[
                pl.BlockSpec((1, 1, 2, n, n), lambda e, sel: (sel[0], e, 0, 0, 0)),
                pl.BlockSpec((1, le, n), lambda e, sel: (sel[0], 0, 0)),
            ],
            out_specs=[pl.BlockSpec((1, n // 2, n), lambda e, sel: (e, 0, 0))] * 2,
        ),
        compiler_params=params(56),
        cost_estimate=cost(le * 6 * n**3, le * n * n * 6),
        name="lesser",
    )(which[None], green, broadening)


def place_kernel(order, where, *refs):
    pieces, (full_ref, turned_ref) = refs[:-2], refs[-2:]
    rows = pieces[0].shape[1]
    for at, c_ref in enumerate(pieces):
        start = pl.ds(pl.multiple_of((where[0] ^ order[at]) * rows, rows), rows)
        for q in range(c_ref.shape[0]):
            full_ref[q, start, :] = c_ref[q]
            turned_ref[q, :, start] = c_ref[q].T


def place_coupling(where, order, pieces):
    nk, rows, n = pieces[0].shape
    each = 2
    return pl.pallas_call(
        functools.partial(place_kernel, order),
        out_shape=[pltpu.HBM((nk, n, n), BF16)] * 2,
        grid_spec=pltpu.PrefetchScalarGridSpec(
            num_scalar_prefetch=1,
            grid=(nk // each,),
            in_specs=[pl.BlockSpec((each, rows, n), lambda q, w: (q, 0, 0))] * len(pieces),
            out_specs=[pl.BlockSpec((each, n, n), lambda q, w: (q, 0, 0))] * 2,
        ),
        compiler_params=params(56),
        cost_estimate=cost(nk * n * n * 4, nk * n * n * 6),
        name="place",
    )(where[None], *pieces)


def source_kernel(odd, steps, strength, boson, keep, recv, kz, rz, *refs):
    le = keep.shape[0]
    weights = []
    for s in range(1, SHIFT_MAX + 1):
        up, down = jnp.float32(0), jnp.float32(0)
        for m in range(steps.shape[0]):
            held = jnp.where(steps[m] == s, strength[m], 0.0)
            up, down = up + held * (boson[m] + 1.0), down + held * boson[m]
        weights = weights + [up, down]
    outs = refs[-2 * le:]

    def emit(order):
        line = [(ref, e) for ref in order for e in range(le)]
        for e in range(le):
            for ref, target in ((keep, outs[e]), (recv, outs[le + e])):
                at = [i for i, held in enumerate(order) if held is ref][0] * le + e
                total = None
                for s in range(1, SHIFT_MAX + 1):
                    for j, sign in ((0, s), (1, -s)):
                        source, index = line[at + sign]
                        term = weights[2 * (s - 1) + j] * source[index].astype(F32)
                        total = term if total is None else total + term
                target[0] = total.astype(BF16)

    @pl.when(odd[0] == 0)
    def _():
        emit((rz, keep, recv, kz))

    @pl.when(odd[0] == 1)
    def _():
        emit((kz, recv, keep, rz))


def sources(odd, modes, j, h, hk, keep, recv, kz, rz, held):
    le, half, n = keep.shape
    rows = half // 2
    at = h * (half // rows)
    big = pl.BlockSpec((le, rows, n), lambda r, *_: (0, r, 0))
    first = pl.BlockSpec((1, rows, n), lambda r, *_: (0, at + r, 0))
    later = pl.BlockSpec((1, rows, n), lambda r, *_: (j, at + r, 0))
    shapes = [(1 if e == 0 else hk, n, n) for e in range(le)] * 2
    specs = [first if e == 0 else later for e in range(le)] * 2
    alias, extra = {}, []
    if held is not None:
        for i, value in enumerate(held):
            if i % le or h:
                alias[5 + len(modes) + len(extra)] = i
                extra.append(value)
    return pl.pallas_call(
        source_kernel,
        out_shape=[pltpu.HBM(shape, BF16) for shape in shapes],
        grid_spec=pltpu.PrefetchScalarGridSpec(
            num_scalar_prefetch=1 + len(modes),
            grid=(half // rows,),
            in_specs=[big] * 4 + [pl.BlockSpec(memory_space=pl.ANY)] * len(extra),
            out_specs=specs,
        ),
        input_output_aliases=alias,
        compiler_params=params(16),
        cost_estimate=cost(le * half * n * 16, le * half * n * 12),
        name="source",
    )(odd[None], *modes, keep, recv, kz, rz, *extra)


def home_kernel(lk, pieces, mine, slots, *refs):
    first = mine[0] * lk
    ins, (c_ref, ct_ref, x_ref, y_ref, q_ref) = refs[:pieces], refs[pieces:]
    each, rows, n = ins[0].shape
    count = pieces * each
    for s in range(pieces):
        for j in range(each):
            q_ref[s * each + j] = ins[s][j]
    tr, tc = 16, 256

    def tile(index, _):
        r = pl.ds(pl.multiple_of((index // (n // tc)) * tr, tr), tr)
        m = pl.ds(pl.multiple_of((index % (n // tc)) * tc, tc), tc)
        xs, ys = [None] * lk, [None] * lk
        for q in range(0, count, 4):
            px, py = [None] * lk, [None] * lk
            for p in (q, q + 2):
                c, ct = [c_ref[p + i, r, m] for i in range(2)], [ct_ref[p + i, r, m] for i in range(2)]
                for k in range(lk):
                    v = [q_ref[slots[first + k, p + i], r, m] for i in range(2)]
                    x, y = c[0] * v[0] + c[1] * v[1], ct[0] * v[0] + ct[1] * v[1]
                    px[k] = x if p == q else px[k] + x
                    py[k] = y if p == q else py[k] + y
            for k in range(lk):
                xs[k] = px[k] if q == 0 else xs[k] + px[k]
                ys[k] = py[k] if q == 0 else ys[k] + py[k]
        for k in range(lk):
            x_ref[k, r, m] = xs[k]
            y_ref[k, r, m] = ys[k]
        return 0

    lax.fori_loop(0, (rows // tr) * (n // tc), tile, 0)


def home_blocks(mine, slots, pieces, full, turned, lk):
    each, n, _ = pieces[0].shape
    count = each * len(pieces)
    rows = n // 4
    block = lambda lead: pl.BlockSpec((lead, rows, n), lambda g, *_: (0, g, 0))
    return pl.pallas_call(
        functools.partial(home_kernel, lk, len(pieces)),
        out_shape=[pltpu.VMEM((lk, n, n), BF16)] * 2,
        grid_spec=pltpu.PrefetchScalarGridSpec(
            num_scalar_prefetch=2,
            grid=(n // rows,),
            in_specs=[block(each)] * len(pieces) + [block(count), block(count)],
            out_specs=[block(lk), block(lk)],
            scratch_shapes=[pltpu.VMEM((count, rows, n), BF16)],
        ),
        compiler_params=params(44),
        cost_estimate=cost(4 * lk * count * n * n, n * n * (6 * count + 4 * lk)),
        name="home",
    )(mine[None], slots, *pieces, full, turned)


def rows_kernel(pieces, base, mine, slots, *refs):
    a_refs, b_refs, refs = refs[:pieces], refs[pieces:2 * pieces], refs[2 * pieces:]
    c_ref, out_ref, d_ref = (refs[0],) + refs[-2:]
    each, rows, cols = a_refs[0].shape
    count = pieces * each
    row, col = row_col(rows, cols)
    above = (col - row) + ((base + pl.program_id(0)) * cols - mine[0] * rows)
    for s in range(pieces):
        for j in range(each):
            a, b = a_refs[s][j].astype(F32), b_refs[s][j].astype(F32).T
            d_ref[s * each + j, 0] = jnp.where(above >= 0, a, b).astype(BF16)
            d_ref[s * each + j, 1] = jnp.where(above < 0, a, jnp.where(above > 0, -b, 0.0)).astype(BF16)
    tr, kg, tc = 32, 2, 256
    wide = cols // tc

    def tile(index, _):
        r = pl.ds(pl.multiple_of(((index // wide) % (rows // tr)) * tr, tr), tr)
        m = pl.ds(pl.multiple_of((index % wide) * tc, tc), tc)
        k0 = (index // (wide * (rows // tr))) * kg
        us, vs = [None] * kg, [None] * kg
        for q in range(0, count, 4):
            pu, pv = [None] * kg, [None] * kg
            for p in (q, q + 2):
                c = [c_ref[p + i, r, m] for i in range(2)]
                for k in range(kg):
                    slot = [slots[k0 + k, p + i] for i in range(2)]
                    u = c[0] * d_ref[slot[0], 0, r, m] + c[1] * d_ref[slot[1], 0, r, m]
                    v = c[0] * d_ref[slot[0], 1, r, m] + c[1] * d_ref[slot[1], 1, r, m]
                    pu[k] = u if p == q else pu[k] + u
                    pv[k] = v if p == q else pv[k] + v
            for k in range(kg):
                us[k] = pu[k] if q == 0 else us[k] + pu[k]
                vs[k] = pv[k] if q == 0 else vs[k] + pv[k]
        for k in range(kg):
            out_ref[k0 + k, 0, 0, r, m] = us[k]
            out_ref[k0 + k, 0, 1, r, m] = vs[k]
        return 0

    lax.fori_loop(0, wide * (rows // tr) * (count // kg), tile, 0)


def own_rows(mine, slots, pieces, coupling, energy, le, base, steps, held):
    each, n, _ = pieces[0].shape
    count, rows, _ = coupling.shape
    cols = n // 2
    alias = [] if held is None else [held]
    in_specs = (
        [pl.BlockSpec((each, rows, cols), lambda t, mine, slots: (0, mine[0], base + t))] * len(pieces)
        + [pl.BlockSpec((each, cols, rows), lambda t, mine, slots: (0, base + t, mine[0]))] * len(pieces)
        + [pl.BlockSpec((count, rows, cols), lambda t, mine, slots: (0, 0, base + t))]
        + [pl.BlockSpec(memory_space=pl.ANY)] * len(alias)
    )
    return pl.pallas_call(
        functools.partial(rows_kernel, len(pieces), base),
        out_shape=jax.ShapeDtypeStruct((count, le, 2, rows, n), BF16),
        grid_spec=pltpu.PrefetchScalarGridSpec(
            num_scalar_prefetch=2,
            grid=(steps,),
            in_specs=in_specs,
            out_specs=pl.BlockSpec((count, 1, 2, rows, cols), lambda t, mine, slots: (0, energy, 0, 0, base + t)),
            scratch_shapes=[pltpu.VMEM((count, 2, rows, cols), BF16)],
        ),
        input_output_aliases={2 + len(in_specs) - 1: 0} if alias else {},
        compiler_params=params(56),
        cost_estimate=cost(4 * count * count * rows * n, rows * n * count * 10),
        name="rows",
    )(mine[None], slots, *pieces, *pieces, coupling, *alias)


def density_terms(energy, g_ref, gamma_ref, x_ref, y_ref):
    n = g_ref.shape[-1]
    gamma = gamma_ref[0, energy:energy + 1, :]
    g_re, g_im = g_ref[0, 0, 0], g_ref[0, 0, 1]
    row, col = row_col(n, n)
    x, yt = x_ref[0].astype(F32), y_ref[0].astype(F32).T
    s_re = jnp.where(col >= row, x, yt).astype(BF16)
    s_im = jnp.where(col < row, x, jnp.where(col > row, -yt, 0.0)).astype(BF16)
    scaled_re = (g_re.astype(F32) * gamma).astype(BF16).astype(F32)
    scaled_im = (g_im.astype(F32) * gamma).astype(BF16).astype(F32)
    m_re = (dot_nn(g_re, s_re) - dot_nn(g_im, s_im) + scaled_re).astype(BF16)
    m_im = (dot_nn(g_re, s_im) + dot_nn(g_im, s_re) + scaled_im).astype(BF16)
    return dot_nt(m_re, g_re) + dot_nt(m_im, g_im), dot_nt(m_im, g_re) - dot_nt(m_re, g_im)


def first_density_kernel(energy, first, g_ref, gamma_ref, x_ref, y_ref, *refs):
    for c, d in enumerate(density_terms(energy, g_ref, gamma_ref, x_ref, y_ref)):
        refs[-1][0, c] = d if first else d + refs[0][0, c]


def first_density(energy, green, broadening, x, y, held):
    lk, le, _, n, _ = green.shape
    alias = [] if held is None else [held]
    pair = pl.BlockSpec((1, 2, n, n), lambda k: (k, 0, 0, 0))
    one = pl.BlockSpec((1, n, n), lambda k: (k, 0, 0))
    return pl.pallas_call(
        functools.partial(first_density_kernel, energy, held is None),
        out_shape=pltpu.HBM((lk, 2, n, n), F32),
        grid=(lk,),
        in_specs=[
            pl.BlockSpec((1, 1, 2, n, n), lambda k: (k, energy, 0, 0, 0)),
            pl.BlockSpec((1, le, n), lambda k: (k, 0, 0)),
            one,
            one,
        ] + [pair] * len(alias),
        out_specs=pair,
        compiler_params=params(44),
        cost_estimate=cost(16 * lk * n**3, lk * n * n * 20),
        name="density",
    )(green, broadening, x, y, *alias)


def last_density_kernel(scale, energy, odd, g_ref, gamma_ref, x_ref, y_ref, held_ref, *refs):
    d_ref, outs = refs[-1], refs[:-1]
    groups, _, rows, _ = outs[0].shape
    for c, d in enumerate(density_terms(energy, g_ref, gamma_ref, x_ref, y_ref)):
        d_ref[c] = (d + held_ref[0, c]) * scale
    for i in range(len(outs) // 2):
        keep_ref, send_ref = outs[2 * i], outs[2 * i + 1]

        @pl.when(pl.program_id(0) == i)
        def _():
            for c in range(2):
                for g in range(groups):
                    mine = pl.multiple_of((2 * g + odd[0]) * rows, rows)
                    other = pl.multiple_of((2 * g + 1 - odd[0]) * rows, rows)
                    keep_ref[g, c] = d_ref[c, pl.ds(mine, rows), :].astype(BF16)
                    send_ref[g, c] = d_ref[c, pl.ds(other, rows), :].astype(BF16)


def last_density(scale, energy, start, count, groups, odd, green, broadening, x, y, held):
    _, le, _, n, _ = green.shape
    rows = n // (2 * groups)
    one = pl.BlockSpec((1, n, n), lambda i, odd: (start + i, 0, 0))
    out = pl.BlockSpec((groups, 2, rows, n), lambda i, odd: (0, 0, 0, 0))
    return pl.pallas_call(
        functools.partial(last_density_kernel, scale, energy),
        out_shape=[jax.ShapeDtypeStruct((groups, 2, rows, n), BF16)] * (2 * count),
        grid_spec=pltpu.PrefetchScalarGridSpec(
            num_scalar_prefetch=1,
            grid=(count,),
            in_specs=[
                pl.BlockSpec((1, 1, 2, n, n), lambda i, odd: (start + i, energy, 0, 0, 0)),
                pl.BlockSpec((1, le, n), lambda i, odd: (start + i, 0, 0)),
                one,
                one,
                pl.BlockSpec((1, 2, n, n), lambda i, odd: (start + i, 0, 0, 0)),
            ],
            out_specs=[out] * (2 * count),
            scratch_shapes=[pltpu.VMEM((2, n, n), F32)],
        ),
        compiler_params=params(44),
        cost_estimate=cost(count * 16 * n**3, count * n * n * 20),
        name="density",
    )(odd[None], green, broadening, x, y, held)


def pair_sum_kernel(group, keep_ref, recv_ref, *outs):
    groups = len(outs)
    for d in range(groups):
        at = lax.rem(group[0] + d, groups)
        outs[d][...] = (keep_ref[at].astype(F32) + recv_ref[at].astype(F32)).astype(BF16)


def pair_sum(group, keep, recv):
    groups = keep.shape[0]
    vmem = pl.BlockSpec(memory_space=pltpu.VMEM)
    return pl.pallas_call(
        pair_sum_kernel,
        out_shape=[jax.ShapeDtypeStruct(keep.shape[1:], BF16)] * groups,
        in_specs=[pl.BlockSpec(memory_space=pltpu.SMEM), vmem, vmem],
        out_specs=[vmem] * groups,
        compiler_params=params(16),
        cost_estimate=cost(keep.size, keep.size * 6),
        name="pairsum",
    )(group[None], keep, recv)


def staged(green_ret, broadening, coupling, shift_steps, mode_weight, occupation, momentum_map):
    lk, le, _, _, _ = green_ret.shape
    ne, nm = lax.axis_size("energy"), lax.axis_size("mom")
    if le != SHIFT_MAX or lk % 2 or ne % 2 or nm & (nm - 1):
        raise ValueError("unsupported sizes")
    hk, groups = lk // 2, ne // 2
    me, mine = lax.axis_index("energy").astype(jnp.int32), lax.axis_index("mom").astype(jnp.int32)
    odd, group = me & 1, me >> 1
    pairs = [(i, i ^ 1) for i in range(ne)]
    away = [(i, i + (2 if i % 2 else -2)) for i in range(ne) if 0 <= i + (2 if i % 2 else -2) < ne]
    across = [(i, i + (-2 if i % 2 else 2)) for i in range(ne) if 0 <= i + (-2 if i % 2 else 2) < ne]
    strides = []
    while (nm >> (len(strides) + 1)) > 0:
        strides.append(nm >> (len(strides) + 1))

    def permuted(x, perm):
        return lax.ppermute(x, "energy", perm)

    def over_energy(x, perm):
        return hbm(permuted(x, perm))

    def swap(x, stride):
        moved = lax.ppermute(x, "mom", [(i, i ^ stride) for i in range(nm)])
        return hbm(moved)

    def spread(x):
        held = [x]
        for s in strides:
            held = held + [swap(piece, s) for piece in held]
        return held

    order = [0]
    for s in strides:
        order = order + [o ^ s for o in order]

    modes = (shift_steps, mode_weight, occupation)

    owner, inner = momentum_map // lk, momentum_map % lk
    place = jnp.zeros_like(owner)
    for at, o in enumerate(order):
        place = jnp.where((owner ^ mine) == o, at, place)
    slots = (place * lk + ((inner // hk) ^ odd) * hk + inner % hk).astype(jnp.int32)

    green_ret = hbm(green_ret)
    coupling = hbm(coupling)
    coupling_pieces = spread(coupling)

    send = [lesser_packed((1 - odd) * hk + j, green_ret, broadening) for j in range(hk)]
    recv = [[over_energy(send[j][h], pairs) for h in range(2)] for j in range(hk)]
    keep = [lesser_packed(odd * hk + j, green_ret, broadening) for j in range(hk)]
    kz = [[permuted(keep[j][h], away) for h in range(2)] for j in range(hk)]
    rz = [[permuted(recv[j][h], across) for h in range(2)] for j in range(hk)]
    got, last = [], None
    for j in range(hk):
        for h in range(2):
            last = sources(
                odd, modes, j, h, hk, keep[j][h], recv[j][h], kz[j][h], rz[j][h], last)
        got.append(last)

    full, turned = place_coupling(mine, tuple(order), coupling_pieces)

    held_rows, held_density = None, None
    scale = 1.0 / (le * ne)
    late = []
    for e in range(le):
        use = [got[j] for j in range(hk)] if e == 0 else [last]
        fresh = [spread(part[e]) for part in use]
        back = [spread(over_energy(part[le + e], pairs)) for part in use]
        pieces = [part[at] for at in range(nm) for part in fresh + back]
        if e < le - 1:
            x, y = home_blocks(mine, slots, pieces, full, turned, lk)
            held_density = first_density(e, green_ret, broadening, x, y, held_density)
        else:
            shares = []
            x, y = home_blocks(mine, slots, pieces, full, turned, lk)
            for first, count in ((0, 1), (1, 1), (2, lk - 2)):
                shares = shares + list(last_density(
                    scale, e, first, count, groups, odd,
                    green_ret, broadening, x, y, held_density))
            for k in range(lk):
                kept, sent = shares[2 * k], shares[2 * k + 1]
                other = permuted(sent, pairs)
                parts = pair_sum(group, kept, other)
                total = parts[0].astype(F32)
                for d in range(1, groups):
                    perm = [(i, (i + 2 * d) % ne) for i in range(ne)]
                    total = total + permuted(parts[d], perm).astype(F32)
                late.append(total)
        for base, steps in (((0, 2),) if e < le - 1 else ((0, 1), (1, 1))):
            held_rows = own_rows(
                mine, slots, pieces, coupling, e, le, base, steps, held_rows)
    density = jnp.transpose(jnp.stack(late), (2, 0, 1, 3))
    return held_rows, density


def solution(mesh):
    return jax.shard_map(
        staged,
        mesh=mesh,
        in_specs=(
            P("mom", "energy", None, None, None),
            P("mom", "energy", None),
            P(None, "mom", None),
            P(),
            P(),
            P(),
            P(),
        ),
        out_specs=(P(None, "energy", None, "mom", None), P("energy", "mom", None, None)),
        check_vma=False,
    )
```

```python
import functools

import jax
import jax.numpy as jnp
from jax import lax
from jax.experimental import pallas as pl
from jax.experimental.pallas import tpu as pltpu
from jax.sharding import PartitionSpec as P


SHIFT_MAX = 2
F32 = jnp.float32
BF16 = jnp.bfloat16


def params(mib):
    return pltpu.CompilerParams(vmem_limit_bytes=mib * 1024 * 1024)


def hbm(x):
    return pltpu.with_memory_space_constraint(x, pltpu.HBM)


def cost(flops, nbytes):
    return pl.CostEstimate(flops=int(flops), bytes_accessed=int(nbytes), transcendentals=0)


def dot_nt(a, b):
    return lax.dot_general(a, b, (((1,), (1,)), ((), ())), preferred_element_type=F32)


def dot_nn(a, b):
    return lax.dot_general(a, b, (((1,), (0,)), ((), ())), preferred_element_type=F32)


def row_col(rows, cols):
    return lax.broadcasted_iota(jnp.int32, (rows, cols), 0), lax.broadcasted_iota(jnp.int32, (rows, cols), 1)


def lesser_kernel(sel, g_ref, gamma_ref, *outs):
    n = g_ref.shape[-1]
    half = n // 2
    e = pl.program_id(0)
    gamma = gamma_ref[0, pl.ds(e, 1), :]
    g_re, g_im = g_ref[0, 0, 0], g_ref[0, 0, 1]
    s_re = (g_re.astype(F32) * gamma).astype(BF16)
    s_im = (g_im.astype(F32) * gamma).astype(BF16)
    row, col = row_col(half, half)

    def real(i, j):
        i, j = slice(i * half, (i + 1) * half), slice(j * half, (j + 1) * half)
        return dot_nt(s_re[i], g_re[j]) + dot_nt(s_im[i], g_im[j])

    def imag(i, j):
        i, j = slice(i * half, (i + 1) * half), slice(j * half, (j + 1) * half)
        return dot_nt(s_im[i], g_re[j]) - dot_nt(s_re[i], g_im[j])

    for d in range(2):
        outs[d][0, :, d * half:(d + 1) * half] = jnp.where(col >= row, real(d, d), imag(d, d)).astype(BF16)
    outs[0][0, :, half:] = real(0, 1).astype(BF16)
    outs[1][0, :, :half] = imag(1, 0).astype(BF16)


def lesser_packed(which, green, broadening):
    _, le, _, n, _ = green.shape
    return pl.pallas_call(
        lesser_kernel,
        out_shape=[pltpu.HBM((le, n // 2, n), BF16)] * 2,
        grid_spec=pltpu.PrefetchScalarGridSpec(
            num_scalar_prefetch=1,
            grid=(le,),
            in_specs=[
                pl.BlockSpec((1, 1, 2, n, n), lambda e, sel: (sel[0], e, 0, 0, 0)),
                pl.BlockSpec((1, le, n), lambda e, sel: (sel[0], 0, 0)),
            ],
            out_specs=[pl.BlockSpec((1, n // 2, n), lambda e, sel: (e, 0, 0))] * 2,
        ),
        compiler_params=params(56),
        cost_estimate=cost(le * 6 * n**3, le * n * n * 6),
        name="lesser",
    )(which[None], green, broadening)


def place_kernel(order, where, *refs):
    pieces, (full_ref, turned_ref) = refs[:-2], refs[-2:]
    rows = pieces[0].shape[1]
    for at, c_ref in enumerate(pieces):
        start = pl.ds(pl.multiple_of((where[0] ^ order[at]) * rows, rows), rows)
        for q in range(c_ref.shape[0]):
            full_ref[q, start, :] = c_ref[q]
            turned_ref[q, :, start] = c_ref[q].T


def place_coupling(where, order, pieces):
    nk, rows, n = pieces[0].shape
    each = 2
    return pl.pallas_call(
        functools.partial(place_kernel, order),
        out_shape=[pltpu.HBM((nk, n, n), BF16)] * 2,
        grid_spec=pltpu.PrefetchScalarGridSpec(
            num_scalar_prefetch=1,
            grid=(nk // each,),
            in_specs=[pl.BlockSpec((each, rows, n), lambda q, w: (q, 0, 0))] * len(pieces),
            out_specs=[pl.BlockSpec((each, n, n), lambda q, w: (q, 0, 0))] * 2,
        ),
        compiler_params=params(56),
        cost_estimate=cost(nk * n * n * 4, nk * n * n * 6),
        name="place",
    )(where[None], *pieces)


def source_kernel(odd, steps, strength, boson, keep, recv, kz, rz, *refs):
    le = keep.shape[0]
    weights = []
    for s in range(1, SHIFT_MAX + 1):
        up, down = jnp.float32(0), jnp.float32(0)
        for m in range(steps.shape[0]):
            held = jnp.where(steps[m] == s, strength[m], 0.0)
            up, down = up + held * (boson[m] + 1.0), down + held * boson[m]
        weights = weights + [up, down]
    outs = refs[-2 * le:]

    def emit(order):
        line = [(ref, e) for ref in order for e in range(le)]
        for e in range(le):
            for ref, target in ((keep, outs[e]), (recv, outs[le + e])):
                at = [i for i, held in enumerate(order) if held is ref][0] * le + e
                total = None
                for s in range(1, SHIFT_MAX + 1):
                    for j, sign in ((0, s), (1, -s)):
                        source, index = line[at + sign]
                        term = weights[2 * (s - 1) + j] * source[index].astype(F32)
                        total = term if total is None else total + term
                target[0] = total.astype(BF16)

    @pl.when(odd[0] == 0)
    def _():
        emit((rz, keep, recv, kz))

    @pl.when(odd[0] == 1)
    def _():
        emit((kz, recv, keep, rz))


def sources(odd, modes, j, h, hk, keep, recv, kz, rz, held):
    le, half, n = keep.shape
    rows = half // 2
    at = h * (half // rows)
    big = pl.BlockSpec((le, rows, n), lambda r, *_: (0, r, 0))
    first = pl.BlockSpec((1, rows, n), lambda r, *_: (0, at + r, 0))
    later = pl.BlockSpec((1, rows, n), lambda r, *_: (j, at + r, 0))
    shapes = [(1 if e == 0 else hk, n, n) for e in range(le)] * 2
    specs = [first if e == 0 else later for e in range(le)] * 2
    alias, extra = {}, []
    if held is not None:
        for i, value in enumerate(held):
            if i % le or h:
                alias[5 + len(modes) + len(extra)] = i
                extra.append(value)
    return pl.pallas_call(
        source_kernel,
        out_shape=[pltpu.HBM(shape, BF16) for shape in shapes],
        grid_spec=pltpu.PrefetchScalarGridSpec(
            num_scalar_prefetch=1 + len(modes),
            grid=(half // rows,),
            in_specs=[big] * 4 + [pl.BlockSpec(memory_space=pl.ANY)] * len(extra),
            out_specs=specs,
        ),
        input_output_aliases=alias,
        compiler_params=params(16),
        cost_estimate=cost(le * half * n * 16, le * half * n * 12),
        name="source",
    )(odd[None], *modes, keep, recv, kz, rz, *extra)


def home_kernel(lk, pieces, mine, slots, *refs):
    first = mine[0] * lk
    ins, (c_ref, ct_ref, x_ref, y_ref, q_ref) = refs[:pieces], refs[pieces:]
    each, rows, n = ins[0].shape
    count = pieces * each
    for s in range(pieces):
        for j in range(each):
            q_ref[s * each + j] = ins[s][j]
    tr, tc = 16, 256

    def tile(index, _):
        r = pl.ds(pl.multiple_of((index // (n // tc)) * tr, tr), tr)
        m = pl.ds(pl.multiple_of((index % (n // tc)) * tc, tc), tc)
        xs, ys = [None] * lk, [None] * lk
        for q in range(0, count, 4):
            px, py = [None] * lk, [None] * lk
            for p in (q, q + 2):
                c, ct = [c_ref[p + i, r, m] for i in range(2)], [ct_ref[p + i, r, m] for i in range(2)]
                for k in range(lk):
                    v = [q_ref[slots[first + k, p + i], r, m] for i in range(2)]
                    x, y = c[0] * v[0] + c[1] * v[1], ct[0] * v[0] + ct[1] * v[1]
                    px[k] = x if p == q else px[k] + x
                    py[k] = y if p == q else py[k] + y
            for k in range(lk):
                xs[k] = px[k] if q == 0 else xs[k] + px[k]
                ys[k] = py[k] if q == 0 else ys[k] + py[k]
        for k in range(lk):
            x_ref[k, r, m] = xs[k]
            y_ref[k, r, m] = ys[k]
        return 0

    lax.fori_loop(0, (rows // tr) * (n // tc), tile, 0)


def home_blocks(mine, slots, pieces, full, turned, lk):
    each, n, _ = pieces[0].shape
    count = each * len(pieces)
    rows = n // 4
    block = lambda lead: pl.BlockSpec((lead, rows, n), lambda g, *_: (0, g, 0))
    return pl.pallas_call(
        functools.partial(home_kernel, lk, len(pieces)),
        out_shape=[pltpu.VMEM((lk, n, n), BF16)] * 2,
        grid_spec=pltpu.PrefetchScalarGridSpec(
            num_scalar_prefetch=2,
            grid=(n // rows,),
            in_specs=[block(each)] * len(pieces) + [block(count), block(count)],
            out_specs=[block(lk), block(lk)],
            scratch_shapes=[pltpu.VMEM((count, rows, n), BF16)],
        ),
        compiler_params=params(44),
        cost_estimate=cost(4 * lk * count * n * n, n * n * (6 * count + 4 * lk)),
        name="home",
    )(mine[None], slots, *pieces, full, turned)


def rows_kernel(pieces, base, mine, slots, *refs):
    a_refs, b_refs, refs = refs[:pieces], refs[pieces:2 * pieces], refs[2 * pieces:]
    c_ref, out_ref, d_ref = (refs[0],) + refs[-2:]
    each, rows, cols = a_refs[0].shape
    count = pieces * each
    row, col = row_col(rows, cols)
    above = (col - row) + ((base + pl.program_id(0)) * cols - mine[0] * rows)
    for s in range(pieces):
        for j in range(each):
            a, b = a_refs[s][j].astype(F32), b_refs[s][j].astype(F32).T
            d_ref[s * each + j, 0] = jnp.where(above >= 0, a, b).astype(BF16)
            d_ref[s * each + j, 1] = jnp.where(above < 0, a, jnp.where(above > 0, -b, 0.0)).astype(BF16)
    tr, kg, tc = 32, 2, 256
    wide = cols // tc

    def tile(index, _):
        r = pl.ds(pl.multiple_of(((index // wide) % (rows // tr)) * tr, tr), tr)
        m = pl.ds(pl.multiple_of((index % wide) * tc, tc), tc)
        k0 = (index // (wide * (rows // tr))) * kg
        us, vs = [None] * kg, [None] * kg
        for q in range(0, count, 4):
            pu, pv = [None] * kg, [None] * kg
            for p in (q, q + 2):
                c = [c_ref[p + i, r, m] for i in range(2)]
                for k in range(kg):
                    slot = [slots[k0 + k, p + i] for i in range(2)]
                    u = c[0] * d_ref[slot[0], 0, r, m] + c[1] * d_ref[slot[1], 0, r, m]
                    v = c[0] * d_ref[slot[0], 1, r, m] + c[1] * d_ref[slot[1], 1, r, m]
                    pu[k] = u if p == q else pu[k] + u
                    pv[k] = v if p == q else pv[k] + v
            for k in range(kg):
                us[k] = pu[k] if q == 0 else us[k] + pu[k]
                vs[k] = pv[k] if q == 0 else vs[k] + pv[k]
        for k in range(kg):
            out_ref[k0 + k, 0, 0, r, m] = us[k]
            out_ref[k0 + k, 0, 1, r, m] = vs[k]
        return 0

    lax.fori_loop(0, wide * (rows // tr) * (count // kg), tile, 0)


def own_rows(mine, slots, pieces, coupling, energy, le, base, steps, held):
    each, n, _ = pieces[0].shape
    count, rows, _ = coupling.shape
    cols = n // 2
    alias = [] if held is None else [held]
    in_specs = (
        [pl.BlockSpec((each, rows, cols), lambda t, mine, slots: (0, mine[0], base + t))] * len(pieces)
        + [pl.BlockSpec((each, cols, rows), lambda t, mine, slots: (0, base + t, mine[0]))] * len(pieces)
        + [pl.BlockSpec((count, rows, cols), lambda t, mine, slots: (0, 0, base + t))]
        + [pl.BlockSpec(memory_space=pl.ANY)] * len(alias)
    )
    return pl.pallas_call(
        functools.partial(rows_kernel, len(pieces), base),
        out_shape=jax.ShapeDtypeStruct((count, le, 2, rows, n), BF16),
        grid_spec=pltpu.PrefetchScalarGridSpec(
            num_scalar_prefetch=2,
            grid=(steps,),
            in_specs=in_specs,
            out_specs=pl.BlockSpec((count, 1, 2, rows, cols), lambda t, mine, slots: (0, energy, 0, 0, base + t)),
            scratch_shapes=[pltpu.VMEM((count, 2, rows, cols), BF16)],
        ),
        input_output_aliases={2 + len(in_specs) - 1: 0} if alias else {},
        compiler_params=params(56),
        cost_estimate=cost(4 * count * count * rows * n, rows * n * count * 10),
        name="rows",
    )(mine[None], slots, *pieces, *pieces, coupling, *alias)


def density_terms(energy, g_ref, gamma_ref, x_ref, y_ref):
    n = g_ref.shape[-1]
    gamma = gamma_ref[0, energy:energy + 1, :]
    g_re, g_im = g_ref[0, 0, 0], g_ref[0, 0, 1]
    row, col = row_col(n, n)
    x, yt = x_ref[0].astype(F32), y_ref[0].astype(F32).T
    s_re = jnp.where(col >= row, x, yt).astype(BF16)
    s_im = jnp.where(col < row, x, jnp.where(col > row, -yt, 0.0)).astype(BF16)
    scaled_re = (g_re.astype(F32) * gamma).astype(BF16).astype(F32)
    scaled_im = (g_im.astype(F32) * gamma).astype(BF16).astype(F32)
    m_re = (dot_nn(g_re, s_re) - dot_nn(g_im, s_im) + scaled_re).astype(BF16)
    m_im = (dot_nn(g_re, s_im) + dot_nn(g_im, s_re) + scaled_im).astype(BF16)
    return dot_nt(m_re, g_re) + dot_nt(m_im, g_im), dot_nt(m_im, g_re) - dot_nt(m_re, g_im)


def first_density_kernel(energy, first, g_ref, gamma_ref, x_ref, y_ref, *refs):
    for c, d in enumerate(density_terms(energy, g_ref, gamma_ref, x_ref, y_ref)):
        refs[-1][0, c] = d if first else d + refs[0][0, c]


def first_density(energy, green, broadening, x, y, held):
    lk, le, _, n, _ = green.shape
    alias = [] if held is None else [held]
    pair = pl.BlockSpec((1, 2, n, n), lambda k: (k, 0, 0, 0))
    one = pl.BlockSpec((1, n, n), lambda k: (k, 0, 0))
    return pl.pallas_call(
        functools.partial(first_density_kernel, energy, held is None),
        out_shape=pltpu.HBM((lk, 2, n, n), F32),
        grid=(lk,),
        in_specs=[
            pl.BlockSpec((1, 1, 2, n, n), lambda k: (k, energy, 0, 0, 0)),
            pl.BlockSpec((1, le, n), lambda k: (k, 0, 0)),
            one,
            one,
        ] + [pair] * len(alias),
        out_specs=pair,
        compiler_params=params(44),
        cost_estimate=cost(16 * lk * n**3, lk * n * n * 20),
        name="density",
    )(green, broadening, x, y, *alias)


def last_density_kernel(scale, energy, odd, g_ref, gamma_ref, x_ref, y_ref, held_ref, *refs):
    d_ref, outs = refs[-1], refs[:-1]
    groups, _, rows, _ = outs[0].shape
    for c, d in enumerate(density_terms(energy, g_ref, gamma_ref, x_ref, y_ref)):
        d_ref[c] = (d + held_ref[0, c]) * scale
    for i in range(len(outs) // 2):
        keep_ref, send_ref = outs[2 * i], outs[2 * i + 1]

        @pl.when(pl.program_id(0) == i)
        def _():
            for c in range(2):
                for g in range(groups):
                    mine = pl.multiple_of((2 * g + odd[0]) * rows, rows)
                    other = pl.multiple_of((2 * g + 1 - odd[0]) * rows, rows)
                    keep_ref[g, c] = d_ref[c, pl.ds(mine, rows), :].astype(BF16)
                    send_ref[g, c] = d_ref[c, pl.ds(other, rows), :].astype(BF16)


def last_density(scale, energy, start, count, groups, odd, green, broadening, x, y, held):
    _, le, _, n, _ = green.shape
    rows = n // (2 * groups)
    one = pl.BlockSpec((1, n, n), lambda i, odd: (start + i, 0, 0))
    out = pl.BlockSpec((groups, 2, rows, n), lambda i, odd: (0, 0, 0, 0))
    return pl.pallas_call(
        functools.partial(last_density_kernel, scale, energy),
        out_shape=[jax.ShapeDtypeStruct((groups, 2, rows, n), BF16)] * (2 * count),
        grid_spec=pltpu.PrefetchScalarGridSpec(
            num_scalar_prefetch=1,
            grid=(count,),
            in_specs=[
                pl.BlockSpec((1, 1, 2, n, n), lambda i, odd: (start + i, energy, 0, 0, 0)),
                pl.BlockSpec((1, le, n), lambda i, odd: (start + i, 0, 0)),
                one,
                one,
                pl.BlockSpec((1, 2, n, n), lambda i, odd: (start + i, 0, 0, 0)),
            ],
            out_specs=[out] * (2 * count),
            scratch_shapes=[pltpu.VMEM((2, n, n), F32)],
        ),
        compiler_params=params(44),
        cost_estimate=cost(count * 16 * n**3, count * n * n * 20),
        name="density",
    )(odd[None], green, broadening, x, y, held)


def pair_sum_kernel(group, keep_ref, recv_ref, *outs):
    groups = len(outs)
    for d in range(groups):
        at = lax.rem(group[0] + d, groups)
        outs[d][...] = (keep_ref[at].astype(F32) + recv_ref[at].astype(F32)).astype(BF16)


def pair_sum(group, keep, recv):
    groups = keep.shape[0]
    vmem = pl.BlockSpec(memory_space=pltpu.VMEM)
    return pl.pallas_call(
        pair_sum_kernel,
        out_shape=[jax.ShapeDtypeStruct(keep.shape[1:], BF16)] * groups,
        in_specs=[pl.BlockSpec(memory_space=pltpu.SMEM), vmem, vmem],
        out_specs=[vmem] * groups,
        compiler_params=params(16),
        cost_estimate=cost(keep.size, keep.size * 6),
        name="pairsum",
    )(group[None], keep, recv)


def staged(green_ret, broadening, coupling, shift_steps, mode_weight, occupation, momentum_map):
    lk, le, _, _, _ = green_ret.shape
    ne, nm = lax.axis_size("energy"), lax.axis_size("mom")
    if le != SHIFT_MAX or lk % 2 or ne % 2 or nm & (nm - 1):
        raise ValueError("unsupported sizes")
    hk, groups = lk // 2, ne // 2
    me, mine = lax.axis_index("energy").astype(jnp.int32), lax.axis_index("mom").astype(jnp.int32)
    odd, group = me & 1, me >> 1
    pairs = [(i, i ^ 1) for i in range(ne)]
    away = [(i, i + (2 if i % 2 else -2)) for i in range(ne) if 0 <= i + (2 if i % 2 else -2) < ne]
    across = [(i, i + (-2 if i % 2 else 2)) for i in range(ne) if 0 <= i + (-2 if i % 2 else 2) < ne]
    strides = []
    while (nm >> (len(strides) + 1)) > 0:
        strides.append(nm >> (len(strides) + 1))

    def permuted(x, perm):
        return lax.ppermute(x, "energy", perm)

    def over_energy(x, perm):
        return hbm(permuted(x, perm))

    def swap(x, stride):
        return lax.ppermute(x, "mom", [(i, i ^ stride) for i in range(nm)])

    def spread(x, last=False):
        held = [x]
        for at, s in enumerate(strides):
            moved = [swap(piece, s) for piece in held]
            held = held + [
                piece if last and at == len(strides) - 1 and i == len(held) - 1 else hbm(piece)
                for i, piece in enumerate(moved)
            ]
        return held

    order = [0]
    for s in strides:
        order = order + [o ^ s for o in order]

    modes = (shift_steps, mode_weight, occupation)

    owner, inner = momentum_map // lk, momentum_map % lk
    place = jnp.zeros_like(owner)
    for at, o in enumerate(order):
        place = jnp.where((owner ^ mine) == o, at, place)
    slots = (place * lk + ((inner // hk) ^ odd) * hk + inner % hk).astype(jnp.int32)

    green_ret = hbm(green_ret)
    coupling = hbm(coupling)
    coupling_pieces = spread(coupling)

    send = [lesser_packed((1 - odd) * hk + j, green_ret, broadening) for j in range(hk)]
    recv = [[over_energy(send[j][h], pairs) for h in range(2)] for j in range(hk)]
    keep = [lesser_packed(odd * hk + j, green_ret, broadening) for j in range(hk)]
    kz = [[permuted(keep[j][h], away) for h in range(2)] for j in range(hk)]
    rz = [[permuted(recv[j][h], across) for h in range(2)] for j in range(hk)]
    got, last = [], None
    for j in range(hk):
        for h in range(2):
            last = sources(
                odd, modes, j, h, hk, keep[j][h], recv[j][h], kz[j][h], rz[j][h], last)
        got.append(last)

    full, turned = place_coupling(mine, tuple(order), coupling_pieces)

    held_rows, held_density = None, None
    scale = 1.0 / (le * ne)
    late = []
    for e in range(le):
        use = [got[j] for j in range(hk)] if e == 0 else [last]
        fresh = [spread(part[e]) for part in use]
        back = [spread(over_energy(part[le + e], pairs), e == le - 1) for part in use]
        pieces = [part[at] for at in range(nm) for part in fresh + back]
        if e < le - 1:
            x, y = home_blocks(mine, slots, pieces, full, turned, lk)
            held_density = first_density(e, green_ret, broadening, x, y, held_density)
        else:
            shares = []
            x, y = home_blocks(mine, slots, pieces, full, turned, lk)
            for first, count in ((0, 1), (1, 1), (2, lk - 2)):
                shares = shares + list(last_density(
                    scale, e, first, count, groups, odd,
                    green_ret, broadening, x, y, held_density))
            for k in range(lk):
                kept, sent = shares[2 * k], shares[2 * k + 1]
                other = permuted(sent, pairs)
                parts = pair_sum(group, kept, other)
                total = parts[0].astype(F32)
                for d in range(1, groups):
                    perm = [(i, (i + 2 * d) % ne) for i in range(ne)]
                    total = total + permuted(parts[d], perm).astype(F32)
                late.append(total)
        for base, steps in (((0, 2),) if e < le - 1 else ((0, 1), (1, 1))):
            held_rows = own_rows(
                mine, slots, pieces, coupling, e, le, base, steps, held_rows)
    density = jnp.transpose(jnp.stack(late), (2, 0, 1, 3))
    return held_rows, density


def solution(mesh):
    return jax.shard_map(
        staged,
        mesh=mesh,
        in_specs=(
            P("mom", "energy", None, None, None),
            P("mom", "energy", None),
            P(None, "mom", None),
            P(),
            P(),
            P(),
            P(),
        ),
        out_specs=(P(None, "energy", None, "mom", None), P("energy", "mom", None, None)),
        check_vma=False,
    )
```
